32 devices in a mesh: dp: 2 (over x), seq: 8 (over z, core), tensor: 2 (over y).
Axes of the slice: x: 2, y: 2, z: 4, core: 2. Of those that a mesh axis runs over, the one named last changes fastest.
Arguments:
- tokens: bfloat16 [2, 4096, 768], P('dp', 'seq'), may hold values from -6 to 6
- doc_ids: int32 [2, 4096], P('dp'), may hold values from 0 to 15, as said below
- memory: bfloat16 [20, 768], replicated, may hold values from -6 to 6
- qkv_weight: bfloat16 [768, 3, 768], P(None, None, 'tensor'), may hold values from -0.21875 to 0.21875
- query_bias: float32 [768], P('tensor'), may hold values from -3 to 3
- value_bias: float32 [768], P('tensor'), may hold values from -3 to 3
- out_weight: bfloat16 [768, 768], P(None, 'tensor'), may hold values from -1.75 to 1.75
- out_bias: float32 [768], replicated, may hold values from -1.75 to 1.75
- norm1_gain: float32 [768], replicated, may hold values from 0.5 to 1.5
- norm1_bias: float32 [768], replicated, may hold values from -1.75 to 1.75
- up_weight: bfloat16 [768, 3072], P(None, 'tensor'), may hold values from -0.21875 to 0.21875
- up_bias: float32 [3072], P('tensor'), may hold values from -3 to 3
- down_weight: bfloat16 [768, 3072], P(None, 'tensor'), may hold values from -0.109375 to 0.109375
- down_bias: float32 [768], replicated, may hold values from -1.75 to 1.75
- norm2_gain: float32 [768], replicated, may hold values from 0.5 to 1.5
- norm2_bias: float32 [768], replicated, may hold values from -1.75 to 1.75
- out_grad: bfloat16 [2, 4096, 768], P('dp', 'seq'), may hold values from -6 to 6
Outputs:
- output: bfloat16 [2, 4096, 768], P('dp', 'seq')
- input_grad: bfloat16 [2, 4096, 768], P('dp', 'seq')
- memory_grad: float32 [20, 768], replicated
- qkv_weight_grad: float32 [768, 3, 768], P('seq', None, 'tensor')
- query_bias_grad: float32 [768], P('tensor')
- value_bias_grad: float32 [768], P('tensor')
- out_weight_grad: float32 [768, 768], P('seq', 'tensor')
- out_bias_grad: float32 [768], P('seq')
- norm1_gain_grad: float32 [768], P('seq')
- norm1_bias_grad: float32 [768], P('seq')
- up_weight_grad: float32 [768, 3072], P('seq', 'tensor')
- up_bias_grad: float32 [3072], P('tensor')
- down_weight_grad: float32 [768, 3072], P('seq', 'tensor')
- down_bias_grad: float32 [768], P('seq')
- norm2_gain_grad: float32 [768], P('seq')
- norm2_bias_grad: float32 [768], P('seq')
The draws below stay inside these ranges and needn't reach their ends.
Inputs may be any that keep to these rules, and one draw needn't show every extreme that they name: In every sequence doc_ids never fall, each document covers 21 to 1536 consecutive rows, every number of 0 to 15 is used, and one document has exactly 1536 rows.
All inputs are finite; a program needn't handle non-finite values.
Results may differ from the reference program's by a relative error of at most 0.024.
Values may be sent and summed in bfloat16 or wider, within the bound.
A program may use at most 192 MiB of HBM per device.

```python
import jax
import jax.numpy as jnp
from jax import lax

HEADS = 12
HEAD_DIM = 64
D = 768
FF = 3072
READ_ROWS = 10
MIN_DOC = 21
MOST = 1536
SEQ_LEN = 4096
SEQS = 2
DOCS = 16


def draw_doc_ids(key, part):
    seq_keys = jax.random.split(key, SEQS)

    def one_sequence(seq_key):
        key_one, key_two = jax.random.split(seq_key)
        weight_kinds = jax.random.randint(key_one, (DOCS,), 0, 3)
        doc_weights = jnp.left_shift(jnp.ones((DOCS,), jnp.int32), weight_kinds)
        biggest = jax.random.randint(key_two, (), 0, DOCS)
        doc_index = jnp.arange(DOCS, dtype=jnp.int32)
        doc_weights = jnp.where(doc_index == biggest, 0, doc_weights)
        spare_rows = SEQ_LEN - DOCS * MIN_DOC - (MOST - MIN_DOC)
        extra_rows = spare_rows * doc_weights // jnp.sum(doc_weights)
        leftover = spare_rows - jnp.sum(extra_rows)
        order_rank = jnp.cumsum((doc_weights > 0).astype(jnp.int32)) - 1
        extra_rows = extra_rows + jnp.where((doc_weights > 0) & (order_rank < leftover), 1, 0)
        doc_lengths = jnp.where(doc_index == biggest, MOST, MIN_DOC + extra_rows)
        doc_ends = jnp.cumsum(doc_lengths)
        positions = jnp.arange(SEQ_LEN, dtype=jnp.int32)
        return jnp.sum((positions[:, None] >= doc_ends[None, :]).astype(jnp.int32), axis=1)
    return jax.vmap(one_sequence)(seq_keys).astype(jnp.int32)


def block_levels(stream_key, shape, pieces, smallest, top_value):
    level = 1.0
    for dim, blocks in pieces:
        steps = jax.random.uniform(jax.random.fold_in(jax.random.fold_in(stream_key, 6), dim), (blocks,), jnp.float32, smallest / len(pieces), top_value / len(pieces))
        level = level * jnp.repeat(jnp.exp(steps), shape[dim] // blocks).reshape((-1,) + (1,) * (len(shape) - 1 - dim))
    return level


def scatter_about(rng, extent, width, bound, shards=(), held_as=jnp.bfloat16):
    level = block_levels(rng, extent, shards, -0.22, 0.18) if shards else 1.0
    entries = jax.random.normal(rng, extent, jnp.float32) * width * level
    return jnp.minimum(jnp.maximum(entries, -bound), bound).astype(held_as)


def setup_inputs(seed: int = 0) -> dict:
    key_list = jax.random.split(jax.random.key(seed), 18)
    tokens = scatter_about(key_list[0], (SEQS, SEQ_LEN, D), 1.0, 6.0, ((0, 2), (1, 8)))
    doc_ids = draw_doc_ids(jax.random.fold_in(key_list[17], 71), 0)
    memory = scatter_about(key_list[2], (2 * READ_ROWS, D), 1.0, 6.0)
    qkv_weight = scatter_about(key_list[3], (D, 3, D), D ** -0.5, 0.21875, ((2, 2),))
    query_bias = scatter_about(key_list[4], (D,), 0.5, 3.0, ((0, 2),), jnp.float32)
    value_bias = scatter_about(key_list[5], (D,), 0.5, 3.0, ((0, 2),), jnp.float32)
    out_weight = scatter_about(key_list[6], (D, D), (D // 64) ** -0.5, 1.75, ((1, 2),))
    out_bias = scatter_about(key_list[7], (D,), 0.3, 1.75, (), jnp.float32)
    norm1_gain = jnp.clip(1.0 + 0.1 * jax.random.normal(key_list[8], (D,), jnp.float32), 0.5, 1.5)
    norm1_bias = scatter_about(key_list[9], (D,), 0.3, 1.75, (), jnp.float32)
    up_weight = scatter_about(key_list[10], (D, FF), D ** -0.5, 0.21875, ((1, 2),))
    up_bias = scatter_about(key_list[11], (FF,), 0.5, 3.0, ((0, 2),), jnp.float32)
    down_weight = scatter_about(key_list[12], (D, FF), FF ** -0.5, 0.109375, ((1, 2),))
    down_bias = scatter_about(key_list[13], (D,), 0.3, 1.75, (), jnp.float32)
    norm2_gain = jnp.clip(1.0 + 0.1 * jax.random.normal(key_list[14], (D,), jnp.float32), 0.5, 1.5)
    norm2_bias = scatter_about(key_list[15], (D,), 0.3, 1.75, (), jnp.float32)
    out_grad = scatter_about(key_list[16], (SEQS, SEQ_LEN, D), 1.0, 6.0, ((0, 2), (1, 8)))
    return dict(tokens=tokens, doc_ids=doc_ids, memory=memory, qkv_weight=qkv_weight, query_bias=query_bias, value_bias=value_bias, out_weight=out_weight, out_bias=out_bias, norm1_gain=norm1_gain, norm1_bias=norm1_bias, up_weight=up_weight, up_bias=up_bias, down_weight=down_weight, down_bias=down_bias, norm2_gain=norm2_gain, norm2_bias=norm2_bias, out_grad=out_grad)


@jax.custom_vjp
def low(v):
    return lax.optimization_barrier(v.astype(jnp.bfloat16)).astype(jnp.float32)

@jax.custom_vjp
def low_back(v):
    return v

def low_keep(v):
    return (low(v), None)

def low_pass(kept, grad):
    return (grad,)

def back_keep(v):
    return (v, None)

def back_low(kept, grad):
    return (low(grad),)
low.defvjp(low_keep, low_pass)
low_back.defvjp(back_keep, back_low)
norm_eps = 1e-05

def memory_slots(id_row):
    count = id_row.shape[0]
    places = jnp.arange(count, dtype=jnp.int32)
    before = jnp.concatenate([jnp.full((1,), -1, jnp.int32), id_row[:-1].astype(jnp.int32)])
    after = jnp.concatenate([id_row[1:].astype(jnp.int32), jnp.full((1,), -1, jnp.int32)])
    starts = lax.cummax(jnp.where(id_row != before, places, 0), axis=0)
    finish = lax.cummin(jnp.where(id_row != after, places, count), axis=0, reverse=True)
    offset = places - starts
    behind = finish - places
    return jnp.where(offset < READ_ROWS, offset, jnp.where(behind < READ_ROWS, 2 * READ_ROWS - 1 - behind, -1)).astype(jnp.int32)

def normalize(hidden, gain, shift):
    centre = lax.optimization_barrier(jnp.mean(hidden, axis=-1, keepdims=True))
    centred = hidden - centre
    spread = lax.optimization_barrier(jnp.mean(centred * centred, axis=-1, keepdims=True))
    return centred * lax.rsqrt(spread + norm_eps) * gain + shift

def attention(query_rows, key_rows, value_rows, doc_row):
    precise = lax.Precision.HIGHEST
    block_rows = min(512, SEQ_LEN)
    key_span = block_rows + 2 * MOST
    pad_width = ((MOST, MOST), (0, 0), (0, 0))
    key_padded = jnp.pad(key_rows, pad_width)
    value_padded = jnp.pad(value_rows, pad_width)
    ids_padded = jnp.pad(doc_row, (MOST, MOST), constant_values=-1)
    scale_factor = HEAD_DIM ** (-0.5)

    def one_block(start):
        query_block = lax.dynamic_slice_in_dim(query_rows, start, block_rows, 0)
        query_ids = lax.dynamic_slice_in_dim(doc_row, start, block_rows, 0)
        key_block = lax.dynamic_slice_in_dim(key_padded, start, key_span, 0)
        value_block = lax.dynamic_slice_in_dim(value_padded, start, key_span, 0)
        key_ids = lax.dynamic_slice_in_dim(ids_padded, start, key_span, 0)
        scores = low_back(scale_factor * jnp.einsum('qhd,khd->hqk', query_block, key_block, precision=precise))
        same_doc = (query_ids[:, None] == key_ids[None, :])[None]
        scores = jnp.where(same_doc, scores, -1e+30)
        weights = jax.nn.softmax(scores, axis=-1)
        return jnp.einsum('hqk,khd->qhd', low(weights), value_block, precision=precise)
    starts = jnp.arange(SEQ_LEN // block_rows, dtype=jnp.int32) * block_rows
    mixed = lax.map(jax.checkpoint(one_block), starts)
    return mixed.reshape(SEQ_LEN, HEADS * HEAD_DIM)

def full_layer(source, memory, slots, doc_row, qkv_weight, query_bias, value_bias, out_weight, out_bias, norm1_gain, norm1_bias, up_weight, up_bias, down_weight, down_bias, norm2_gain, norm2_bias):
    precise = lax.Precision.HIGHEST
    selector = (slots[:, None] == jnp.arange(2 * READ_ROWS, dtype=jnp.int32)[None, :]).astype(jnp.float32)
    memory_rows = jnp.dot(selector, memory, precision=precise)
    source = jnp.where((slots >= 0)[:, None], memory_rows, source)
    projected = jnp.einsum('td,dcf->tcf', source, qkv_weight, precision=precise)
    query_rows = low_back(low(projected[:, 0] + query_bias))
    key_rows = low_back(low(projected[:, 1]))
    value_rows = low_back(low(projected[:, 2] + value_bias))
    head_shape = (SEQ_LEN, HEADS, HEAD_DIM)
    mixed = attention(query_rows.reshape(head_shape), key_rows.reshape(head_shape), value_rows.reshape(head_shape), doc_row)
    mixed = low_back(low(mixed))
    branch = low_back(jnp.einsum('tf,of->to', mixed, out_weight, precision=precise) + out_bias)
    first_out = normalize(source + branch, norm1_gain, norm1_bias)
    up_proj = low_back(jnp.einsum('td,df->tf', low(first_out), up_weight, precision=precise) + up_bias)
    act_low = low(jax.nn.gelu(up_proj, approximate=False))
    down_out = low_back(jnp.einsum('tf,of->to', act_low, down_weight, precision=precise) + down_bias)
    return normalize(first_out + down_out, norm2_gain, norm2_bias)

def reference(tokens, doc_ids, memory, qkv_weight, query_bias, value_bias, out_weight, out_bias, norm1_gain, norm1_bias, up_weight, up_bias, down_weight, down_bias, norm2_gain, norm2_bias, out_grad):
    params = tuple((each_param.astype(jnp.float32) for each_param in (memory, qkv_weight, query_bias, value_bias, out_weight, out_bias, norm1_gain, norm1_bias, up_weight, up_bias, down_weight, down_bias, norm2_gain, norm2_bias)))

    def per_sequence(totals, seq_item):
        source_row, doc_row, cotangent = seq_item
        slots = memory_slots(doc_row)

        def run_layer(source, memory_param, *weight_list):
            return full_layer(source, memory_param, slots, doc_row, *weight_list)
        layer_out, pull_back = jax.vjp(run_layer, source_row.astype(jnp.float32), *params)
        grad_list = pull_back(cotangent.astype(jnp.float32))
        summed = tuple((total + grad for total, grad in zip(totals, grad_list[1:])))
        return (summed, (layer_out.astype(jnp.bfloat16), grad_list[0].astype(jnp.bfloat16)))
    zero_grads = tuple((jnp.zeros(each_param.shape, jnp.float32) for each_param in params))
    totals, (outputs, input_grads) = lax.scan(per_sequence, zero_grads, (tokens, doc_ids, out_grad))
    return (outputs, input_grads, totals[0], totals[1], totals[2], totals[3], totals[4], totals[5], totals[6], totals[7], totals[8], totals[9], totals[10], totals[11], totals[12], totals[13])
```

```python
import functools

import jax
import jax.numpy as jnp
from jax import lax
from jax.experimental import pallas as pl
from jax.experimental.pallas import tpu as pltpu
from jax.sharding import PartitionSpec as P

HEAD_DIM = 64
READ_ROWS = 10
REACH = 3
NORM_EPS = 1e-05
F32, BF16 = jnp.float32, jnp.bfloat16
NT = (((1,), (1,)), ((), ()))
NN = (((1,), (0,)), ((), ()))
NEG = -1e30
FLOOR = -1e29
VMEM = pl.BlockSpec(memory_space=pltpu.VMEM)
SMEM = pl.BlockSpec(memory_space=pltpu.SMEM)


def remote(source, target, send_sem, recv_sem, **where):
    return pltpu.make_async_remote_copy(
        source, target, send_sem, recv_sem, device_id=where, device_id_type=pl.DeviceIdType.MESH
    )


def greet(partners):
    barrier = pltpu.get_barrier_semaphore()
    total = 0
    for present, where in partners:
        total = total + present.astype(jnp.int32)

        @pl.when(present)
        def _():
            pl.semaphore_signal(barrier, inc=1, device_id=where, device_id_type=pl.DeviceIdType.MESH)

    pl.semaphore_wait(barrier, total)


def dot(a, b, dims=NN):
    return lax.dot_general(a, b, dims, preferred_element_type=F32)

def low_half(shape):
    return lax.broadcasted_iota(jnp.int32, shape, len(shape) - 1) < 64

def id_columns(ids_ref, start, count):
    row = jnp.broadcast_to(ids_ref[0:1, pl.ds(start, count)], (128, count))
    return jnp.transpose(row)

def wide(x, count):
    return jnp.concatenate([x] * (count // 128), axis=1)

def split_heads(source_ref, rows, target_ref, pairs, keep):
    for pair in range(pairs):
        block = source_ref[rows, pair * 128:pair * 128 + 128]
        target_ref[2 * pair] = jnp.where(keep, block, jnp.zeros_like(block))
        target_ref[2 * pair + 1] = jnp.where(keep, jnp.zeros_like(block), block)

def sweep(rng_ref, b, body):
    first, full_first, full_last, last = (rng_ref[4 * b + i] for i in range(4))
    lax.fori_loop(full_first, full_last, lambda j, c: body(j, False, c), 0)

    def edge(i, c):
        j = first + i
        return body(jnp.where(j < full_first, j, j + full_last - full_first), True, c)

    lax.fori_loop(0, last - first - (full_last - full_first), edge, 0)

def fwd_kernel(bq, bk, own, rng_ref, q_ref, k_ref, v_ref, ids_ref, o_ref, lse_ref, acc_ref, max_ref, q_heads, cols_ref):
    pairs = q_ref.shape[1] // 128
    rows = q_ref.shape[0]
    low_q, low_k = low_half((bq, 128)), low_half((bk, 128))

    def block(qb, carry):
        mine = pl.ds(pl.multiple_of(qb * bq, bq), bq)
        cols_ref[...] = id_columns(ids_ref, pl.multiple_of(own + qb * bq, bq), bq)
        split_heads(q_ref, mine, q_heads, pairs, low_q)
        acc_ref[...] = jnp.zeros_like(acc_ref)
        max_ref[...] = jnp.full_like(max_ref, FLOOR)

        def step(j, masked, carry):
            there = pl.ds(pl.multiple_of(j * bk, bk), bk)
            def pair_step(pair, carry):
                lanes = pl.ds(pair * 128, 128)
                key = k_ref[there, lanes]
                value = v_ref[there, lanes]
                for odd in range(2):
                    head = 2 * pair + odd
                    scores = dot(q_heads[head], key, NT)
                    if masked:
                        scores = jnp.where(wide(cols_ref[...], bk) == ids_ref[0:1, there], scores, NEG)
                    old = max_ref[head]
                    new = jnp.maximum(old, jnp.max(scores, axis=1, keepdims=True))
                    probs = jnp.exp(scores - wide(new, bk)).astype(BF16)
                    ones = jnp.where(low_k if odd == 0 else ~low_k, value, jnp.ones_like(value))
                    acc_ref[head] = acc_ref[head] * jnp.exp(old - new) + dot(probs, ones)
                    max_ref[head] = new
                return carry
            for pair in range(pairs):
                pair_step(pair, carry)
            return carry

        sweep(rng_ref, qb, step)
        stats = jnp.zeros((bq, 128), F32)
        lane = lax.broadcasted_iota(jnp.int32, (bq, 128), 1)
        for pair in range(pairs):
            even, odd = acc_ref[2 * pair], acc_ref[2 * pair + 1]
            total_even, total_odd = even[:, 64:65], odd[:, 0:1]
            mixed = jnp.where(low_q, even / total_even, odd / total_odd)
            o_ref[mine, pair * 128:pair * 128 + 128] = mixed.astype(BF16)
            stats = jnp.where(lane == 2 * pair, max_ref[2 * pair] + jnp.log(total_even), stats)
            stats = jnp.where(lane == 2 * pair + 1, max_ref[2 * pair + 1] + jnp.log(total_odd), stats)
        lse_ref[mine, :] = stats
        return carry

    lax.fori_loop(0, rows // bq, block, 0)

def attention_forward(rng, query, key, value, ids, own, bq=256, bk=256):
    rows, width = query.shape
    heads = width // 64
    return pl.pallas_call(
        functools.partial(fwd_kernel, bq, bk, own),
        out_shape=(jax.ShapeDtypeStruct((rows, width), BF16), jax.ShapeDtypeStruct((rows, 128), F32)),
        in_specs=[pl.BlockSpec(memory_space=pltpu.SMEM)] + [pl.BlockSpec(memory_space=pltpu.VMEM)] * 4,
        out_specs=(pl.BlockSpec(memory_space=pltpu.VMEM),) * 2,
        scratch_shapes=[pltpu.VMEM((heads, bq, 128), F32), pltpu.VMEM((heads, bq, 128), F32), pltpu.VMEM((heads, bq, 128), BF16), pltpu.VMEM((bq, 128), F32)],
        compiler_params=pltpu.CompilerParams(vmem_limit_bytes=40 << 20),
        name="attention_forward",
    )(rng, query, key, value, ids)

def bwd_kernel(bq, bk, own, rng_ref, q_ref, k_ref, v_ref, g_ref, ids_ref, lse_ref, along_ref, rows_ref, out_ref, dq_acc, dk_acc, dv_acc, q_heads, k_heads, v_heads, g_heads, lse_cols, along_cols, cols_ref):
    rows, width = out_ref.shape[0], q_ref.shape[1]
    pairs = width // 128
    heads = 2 * pairs
    low_q = low_half((bq, 128))

    def block(b, carry):
        start = pl.multiple_of(b * bq, bq)
        mine = pl.ds(start, bq)
        here = pl.ds(pl.multiple_of(own + start, bq), bq)
        cols_ref[...] = id_columns(ids_ref, pl.multiple_of(own + start, bq), bq)
        for source, target in ((q_ref, q_heads), (k_ref, k_heads), (v_ref, v_heads), (g_ref, g_heads)):
            split_heads(source, here, target, pairs, low_q)
        for head in range(heads):
            lse_cols[head] = jnp.broadcast_to(lse_ref[mine, head:head + 1], (bq, 128))
            along_cols[head] = jnp.broadcast_to(along_ref[mine, head:head + 1], (bq, 128))
        for acc in (dq_acc, dk_acc, dv_acc):
            acc[...] = jnp.zeros_like(acc)

        def step(j, masked, carry):
            there = pl.ds(pl.multiple_of(j * bk, bk), bk)
            def pair_step(pair, carry):
                lanes = pl.ds(pair * 128, 128)
                q_far, k_far, v_far, g_far = (r[there, lanes] for r in (q_ref, k_ref, v_ref, g_ref))
                def hide(x):
                    return jnp.where(wide(cols_ref[...], bk) == ids_ref[0:1, there], x, 0.0) if masked else x
                for odd in range(2):
                    head = 2 * pair + odd
                    scores = dot(q_heads[head], k_far, NT)
                    probs = hide(jnp.exp(scores - wide(lse_cols[head], bk)))
                    slope = dot(g_heads[head], v_far, NT)
                    grad = (probs * (slope - wide(along_cols[head], bk))).astype(BF16)
                    dq_acc[head] += dot(grad, k_far)
                    scores = dot(k_heads[head], q_far, NT)
                    probs = hide(jnp.exp(scores - rows_ref[pl.ds(head, 1), there]))
                    slope = dot(v_heads[head], g_far, NT)
                    grad = (probs * (slope - rows_ref[pl.ds(8 + head, 1), there])).astype(BF16)
                    dv_acc[head] += dot(probs.astype(BF16), g_far)
                    dk_acc[head] += dot(grad, q_far)
                return carry
            for pair in range(pairs):
                pair_step(pair, carry)
            return carry

        sweep(rng_ref, b, step)
        for which, (acc, factor) in enumerate(((dq_acc, 0.125), (dk_acc, 1.0), (dv_acc, 1.0))):
            for pair in range(pairs):
                both = jnp.where(low_q, acc[2 * pair], acc[2 * pair + 1]) * factor
                out_ref[mine, which * width + pair * 128:which * width + pair * 128 + 128] = both.astype(BF16)
        return carry

    lax.fori_loop(0, rows // bq, block, 0)

def attention_backward(rng, query, key, value, grads, ids, lse, along, stat_rows, rows, own, bq=256, bk=256):
    width = query.shape[1]
    heads = width // 64
    return pl.pallas_call(
        functools.partial(bwd_kernel, bq, bk, own),
        out_shape=jax.ShapeDtypeStruct((rows, 3 * width), BF16),
        in_specs=[pl.BlockSpec(memory_space=pltpu.SMEM)] + [pl.BlockSpec(memory_space=pltpu.VMEM)] * 8,
        out_specs=pl.BlockSpec(memory_space=pltpu.VMEM),
        scratch_shapes=[pltpu.VMEM((heads, bq, 128), F32)] * 3 + [pltpu.VMEM((heads, bq, 128), BF16)] * 4 + [pltpu.VMEM((heads, bq, 128), F32)] * 2 + [pltpu.VMEM((bq, 128), F32)],
        compiler_params=pltpu.CompilerParams(vmem_limit_bytes=56 << 20),
        name="attention_backward",
    )(rng, query, key, value, grads, ids, lse, along, stat_rows)

def halo_kernel(count, parts, own_ref, window_ref, send_sem, recv_sem, local_sem):
    s = lax.axis_index("seq")
    core = lax.rem(s, 2)
    sibling = s + 1 - 2 * core
    rows = own_ref.shape[0] // parts
    left, right = s >= 2, s < count - 2
    greet(
        [(s >= k, {"seq": s - k}) for k in (1, 2)] + [(s < count - k, {"seq": s + k}) for k in (1, 2)]
    )

    def own(part, kind, slot, target):
        at = pl.ds(part * rows, rows)
        return remote(own_ref.at[at], window_ref.at[slot, at], send_sem.at[kind, part], recv_sem.at[slot, part], seq=target)

    def moved(part, kind, held, slot, target):
        at = pl.ds(part * rows, rows)
        return remote(window_ref.at[held, at], window_ref.at[slot, at], send_sem.at[kind, part], recv_sem.at[slot, part], seq=target)

    def first_copies(part):
        return (
            (right, own(part, 0, 1, s + 2)),
            (left, own(part, 1, 5, s - 2)),
            (core == 0, own(part, 2, 2, sibling)),
            (core == 1, own(part, 2, 4, sibling)),
        )

    def from_left(part):
        return (
            (jnp.logical_and(left, jnp.logical_and(core == 1, right)), moved(part, 3, 1, 0, s + 1)),
            (jnp.logical_and(left, core == 0), moved(part, 4, 1, 0, sibling)),
            (jnp.logical_and(left, core == 1), moved(part, 4, 1, 2, sibling)),
        )

    def from_right(part):
        return (
            (jnp.logical_and(right, jnp.logical_and(core == 0, left)), moved(part, 5, 5, 6, s - 1)),
            (jnp.logical_and(right, core == 0), moved(part, 6, 5, 4, sibling)),
            (jnp.logical_and(right, core == 1), moved(part, 6, 5, 6, sibling)),
        )

    def each(copies, act):
        for present, copy in copies:
            pl.when(present)(functools.partial(act, copy))

    start = lambda copy: copy.start()
    wait_send = lambda copy: copy.wait_send()

    def arrived(slot, part):
        own(part, 0, slot, s).wait_recv()

    for part in range(parts):
        each(first_copies(part), start)
    local = pltpu.make_async_copy(own_ref, window_ref.at[REACH], local_sem)
    local.start()
    for part in range(parts):
        pl.when(left)(functools.partial(arrived, 1, part))
        each(from_left(part), start)
        pl.when(right)(functools.partial(arrived, 5, part))
        each(from_right(part), start)
    local.wait()
    for part in range(parts):
        for slot in (0, 2, 4, 6):
            block = s + slot - REACH
            pl.when(jnp.logical_and(block >= 0, block < count))(functools.partial(arrived, slot, part))
        each(first_copies(part) + from_left(part) + from_right(part), wait_send)


def gather_window(own, count, collective_id, parts=2):
    return pl.pallas_call(
        functools.partial(halo_kernel, count, parts),
        out_shape=jax.ShapeDtypeStruct((2 * REACH + 1,) + own.shape, own.dtype),
        in_specs=[VMEM],
        out_specs=VMEM,
        scratch_shapes=[
            pltpu.SemaphoreType.DMA((7, parts)),
            pltpu.SemaphoreType.DMA((7, parts)),
            pltpu.SemaphoreType.DMA,
        ],
        compiler_params=pltpu.CompilerParams(collective_id=collective_id, has_side_effects=True),
        name="gather_window",
    )(own)


def split_dot(left, right, dims):
    high = right.astype(BF16)
    low = (right - high.astype(F32)).astype(BF16)
    return dot(left, high, dims) + dot(left, low, dims)


def tail_kernel(dps, seqs, chunks, chunk, width, up_ref, down_ref, out_grad_ref, proj_ref, source_ref, weight_ref, input1_ref, select_ref, small_ref,
                up_out, down_out, mix_out, input_out, small_out,
                mix, y_send, y_recv, a_recv, parts, b_recv, mine, c_recv, last, d_recv, small_in, small_recv, small_mine, small_dp,
                y_sems, a_sems, b_sems, c_sems, d_sems, s_sems):
    zs = seqs // 2
    bits = zs.bit_length() - 1
    t, d, s = lax.axis_index("tensor"), lax.axis_index("dp"), lax.axis_index("seq")
    z, core = s // 2, lax.rem(s, 2)
    sibling = s + 1 - 2 * core
    shares = -(-chunk // width)
    owners = small_ref.shape[0]
    block = up_ref.shape[0] // seqs
    rows, columns = proj_ref.shape
    steps = y_send.shape[0]
    span = rows // steps
    true = s >= 0
    partners = [(true, {"seq": lax.rem(s + k, seqs)}) for k in range(1, seqs)]
    partners += [(true, {"dp": lax.rem(d + k, dps)}) for k in range(1, dps)]
    partners += [(true, {"tensor": 1 - t})]
    greet(partners)
    grads = (up_ref, down_ref, mix)
    results = (up_out, down_out, mix_out)
    per = up_ref.shape[1] // chunk

    def piece(c):
        return grads[c // per], (c % per) * chunk

    def a_copy(c, j):
        ref, at = piece(c)
        start = pl.multiple_of((2 * j + 1 - core) * block, 16)
        return remote(ref.at[pl.ds(start, block), pl.ds(at, chunk)], a_recv.at[c, j], a_sems.at[0, c, j], a_sems.at[1, c, j], seq=sibling)

    def b_copy(c, k):
        other = lax.rem(d + k, dps)
        return other, remote(parts.at[c, other], b_recv.at[c, k], b_sems.at[0, c, k], b_sems.at[1, c, k], dp=other)

    def c_copies(c, b):
        size = 2 << b
        high = lax.rem(z // (1 << b), 2)
        partner = z + (1 << b) - (size * high)
        low = lax.rem(partner, size)
        return [
            remote(mine.at[c, i * size + low], c_recv.at[c, (1 << b) * 0 + first_slot(b) + i], c_sems.at[0, c, first_slot(b) + i], c_sems.at[1, c, first_slot(b) + i], seq=2 * partner + core)
            for i in range(zs // size)
        ]

    def first_slot(b):
        return sum(zs // (2 << e) for e in range(b))

    def d_copy(c, k):
        return remote(last.at[c], d_recv.at[c, k], d_sems.at[0, c, k], d_sems.at[1, c, k], dp=lax.rem(d + k, dps))

    def start_a(c):
        for j in range(zs):
            a_copy(c, j).start()

    def end_a(c):
        ref, at = piece(c)
        for j in range(zs):
            a_copy(c, j).wait()
            start = pl.multiple_of((2 * j + core) * block, 16)
            for p in range(shares):
                real = min(width, chunk - p * width)
                lanes = pl.ds(at + p * width, real)
                total = ref[pl.ds(start, block), lanes].astype(F32) + a_recv[c, j, :, p * width:p * width + real].astype(F32)
                parts[c, p, j, :, 0:real] = total.astype(BF16)
                if real < width:
                    parts[c, p, j, :, real:width] = jnp.zeros((block, width - real), BF16)
        for k in range(1, dps):
            other, copy = b_copy(c, k)
            pl.when(other < shares)(copy.start)

    def end_b(c):
        for k in range(1, dps):
            other, copy = b_copy(c, k)
            pl.when(other < shares)(copy.wait_send)

        @pl.when(d < shares)
        def _():
            for k in range(1, dps):
                b_copy(c, k)[1].wait_recv()
            for j in range(zs):
                total = parts[c, d, j].astype(F32)
                for k in range(1, dps):
                    total = total + b_recv[c, k, j].astype(F32)
                mine[c, j] = total.astype(BF16)
            for copy in c_copies(c, 0):
                copy.start()

    def end_c(c, b):
        size = 2 << b
        kept = lax.rem(z, size)

        @pl.when(d < shares)
        def _():
            for i, copy in enumerate(c_copies(c, b)):
                copy.wait()
                held = mine[c, i * size + kept].astype(F32) + c_recv[c, first_slot(b) + i].astype(F32)
                if b < bits - 1:
                    mine[c, i * size + kept] = held.astype(BF16)
                else:
                    last[c] = held.astype(BF16)
            if b < bits - 1:
                for copy in c_copies(c, b + 1):
                    copy.start()
            else:
                for k in range(1, dps):
                    d_copy(c, k).start()

    def end_d(c):
        result = results[c // per]
        at = (c % per) * chunk

        def put(share, value):
            for p in range(shares):
                real = min(width, chunk - p * width)

                @pl.when(share == p)
                def _():
                    result[:, at + p * width:at + p * width + real] = value[:, 0:real].astype(F32)

        @pl.when(d < shares)
        def _():
            put(d, last[c])
            for k in range(1, dps):
                d_copy(c, k).wait_send()
        for k in range(1, dps):
            share = lax.rem(d + dps - k, dps)

            @pl.when(share < shares)
            def _():
                d_copy(c, k).wait_recv()
                put(share, d_recv[c, k])

    stages = [end_a, end_b] + [functools.partial(end_c, b=b) for b in range(bits)] + [end_d]

    def y_copy(i):
        return remote(y_send.at[i], y_recv.at[i], y_sems.at[0, i], y_sems.at[1, i], tensor=1 - t)

    for c in range(2 * per):
        start_a(c)
    for i in range(steps):
        y_send[i] = dot(proj_ref[i * span:(i + 1) * span, :], weight_ref[...], NT).astype(BF16)
        y_copy(i).start()
    out_width = out_grad_ref.shape[1]
    mix[:, 0:out_width] = out_grad_ref[...]
    third = columns // 3
    for i in range(3):
        part = lax.dot_general(source_ref[...], proj_ref[:, i * third:(i + 1) * third], (((0,), (0,)), ((), ())), preferred_element_type=F32)
        mix[:, out_width + i * third:out_width + (i + 1) * third] = part.astype(BF16)
    for c in range(2 * per, chunks):
        start_a(c)
    for i in range(owners):
        small_in[i] = small_ref[i]
    small_in[1, 0:1, 0:third] = jnp.sum(proj_ref[:, 0:third].astype(F32), axis=0, keepdims=True)
    small_in[1, 0:1, third:2 * third] = jnp.sum(proj_ref[:, 2 * third:3 * third].astype(F32), axis=0, keepdims=True)

    def end_y():
        memory = jnp.zeros((32, input_out.shape[1]), F32)
        for i in range(steps):
            y_copy(i).wait()
            at = slice(i * span, (i + 1) * span)
            total = input1_ref[at, :] + (y_send[i].astype(F32) + y_recv[i].astype(F32))
            select = select_ref[at, :]
            memory = memory + split_dot(select, total, (((0,), (0,)), ((), ())))
            inside = dot(select, jnp.ones((32, total.shape[1]), BF16))
            input_out[at, :] = jnp.where(inside > 0.5, 0.0, total).astype(BF16)
        small_in[1, 1:8, :] = memory[0:7]
        small_in[2] = memory[7:15]
        small_in[3, 0:5, :] = memory[15:20]
        for hop in range(1, seqs):
            owner = lax.rem(s + hop, seqs)
            pl.when(owner < owners)(to_owner(hop, owner).start)

    def to_owner(hop, owner):
        return remote(small_in.at[owner], small_recv.at[hop], s_sems.at[0, 0, hop], s_sems.at[1, 0, hop], seq=owner)

    def across(k):
        return remote(small_mine, small_dp.at[k], s_sems.at[0, 1, k], s_sems.at[1, 1, k], dp=lax.rem(d + k, dps))

    def back(hop, owner, target):
        return remote(small_out.at[owner], small_out.at[owner], s_sems.at[0, 2, hop], s_sems.at[1, 2, hop], seq=target)

    def small_one():
        @pl.when(s < owners)
        def _():
            total = small_in[s]
            for hop in range(1, seqs):
                to_owner(hop, s).wait_recv()
                total = total + small_recv[hop]
            small_mine[...] = total
            for k in range(1, dps):
                across(k).start()

    def small_two():
        @pl.when(s < owners)
        def _():
            small_dp[0] = small_mine[...]
            for k in range(1, dps):
                across(k).wait()
            ordered = jnp.zeros(small_mine.shape, F32)
            for index in range(dps):
                ordered = ordered + small_dp[lax.rem(d + dps - index, dps)]
            small_out[s] = ordered
            for hop in range(1, seqs):
                back(hop, s, lax.rem(s + hop, seqs)).start()

    def small_three():
        for hop in range(1, seqs):
            owner = lax.rem(s + hop, seqs)
            pl.when(owner < owners)(to_owner(hop, owner).wait_send)
        for hop in range(1, seqs):
            pl.when(lax.rem(s + seqs - hop, seqs) < owners)(back(hop, 0, s).wait_recv)
            pl.when(s < owners)(back(hop, 0, s).wait_send)

    extra = {2: end_y, 4: small_one, 5: small_two}
    for phase in range(chunks + len(stages) - 1):
        for index in reversed(range(len(stages))):
            c = phase - index
            if 0 <= c < chunks:
                stages[index](c)
        if phase in extra:
            extra[phase]()
    small_three()


def tail(up, down, out, proj, source, weight, input1, select, small, dps, seqs):
    zs = seqs // 2
    dim, hidden = up.shape
    rows = proj.shape[0]
    chunk = hidden // 2
    chunks = 6
    width = -(-chunk // (128 * dps)) * 128
    block = dim // seqs
    steps = 4
    owners = small.shape[0]
    dma = pltpu.SemaphoreType.DMA
    return pl.pallas_call(
        functools.partial(tail_kernel, dps, seqs, chunks, chunk, width),
        out_shape=(
            jax.ShapeDtypeStruct((block, hidden), F32),
            jax.ShapeDtypeStruct((block, hidden), F32),
            jax.ShapeDtypeStruct((block, hidden), F32),
            jax.ShapeDtypeStruct((rows, dim), BF16),
            jax.ShapeDtypeStruct(small.shape, F32),
        ),
        in_specs=[VMEM] * 9,
        out_specs=(VMEM,) * 5,
        scratch_shapes=[
            pltpu.VMEM((dim, hidden), BF16),
            pltpu.VMEM((steps, rows // steps, dim), BF16),
            pltpu.VMEM((steps, rows // steps, dim), BF16),
            pltpu.VMEM((chunks, zs, block, chunk), BF16),
            pltpu.VMEM((chunks, dps, zs, block, width), BF16),
            pltpu.VMEM((chunks, dps, zs, block, width), BF16),
            pltpu.VMEM((chunks, zs, block, width), BF16),
            pltpu.VMEM((chunks, zs - 1, block, width), BF16),
            pltpu.VMEM((chunks, block, width), BF16),
            pltpu.VMEM((chunks, dps, block, width), BF16),
            pltpu.VMEM(small.shape, F32),
            pltpu.VMEM((seqs,) + small.shape[1:], F32),
            pltpu.VMEM(small.shape[1:], F32),
            pltpu.VMEM((dps,) + small.shape[1:], F32),
            dma((2, steps)),
            dma((2, chunks, zs)),
            dma((2, chunks, dps)),
            dma((2, chunks, zs)),
            dma((2, chunks, dps)),
            dma((2, 3, max(seqs, dps))),
        ],
        compiler_params=pltpu.CompilerParams(collective_id=7, has_side_effects=True, vmem_limit_bytes=60 << 20),
        name="tail",
    )(up, down, out, proj, source, weight, input1, select, small)


def memory_slots(id_row):
    count = id_row.shape[0]
    edge = jnp.full((READ_ROWS,), -1, jnp.int32)
    padded = jnp.concatenate([edge, id_row, edge])
    before = sum((padded[READ_ROWS - k:READ_ROWS - k + count] == id_row).astype(jnp.int32) for k in range(1, READ_ROWS + 1))
    behind = sum((padded[READ_ROWS + k:READ_ROWS + k + count] == id_row).astype(jnp.int32) for k in range(1, READ_ROWS + 1))
    return jnp.where(before < READ_ROWS, before, jnp.where(behind < READ_ROWS, 2 * READ_ROWS - 1 - behind, -1))


def document_blocks(id_row, own_ids, window_start, bq, bk):
    table = []
    for b in range(own_ids.shape[0] // bq):
        low, high = own_ids[b * bq], own_ids[b * bq + bq - 1]
        start = jnp.sum((id_row < low).astype(jnp.int32)) - window_start
        end = jnp.sum((id_row <= high).astype(jnp.int32)) - window_start
        first, last = start // bk, (end + bk - 1) // bk
        full_first, full_last = (start + bk - 1) // bk, end // bk
        whole = jnp.logical_and(low == high, full_first < full_last)
        table += [first, jnp.where(whole, full_first, first), jnp.where(whole, full_last, first), last]
    return jnp.stack(table).astype(jnp.int32)


def normalize(hidden, gain, shift):
    centre = jnp.mean(hidden, axis=-1, keepdims=True)
    centred = hidden - centre
    spread = jnp.mean(centred * centred, axis=-1, keepdims=True)
    return centred * lax.rsqrt(spread + NORM_EPS) * gain + shift


def gelu_exact(values):
    return jax.nn.gelu(values, approximate=False)


def column_sums(matrix):
    return jnp.sum(matrix.astype(F32), axis=0)


def on_device(dps, seqs, tokens, doc_ids, memory, qkv_weight, query_bias, value_bias, out_weight, out_bias, norm1_gain, norm1_bias, up_weight, up_bias, down_weight, down_bias, norm2_gain, norm2_bias, out_grad):
    rows = tokens.shape[1]
    width = qkv_weight.shape[2]
    heads = width // HEAD_DIM
    bq, bk = rows, 256
    own = REACH * rows
    pieces = 2 * REACH + 1
    s = lax.axis_index("seq")
    id_row = doc_ids[0]
    edge = jnp.full((own,), -1, jnp.int32)
    window_start = s * rows - own
    slots = memory_slots(id_row)
    window_slots = lax.dynamic_slice_in_dim(jnp.concatenate([edge, slots, edge]), s * rows, pieces * rows, 0)
    window_ids = lax.dynamic_slice_in_dim(jnp.concatenate([edge, id_row, edge]), s * rows, pieces * rows, 0)
    own_ids = window_ids[own:own + rows]
    blocks = document_blocks(id_row, own_ids, window_start, bq, bk)
    ids = jnp.broadcast_to(window_ids.astype(F32)[None], (8, pieces * rows))

    tokens_window = gather_window(tokens[0], seqs, 1).reshape(pieces * rows, -1)
    selector = window_slots[:, None] == jnp.arange(2 * READ_ROWS, dtype=jnp.int32)[None, :]
    memory_rows = jnp.dot(selector.astype(BF16), memory, preferred_element_type=F32).astype(BF16)
    source_window = jnp.where((window_slots >= 0)[:, None], memory_rows, tokens_window)
    projected = jnp.dot(source_window, qkv_weight.reshape(-1, 3 * width), preferred_element_type=F32)
    query = (projected[:, :width] + query_bias).astype(BF16) * 0.125
    key = projected[:, width:2 * width].astype(BF16)
    value = (projected[:, 2 * width:] + value_bias).astype(BF16)
    here = slice(own, own + rows)
    source = source_window[here]
    is_memory = (window_slots[here] >= 0)[:, None]

    mixed_low, logsums = attention_forward(blocks, query[here], key, value, ids, own, bq, bk)

    def both(part):
        low = part.astype(BF16)
        return low.astype(F32) + lax.ppermute(low, "tensor", [(0, 1), (1, 0)]).astype(F32)

    branch = both(jnp.einsum("tf,of->to", mixed_low, out_weight, preferred_element_type=F32)) + out_bias
    first_input = source.astype(F32) + branch
    first_out, first_pull = jax.vjp(normalize, first_input, norm1_gain, norm1_bias)
    first_low = first_out.astype(BF16)
    up_proj = jnp.dot(first_low, up_weight, preferred_element_type=F32) + up_bias
    act_full, gelu_pull = jax.vjp(gelu_exact, up_proj)
    act_low = act_full.astype(BF16)
    down_out = both(jnp.einsum("tf,of->to", act_low, down_weight, preferred_element_type=F32)) + down_bias
    result, second_pull = jax.vjp(normalize, first_out + down_out, norm2_gain, norm2_bias)
    output = result.astype(BF16)[None]
    grad_second, grad_gain2, grad_shift2 = second_pull(out_grad[0].astype(F32))
    down_grad = grad_second.astype(BF16)
    grad_down_weight = jnp.einsum("to,tf->of", down_grad, act_low, preferred_element_type=F32)
    act_grad = jnp.einsum("to,of->tf", down_grad, down_weight, preferred_element_type=F32)
    up_grad = gelu_pull(act_grad)[0].astype(BF16)
    grad_up_weight = jnp.einsum("td,tf->df", first_low, up_grad, preferred_element_type=F32)
    grad_first = grad_second + both(jnp.einsum("tf,df->td", up_grad, up_weight, preferred_element_type=F32))
    grad_input1, grad_gain1, grad_shift1 = first_pull(grad_first)
    branch_grad = grad_input1.astype(BF16)
    grad_out_weight = jnp.einsum("to,tf->of", branch_grad, mixed_low, preferred_element_type=F32)
    mixed_grad = jnp.einsum("to,of->tf", branch_grad, out_weight, preferred_element_type=F32).astype(BF16)
    along = jnp.sum((mixed_grad.astype(F32) * mixed_low.astype(F32)).reshape(rows, heads, HEAD_DIM), axis=-1)

    gap = jnp.zeros((rows, 8 - heads), F32)
    stats = jnp.concatenate([logsums[:, :heads], gap, along, gap], axis=1).T
    grads_window = gather_window(mixed_grad, seqs, 2).reshape(pieces * rows, -1)
    stats_window = gather_window(stats, seqs, 3, 1)
    stats_window = stats_window.transpose(1, 0, 2).reshape(16, pieces * rows)
    along_cols = jnp.pad(along, ((0, 0), (0, 128 - heads)))
    proj_grad = attention_backward(blocks, query, key, value, grads_window, ids, logsums, along_cols, stats_window, rows, own, bq, bk)

    select = jnp.pad(selector[here].astype(BF16), ((0, 0), (0, 12)))
    small = jnp.concatenate([
        jnp.stack([grad_gain1, grad_shift1, grad_gain2, grad_shift2, column_sums(branch_grad), column_sums(down_grad)]),
        column_sums(up_grad).reshape(2, -1), jnp.zeros((24, 2 * width), F32)])
    up_sum, down_sum, mix_sum, input_grad, small = tail(
        grad_up_weight.astype(BF16), grad_down_weight.astype(BF16), grad_out_weight.astype(BF16), proj_grad, source,
        qkv_weight.reshape(-1, 3 * width), grad_input1, select, small.reshape(4, 8, 2 * width), dps, seqs)
    small = small.reshape(32, 2 * width)
    input_grad = input_grad[None]
    piece = small.shape[1] // seqs
    vectors = lax.dynamic_slice_in_dim(small[:6], s * piece, piece, 1)
    memory_grad = small[9:29]
    return (
        output, input_grad, memory_grad,
        mix_sum[:, width:].reshape(-1, 3, width), small[8, :width], small[8, width:],
        mix_sum[:, :width], vectors[4], vectors[0], vectors[1],
        up_sum, small[6:8].reshape(-1), down_sum, vectors[5], vectors[2], vectors[3],
    )


def solution(mesh):
    in_specs = (
        P("dp", "seq", None), P("dp", None), P(), P(None, None, "tensor"), P("tensor"), P("tensor"), P(None, "tensor"), P(), P(), P(),
        P(None, "tensor"), P("tensor"), P(None, "tensor"), P(), P(), P(), P("dp", "seq", None),
    )
    out_specs = (
        P("dp", "seq", None), P("dp", "seq", None), P(), P("seq", None, "tensor"), P("tensor"), P("tensor"), P("seq", "tensor"), P("seq"), P("seq"), P("seq"),
        P("seq", "tensor"), P("tensor"), P("seq", "tensor"), P("seq"), P("seq"), P("seq"),
    )
    step = functools.partial(on_device, mesh.shape["dp"], mesh.shape["seq"])
    return jax.shard_map(step, mesh=mesh, in_specs=in_specs, out_specs=out_specs, check_vma=False)
```

```python
import functools

import jax
import jax.numpy as jnp
from jax import lax
from jax.experimental import pallas as pl
from jax.experimental.pallas import tpu as pltpu
from jax.sharding import PartitionSpec as P

HEAD_DIM = 64
READ_ROWS = 10
REACH = 3
NORM_EPS = 1e-05
F32, BF16 = jnp.float32, jnp.bfloat16
NT = (((1,), (1,)), ((), ()))
NN = (((1,), (0,)), ((), ()))
NEG = -1e30
FLOOR = -1e29
VMEM = pl.BlockSpec(memory_space=pltpu.VMEM)
SMEM = pl.BlockSpec(memory_space=pltpu.SMEM)


def remote(source, target, send_sem, recv_sem, **where):
    return pltpu.make_async_remote_copy(
        source, target, send_sem, recv_sem, device_id=where, device_id_type=pl.DeviceIdType.MESH
    )


def greet(partners):
    barrier = pltpu.get_barrier_semaphore()
    total = 0
    for present, where in partners:
        total = total + present.astype(jnp.int32)

        @pl.when(present)
        def _():
            pl.semaphore_signal(barrier, inc=1, device_id=where, device_id_type=pl.DeviceIdType.MESH)

    pl.semaphore_wait(barrier, total)


def dot(a, b, dims=NN):
    return lax.dot_general(a, b, dims, preferred_element_type=F32)

def low_half(shape):
    return lax.broadcasted_iota(jnp.int32, shape, len(shape) - 1) < 64

def id_columns(ids_ref, start, count):
    row = jnp.broadcast_to(ids_ref[0:1, pl.ds(start, count)], (128, count))
    return jnp.transpose(row)

def wide(x, count):
    return jnp.concatenate([x] * (count // 128), axis=1)

def split_heads(source_ref, rows, target_ref, pairs, keep):
    for pair in range(pairs):
        block = source_ref[rows, pair * 128:pair * 128 + 128]
        target_ref[2 * pair] = jnp.where(keep, block, jnp.zeros_like(block))
        target_ref[2 * pair + 1] = jnp.where(keep, jnp.zeros_like(block), block)

def sweep(rng_ref, b, body):
    first, full_first, full_last, last = (rng_ref[4 * b + i] for i in range(4))
    lax.fori_loop(full_first, full_last, lambda j, c: body(j, False, c), 0)

    def edge(i, c):
        j = first + i
        return body(jnp.where(j < full_first, j, j + full_last - full_first), True, c)

    lax.fori_loop(0, last - first - (full_last - full_first), edge, 0)

def fwd_kernel(bq, bk, own, rng_ref, q_ref, k_ref, v_ref, ids_ref, o_ref, lse_ref, acc_ref, max_ref, q_heads, cols_ref):
    pairs = q_ref.shape[1] // 128
    rows = o_ref.shape[0]
    low_q, low_k = low_half((bq, 128)), low_half((bk, 128))

    def block(qb, carry):
        mine = pl.ds(pl.multiple_of(qb * bq, bq), bq)
        cols_ref[...] = id_columns(ids_ref, pl.multiple_of(own + qb * bq, bq), bq)
        split_heads(q_ref, pl.ds(pl.multiple_of(own + qb * bq, bq), bq), q_heads, pairs, low_q)
        acc_ref[...] = jnp.zeros_like(acc_ref)
        max_ref[...] = jnp.full_like(max_ref, FLOOR)

        def step(j, masked, carry):
            there = pl.ds(pl.multiple_of(j * bk, bk), bk)
            def pair_step(pair, carry):
                lanes = pl.ds(pair * 128, 128)
                key = k_ref[there, lanes]
                value = v_ref[there, lanes]
                for odd in range(2):
                    head = 2 * pair + odd
                    scores = dot(q_heads[head], key, NT)
                    if masked:
                        scores = jnp.where(wide(cols_ref[...], bk) == ids_ref[0:1, there], scores, NEG)
                    old = max_ref[head]
                    new = jnp.maximum(old, jnp.max(scores, axis=1, keepdims=True))
                    probs = jnp.exp(scores - wide(new, bk)).astype(BF16)
                    ones = jnp.where(low_k if odd == 0 else ~low_k, value, jnp.ones_like(value))
                    acc_ref[head] = acc_ref[head] * jnp.exp(old - new) + dot(probs, ones)
                    max_ref[head] = new
                return carry
            for pair in range(pairs):
                pair_step(pair, carry)
            return carry

        sweep(rng_ref, qb, step)
        stats = jnp.zeros((bq, 128), F32)
        lane = lax.broadcasted_iota(jnp.int32, (bq, 128), 1)
        for pair in range(pairs):
            even, odd = acc_ref[2 * pair], acc_ref[2 * pair + 1]
            total_even, total_odd = even[:, 64:65], odd[:, 0:1]
            mixed = jnp.where(low_q, even / total_even, odd / total_odd)
            o_ref[mine, pair * 128:pair * 128 + 128] = mixed.astype(BF16)
            stats = jnp.where(lane == 2 * pair, max_ref[2 * pair] + jnp.log(total_even), stats)
            stats = jnp.where(lane == 2 * pair + 1, max_ref[2 * pair + 1] + jnp.log(total_odd), stats)
        lse_ref[mine, :] = stats
        return carry

    lax.fori_loop(0, rows // bq, block, 0)

def attention_forward(rng, query, key, value, ids, rows, own, bq=256, bk=256):
    width = query.shape[1]
    heads = width // 64
    return pl.pallas_call(
        functools.partial(fwd_kernel, bq, bk, own),
        out_shape=(jax.ShapeDtypeStruct((rows, width), BF16), jax.ShapeDtypeStruct((rows, 128), F32)),
        in_specs=[pl.BlockSpec(memory_space=pltpu.SMEM)] + [pl.BlockSpec(memory_space=pltpu.VMEM)] * 4,
        out_specs=(pl.BlockSpec(memory_space=pltpu.VMEM),) * 2,
        scratch_shapes=[pltpu.VMEM((heads, bq, 128), F32), pltpu.VMEM((heads, bq, 128), F32), pltpu.VMEM((heads, bq, 128), BF16), pltpu.VMEM((bq, 128), F32)],
        compiler_params=pltpu.CompilerParams(vmem_limit_bytes=24 << 20),
        name="attention_forward",
    )(rng, query, key, value, ids)

def bwd_kernel(bq, bk, own, rng_ref, q_ref, k_ref, v_ref, g_ref, ids_ref, lse_ref, along_ref, rows_ref, out_ref, dq_acc, dk_acc, dv_acc, q_heads, k_heads, v_heads, g_heads, lse_cols, along_cols, cols_ref):
    rows, width = out_ref.shape[0], q_ref.shape[1]
    pairs = width // 128
    heads = 2 * pairs
    low_q = low_half((bq, 128))

    def block(b, carry):
        start = pl.multiple_of(b * bq, bq)
        mine = pl.ds(start, bq)
        here = pl.ds(pl.multiple_of(own + start, bq), bq)
        cols_ref[...] = id_columns(ids_ref, pl.multiple_of(own + start, bq), bq)
        for source, target in ((q_ref, q_heads), (k_ref, k_heads), (v_ref, v_heads), (g_ref, g_heads)):
            split_heads(source, here, target, pairs, low_q)
        for head in range(heads):
            lse_cols[head] = jnp.broadcast_to(lse_ref[mine, head:head + 1], (bq, 128))
            along_cols[head] = jnp.broadcast_to(along_ref[mine, head:head + 1], (bq, 128))
        for acc in (dq_acc, dk_acc, dv_acc):
            acc[...] = jnp.zeros_like(acc)

        def step(j, masked, carry):
            there = pl.ds(pl.multiple_of(j * bk, bk), bk)
            def pair_step(pair, carry):
                lanes = pl.ds(pair * 128, 128)
                q_far, k_far, v_far, g_far = (r[there, lanes] for r in (q_ref, k_ref, v_ref, g_ref))
                def hide(x):
                    return jnp.where(wide(cols_ref[...], bk) == ids_ref[0:1, there], x, 0.0) if masked else x
                for odd in range(2):
                    head = 2 * pair + odd
                    scores = dot(q_heads[head], k_far, NT)
                    probs = hide(jnp.exp(scores - wide(lse_cols[head], bk)))
                    slope = dot(g_heads[head], v_far, NT)
                    grad = (probs * (slope - wide(along_cols[head], bk))).astype(BF16)
                    dq_acc[head] += dot(grad, k_far)
                    scores = dot(k_heads[head], q_far, NT)
                    probs = hide(jnp.exp(scores - rows_ref[pl.ds(head, 1), there]))
                    slope = dot(v_heads[head], g_far, NT)
                    grad = (probs * (slope - rows_ref[pl.ds(8 + head, 1), there])).astype(BF16)
                    dv_acc[head] += dot(probs.astype(BF16), g_far)
                    dk_acc[head] += dot(grad, q_far)
                return carry
            for pair in range(pairs):
                pair_step(pair, carry)
            return carry

        sweep(rng_ref, b, step)
        for which, (acc, factor) in enumerate(((dq_acc, 0.125), (dk_acc, 1.0), (dv_acc, 1.0))):
            for pair in range(pairs):
                both = jnp.where(low_q, acc[2 * pair], acc[2 * pair + 1]) * factor
                out_ref[mine, which * width + pair * 128:which * width + pair * 128 + 128] = both.astype(BF16)
        return carry

    lax.fori_loop(0, rows // bq, block, 0)

def attention_backward(rng, query, key, value, grads, ids, lse, along, stat_rows, rows, own, bq=256, bk=256):
    width = query.shape[1]
    heads = width // 64
    return pl.pallas_call(
        functools.partial(bwd_kernel, bq, bk, own),
        out_shape=jax.ShapeDtypeStruct((rows, 3 * width), BF16),
        in_specs=[pl.BlockSpec(memory_space=pltpu.SMEM)] + [pl.BlockSpec(memory_space=pltpu.VMEM)] * 8,
        out_specs=pl.BlockSpec(memory_space=pltpu.VMEM),
        scratch_shapes=[pltpu.VMEM((heads, bq, 128), F32)] * 3 + [pltpu.VMEM((heads, bq, 128), BF16)] * 4 + [pltpu.VMEM((heads, bq, 128), F32)] * 2 + [pltpu.VMEM((bq, 128), F32)],
        compiler_params=pltpu.CompilerParams(vmem_limit_bytes=40 << 20),
        name="attention_backward",
    )(rng, query, key, value, grads, ids, lse, along, stat_rows)

class Halo:
    def __init__(self, count, pieces, send_sem, recv_sem):
        self.count, self.pieces, self.send_sem, self.recv_sem = count, pieces, send_sem, recv_sem
        s = self.s = lax.axis_index("seq")
        self.core = lax.rem(s, 2)
        self.sibling = s + 1 - 2 * self.core
        self.left, self.right = s >= 2, s < count - 2

    def greet(self):
        s, count = self.s, self.count
        greet([(s >= k, {"seq": s - k}) for k in (1, 2)] + [(s < count - k, {"seq": s + k}) for k in (1, 2)])

    def own(self, part, kind, slot, target):
        source, window = self.pieces[part]
        return remote(source, window(slot), self.send_sem.at[kind, part], self.recv_sem.at[slot, part], seq=target)

    def moved(self, part, kind, held, slot, target):
        window = self.pieces[part][1]
        return remote(window(held), window(slot), self.send_sem.at[kind, part], self.recv_sem.at[slot, part], seq=target)

    def first_copies(self, part):
        s, core = self.s, self.core
        return (
            (self.right, self.own(part, 0, 1, s + 2)),
            (self.left, self.own(part, 1, 5, s - 2)),
            (core == 0, self.own(part, 2, 2, self.sibling)),
            (core == 1, self.own(part, 2, 4, self.sibling)),
        )

    def from_left(self, part):
        s, core, left, right = self.s, self.core, self.left, self.right
        return (
            (jnp.logical_and(left, jnp.logical_and(core == 1, right)), self.moved(part, 3, 1, 0, s + 1)),
            (jnp.logical_and(left, core == 0), self.moved(part, 4, 1, 0, self.sibling)),
            (jnp.logical_and(left, core == 1), self.moved(part, 4, 1, 2, self.sibling)),
        )

    def from_right(self, part):
        s, core, left, right = self.s, self.core, self.left, self.right
        return (
            (jnp.logical_and(right, jnp.logical_and(core == 0, left)), self.moved(part, 5, 5, 6, s - 1)),
            (jnp.logical_and(right, core == 0), self.moved(part, 6, 5, 4, self.sibling)),
            (jnp.logical_and(right, core == 1), self.moved(part, 6, 5, 6, self.sibling)),
        )

    def each(self, copies, act):
        for present, copy in copies:
            pl.when(present)(functools.partial(act, copy))

    def send(self, part):
        self.each(self.first_copies(part), lambda copy: copy.start())

    def arrived(self, slot, part):
        self.own(part, 0, slot, self.s).wait_recv()

    def relay(self, part):
        pl.when(self.left)(functools.partial(self.arrived, 1, part))
        self.each(self.from_left(part), lambda copy: copy.start())
        pl.when(self.right)(functools.partial(self.arrived, 5, part))
        self.each(self.from_right(part), lambda copy: copy.start())

    def present(self, slot):
        block = self.s + slot - REACH
        return jnp.logical_and(block >= 0, block < self.count)

    def receive(self, slot):
        for part in range(len(self.pieces)):
            pl.when(self.present(slot))(functools.partial(self.arrived, slot, part))

    def finish(self):
        for part in range(len(self.pieces)):
            self.each(self.first_copies(part) + self.from_left(part) + self.from_right(part), lambda copy: copy.wait_send())


def project_kernel(count, parts, own_ref, slots_ref, memory_ref, weight_ref, query_bias_ref, value_bias_ref,
                   q_ref, k_ref, v_ref, source_ref, window_ref, send_sem, recv_sem):
    block = own_ref.shape[0]
    rows = block // parts
    tile = 256
    tiles = block // tile

    def piece(part):
        return own_ref.at[pl.ds(part * rows, rows)], lambda slot: window_ref.at[pl.ds(slot * block + part * rows, rows)]

    halo = Halo(count, [piece(part) for part in range(parts)], send_sem, recv_sem)
    halo.greet()
    for part in range(parts):
        halo.send(part)

    def project(load, start, keep):
        hot = (lax.broadcasted_iota(jnp.int32, (32, tile), 0) == slots_ref[0:1, pl.ds(start, tile)]).astype(F32).astype(BF16)
        tn = (((0,), (0,)), ((), ()))
        chosen = dot(hot, memory_ref[...], tn)
        inside = wide(dot(hot, jnp.ones((32, 128), BF16), tn), chosen.shape[1])
        source = jnp.where(inside > 0.5, chosen, load().astype(F32)).astype(BF16)
        keep(source)
        out = pl.ds(start, tile)
        q_ref[out, :] = (dot(source, weight_ref[0]) + query_bias_ref[...]).astype(BF16) * 0.125
        k_ref[out, :] = dot(source, weight_ref[1]).astype(BF16)
        v_ref[out, :] = (dot(source, weight_ref[2]) + value_bias_ref[...]).astype(BF16)

    def own_tile(i, carry):
        at = pl.ds(pl.multiple_of(i * tile, tile), tile)

        def keep(source):
            source_ref[at, :] = source

        project(lambda: own_ref[at, :], pl.multiple_of(REACH * block + i * tile, tile), keep)
        return carry

    lax.fori_loop(0, tiles, own_tile, 0)
    for part in range(parts):
        halo.relay(part)

    def two_blocks(low, high):
        def step(i, carry):
            slot = low + (high - low) * (i // tiles)

            @pl.when(halo.present(slot))
            def _():
                start = pl.multiple_of(slot * block + lax.rem(i, tiles) * tile, tile)
                project(lambda: window_ref[pl.ds(start, tile), :], start, lambda source: None)

            return carry

        lax.fori_loop(0, 2 * tiles, step, 0)

    two_blocks(1, 5)
    for slots in ((2, 4), (0, 6)):
        for slot in slots:
            halo.receive(slot)
        two_blocks(*slots)
    halo.finish()


def project_window(own, slots, memory, weight, query_bias, value_bias, count, collective_id, parts=2):
    rows, dim = own.shape
    width = weight.shape[2]
    total = (2 * REACH + 1) * rows
    wide_out = jax.ShapeDtypeStruct((total, width), BF16)
    return pl.pallas_call(
        functools.partial(project_kernel, count, parts),
        out_shape=(wide_out, wide_out, wide_out, jax.ShapeDtypeStruct((rows, dim), BF16)),
        in_specs=[VMEM] * 6,
        out_specs=(VMEM,) * 4,
        scratch_shapes=[
            pltpu.VMEM((total, dim), BF16),
            pltpu.SemaphoreType.DMA((7, parts)),
            pltpu.SemaphoreType.DMA((7, parts)),
        ],
        compiler_params=pltpu.CompilerParams(collective_id=collective_id, has_side_effects=True, vmem_limit_bytes=40 << 20),
        name="project_window",
    )(own, slots, memory, weight, query_bias, value_bias)


def grads_kernel(count, parts, grad_ref, mixed_ref, lse_ref, window_ref, stats_ref, along_ref, own_stats, send_sem, recv_sem):
    block, width = grad_ref.shape
    rows = block // parts

    def piece(part):
        return grad_ref.at[pl.ds(part * rows, rows)], lambda slot: window_ref.at[pl.ds(slot * block + part * rows, rows)]

    stats_piece = own_stats, lambda slot: stats_ref.at[:, pl.ds(slot * block, block)]
    halo = Halo(count, [piece(part) for part in range(parts)] + [stats_piece], send_sem, recv_sem)
    halo.greet()
    for part in range(parts):
        halo.send(part)
    window_ref[REACH * block:(REACH + 1) * block, :] = grad_ref[...]
    lane = lax.broadcasted_iota(jnp.int32, (block, 128), 1)
    along = jnp.zeros((block, 128), F32)
    for pair in range(width // 128):
        lanes = slice(pair * 128, pair * 128 + 128)
        product = grad_ref[:, lanes].astype(F32) * mixed_ref[:, lanes].astype(F32)
        even = jnp.sum(jnp.where(lane < 64, product, 0.0), axis=1, keepdims=True)
        odd = jnp.sum(jnp.where(lane < 64, 0.0, product), axis=1, keepdims=True)
        along = jnp.where(lane == 2 * pair, even, jnp.where(lane == 2 * pair + 1, odd, along))
    along_ref[...] = along
    own_stats[0:8, :] = jnp.transpose(lse_ref[...])[0:8, :]
    own_stats[8:16, :] = jnp.transpose(along)[0:8, :]
    stats_ref[:, REACH * block:(REACH + 1) * block] = own_stats[...]
    halo.send(parts)
    for part in range(parts + 1):
        halo.relay(part)
    for slot in (0, 2, 4, 6):
        halo.receive(slot)
    halo.finish()


def gather_grads(grad, mixed, lse, count, collective_id, parts=2):
    rows, width = grad.shape
    total = (2 * REACH + 1) * rows
    return pl.pallas_call(
        functools.partial(grads_kernel, count, parts),
        out_shape=(
            jax.ShapeDtypeStruct((total, width), BF16),
            jax.ShapeDtypeStruct((16, total), F32),
            jax.ShapeDtypeStruct((rows, 128), F32),
        ),
        in_specs=[VMEM] * 3,
        out_specs=(VMEM,) * 3,
        scratch_shapes=[
            pltpu.VMEM((16, rows), F32),
            pltpu.SemaphoreType.DMA((7, parts + 1)),
            pltpu.SemaphoreType.DMA((7, parts + 1)),
        ],
        compiler_params=pltpu.CompilerParams(collective_id=collective_id, has_side_effects=True, vmem_limit_bytes=24 << 20),
        name="gather_grads",
    )(grad, mixed, lse)


def split_dot(left, right, dims):
    high = right.astype(BF16)
    low = (right - high.astype(F32)).astype(BF16)
    return dot(left, high, dims) + dot(left, low, dims)


def tail_kernel(dps, seqs, chunks, chunk, width, up_ref, down_ref, out_grad_ref, proj_ref, source_ref, weight_ref, input1_ref, select_ref, small_ref,
                up_out, down_out, out_out, qkv_out, input_out, small_out,
                mix, y_send, y_recv, a_recv, parts, b_recv, mine, c_recv, last, d_recv, small_in, small_recv, small_mine, small_dp,
                y_sems, a_sems, b_sems, c_sems, d_sems, s_sems):
    zs = seqs // 2
    bits = zs.bit_length() - 1
    t, d, s = lax.axis_index("tensor"), lax.axis_index("dp"), lax.axis_index("seq")
    z, core = s // 2, lax.rem(s, 2)
    sibling = s + 1 - 2 * core
    shares = -(-chunk // width)
    owners = small_ref.shape[0]
    block = up_ref.shape[0] // seqs
    rows, columns = proj_ref.shape
    third = columns // 3
    steps = y_send.shape[0]
    span = rows // steps
    true = s >= 0
    partners = [(true, {"seq": lax.rem(s + k, seqs)}) for k in range(1, seqs)]
    partners += [(true, {"dp": lax.rem(d + k, dps)}) for k in range(1, dps)]
    partners += [(true, {"tensor": 1 - t})]
    greet(partners)
    grads = (up_ref, down_ref, mix)
    per = up_ref.shape[1] // chunk

    def piece(c):
        return grads[c // per], (c % per) * chunk

    def a_copy(c, j):
        ref, at = piece(c)
        start = pl.multiple_of((2 * j + 1 - core) * block, 16)
        return remote(ref.at[pl.ds(start, block), pl.ds(at, chunk)], a_recv.at[c, j], a_sems.at[0, c, j], a_sems.at[1, c, j], seq=sibling)

    def b_copy(c, k):
        other = lax.rem(d + k, dps)
        return other, remote(parts.at[c, other], b_recv.at[c, k], b_sems.at[0, c, k], b_sems.at[1, c, k], dp=other)

    def c_copies(c, b):
        size = 2 << b
        high = lax.rem(z // (1 << b), 2)
        partner = z + (1 << b) - (size * high)
        low = lax.rem(partner, size)
        return [
            remote(mine.at[c, i * size + low], c_recv.at[c, (1 << b) * 0 + first_slot(b) + i], c_sems.at[0, c, first_slot(b) + i], c_sems.at[1, c, first_slot(b) + i], seq=2 * partner + core)
            for i in range(zs // size)
        ]

    def first_slot(b):
        return sum(zs // (2 << e) for e in range(b))

    def d_copy(c, k):
        return remote(last.at[c], d_recv.at[c, k], d_sems.at[0, c, k], d_sems.at[1, c, k], dp=lax.rem(d + k, dps))

    def start_a(c):
        for j in range(zs):
            a_copy(c, j).start()

    def end_a(c):
        ref, at = piece(c)
        for j in range(zs):
            a_copy(c, j).wait()
            start = pl.multiple_of((2 * j + core) * block, 16)
            for p in range(shares):
                real = min(width, chunk - p * width)
                lanes = pl.ds(at + p * width, real)
                total = ref[pl.ds(start, block), lanes].astype(F32) + a_recv[c, j, :, p * width:p * width + real].astype(F32)
                parts[c, p, j, :, 0:real] = total.astype(BF16)
                if real < width:
                    parts[c, p, j, :, real:width] = jnp.zeros((block, width - real), BF16)
        for k in range(1, dps):
            other, copy = b_copy(c, k)
            pl.when(other < shares)(copy.start)

    def end_b(c):
        for k in range(1, dps):
            other, copy = b_copy(c, k)
            pl.when(other < shares)(copy.wait_send)

        @pl.when(d < shares)
        def _():
            for k in range(1, dps):
                b_copy(c, k)[1].wait_recv()
            for j in range(zs):
                total = parts[c, d, j].astype(F32)
                for k in range(1, dps):
                    total = total + b_recv[c, k, j].astype(F32)
                mine[c, j] = total.astype(BF16)
            for copy in c_copies(c, 0):
                copy.start()

    def end_c(c, b):
        size = 2 << b
        kept = lax.rem(z, size)

        @pl.when(d < shares)
        def _():
            for i, copy in enumerate(c_copies(c, b)):
                copy.wait()
                held = mine[c, i * size + kept].astype(F32) + c_recv[c, first_slot(b) + i].astype(F32)
                if b < bits - 1:
                    mine[c, i * size + kept] = held.astype(BF16)
                else:
                    last[c] = held.astype(BF16)
            if b < bits - 1:
                for copy in c_copies(c, b + 1):
                    copy.start()
            else:
                for k in range(1, dps):
                    d_copy(c, k).start()

    def end_d(c):
        at = (c % per) * chunk

        def put(share, value):
            for p in range(shares):
                real = min(width, chunk - p * width)
                first = at + p * width

                @pl.when(share == p)
                def _():
                    if c < 2 * per:
                        (up_out, down_out)[c // per][:, first:first + real] = value[:, 0:real].astype(F32)
                        return
                    for lane in range(0, real, 128):
                        which, column = divmod(first + lane, third)
                        part = value[:, lane:lane + 128].astype(F32)
                        if which == 0:
                            out_out[:, column:column + 128] = part
                        else:
                            qkv_out[which - 1, :, column:column + 128] = part

        @pl.when(d < shares)
        def _():
            put(d, last[c])
            for k in range(1, dps):
                d_copy(c, k).wait_send()
        for k in range(1, dps):
            share = lax.rem(d + dps - k, dps)

            @pl.when(share < shares)
            def _():
                d_copy(c, k).wait_recv()
                put(share, d_recv[c, k])

    stages = [end_a, end_b] + [functools.partial(end_c, b=b) for b in range(bits)] + [end_d]

    def y_copy(i):
        return remote(y_send.at[i], y_recv.at[i], y_sems.at[0, i], y_sems.at[1, i], tensor=1 - t)

    for c in range(2 * per):
        start_a(c)
    for i in range(steps):
        at = slice(i * span, (i + 1) * span)
        y_send[i] = sum(dot(proj_ref[at, j * third:(j + 1) * third], weight_ref[j], NT) for j in range(3)).astype(BF16)
        y_copy(i).start()
    out_width = out_grad_ref.shape[1]
    mix[:, 0:out_width] = out_grad_ref[...]
    for i in range(3):
        part = lax.dot_general(source_ref[...], proj_ref[:, i * third:(i + 1) * third], (((0,), (0,)), ((), ())), preferred_element_type=F32)
        mix[:, out_width + i * third:out_width + (i + 1) * third] = part.astype(BF16)
    for c in range(2 * per, chunks):
        start_a(c)
    for i in range(owners):
        small_in[i] = small_ref[i]
    small_in[1, 0:1, 0:third] = jnp.sum(proj_ref[:, 0:third].astype(F32), axis=0, keepdims=True)
    small_in[1, 0:1, third:2 * third] = jnp.sum(proj_ref[:, 2 * third:3 * third].astype(F32), axis=0, keepdims=True)

    def end_y():
        memory = jnp.zeros((32, input_out.shape[1]), F32)
        for i in range(steps):
            y_copy(i).wait()
            at = slice(i * span, (i + 1) * span)
            total = input1_ref[at, :] + (y_send[i].astype(F32) + y_recv[i].astype(F32))
            select = select_ref[at, :]
            memory = memory + split_dot(select, total, (((0,), (0,)), ((), ())))
            inside = dot(select, jnp.ones((32, total.shape[1]), BF16))
            input_out[at, :] = jnp.where(inside > 0.5, 0.0, total).astype(BF16)
        small_in[1, 1:8, :] = memory[0:7]
        small_in[2] = memory[7:15]
        small_in[3, 0:5, :] = memory[15:20]
        for hop in range(1, seqs):
            owner = lax.rem(s + hop, seqs)
            pl.when(owner < owners)(to_owner(hop, owner).start)

    def to_owner(hop, owner):
        return remote(small_in.at[owner], small_recv.at[hop], s_sems.at[0, 0, hop], s_sems.at[1, 0, hop], seq=owner)

    def across(k):
        return remote(small_mine, small_dp.at[k], s_sems.at[0, 1, k], s_sems.at[1, 1, k], dp=lax.rem(d + k, dps))

    def back(hop, owner, target):
        return remote(small_out.at[owner], small_out.at[owner], s_sems.at[0, 2, hop], s_sems.at[1, 2, hop], seq=target)

    def small_one():
        @pl.when(s < owners)
        def _():
            total = small_in[s]
            for hop in range(1, seqs):
                to_owner(hop, s).wait_recv()
                total = total + small_recv[hop]
            small_mine[...] = total
            for k in range(1, dps):
                across(k).start()

    def small_two():
        @pl.when(s < owners)
        def _():
            small_dp[0] = small_mine[...]
            for k in range(1, dps):
                across(k).wait()
            ordered = jnp.zeros(small_mine.shape, F32)
            for index in range(dps):
                ordered = ordered + small_dp[lax.rem(d + dps - index, dps)]
            small_out[s] = ordered
            for hop in range(1, seqs):
                back(hop, s, lax.rem(s + hop, seqs)).start()

    def small_three():
        for hop in range(1, seqs):
            owner = lax.rem(s + hop, seqs)
            pl.when(owner < owners)(to_owner(hop, owner).wait_send)
        for hop in range(1, seqs):
            pl.when(lax.rem(s + seqs - hop, seqs) < owners)(back(hop, 0, s).wait_recv)
            pl.when(s < owners)(back(hop, 0, s).wait_send)

    extra = {2: end_y, 4: small_one, 5: small_two}
    for phase in range(chunks + len(stages) - 1):
        for index in reversed(range(len(stages))):
            c = phase - index
            if 0 <= c < chunks:
                stages[index](c)
        if phase in extra:
            extra[phase]()
    small_three()


def tail(up, down, out, proj, source, weight, input1, select, small, dps, seqs):
    zs = seqs // 2
    dim, hidden = up.shape
    rows = proj.shape[0]
    chunk = hidden // 2
    chunks = 6
    width = -(-chunk // (128 * dps)) * 128
    block = dim // seqs
    steps = 4
    owners = small.shape[0]
    dma = pltpu.SemaphoreType.DMA
    return pl.pallas_call(
        functools.partial(tail_kernel, dps, seqs, chunks, chunk, width),
        out_shape=(
            jax.ShapeDtypeStruct((block, hidden), F32),
            jax.ShapeDtypeStruct((block, hidden), F32),
            jax.ShapeDtypeStruct((block, out.shape[1]), F32),
            jax.ShapeDtypeStruct((3, block, out.shape[1]), F32),
            jax.ShapeDtypeStruct((rows, dim), BF16),
            jax.ShapeDtypeStruct(small.shape, F32),
        ),
        in_specs=[VMEM] * 9,
        out_specs=(VMEM,) * 6,
        scratch_shapes=[
            pltpu.VMEM((dim, hidden), BF16),
            pltpu.VMEM((steps, rows // steps, dim), BF16),
            pltpu.VMEM((steps, rows // steps, dim), BF16),
            pltpu.VMEM((chunks, zs, block, chunk), BF16),
            pltpu.VMEM((chunks, dps, zs, block, width), BF16),
            pltpu.VMEM((chunks, dps, zs, block, width), BF16),
            pltpu.VMEM((chunks, zs, block, width), BF16),
            pltpu.VMEM((chunks, zs - 1, block, width), BF16),
            pltpu.VMEM((chunks, block, width), BF16),
            pltpu.VMEM((chunks, dps, block, width), BF16),
            pltpu.VMEM(small.shape, F32),
            pltpu.VMEM((seqs,) + small.shape[1:], F32),
            pltpu.VMEM(small.shape[1:], F32),
            pltpu.VMEM((dps,) + small.shape[1:], F32),
            dma((2, steps)),
            dma((2, chunks, zs)),
            dma((2, chunks, dps)),
            dma((2, chunks, zs)),
            dma((2, chunks, dps)),
            dma((2, 3, max(seqs, dps))),
        ],
        compiler_params=pltpu.CompilerParams(collective_id=7, has_side_effects=True, vmem_limit_bytes=60 << 20),
        name="tail",
    )(up, down, out, proj, source, weight, input1, select, small)


def memory_slots(id_row):
    count = id_row.shape[0]
    edge = jnp.full((READ_ROWS,), -1, jnp.int32)
    padded = jnp.concatenate([edge, id_row, edge])
    before = sum((padded[READ_ROWS - k:READ_ROWS - k + count] == id_row).astype(jnp.int32) for k in range(1, READ_ROWS + 1))
    behind = sum((padded[READ_ROWS + k:READ_ROWS + k + count] == id_row).astype(jnp.int32) for k in range(1, READ_ROWS + 1))
    return jnp.where(before < READ_ROWS, before, jnp.where(behind < READ_ROWS, 2 * READ_ROWS - 1 - behind, -1))


def document_blocks(id_row, own_ids, window_start, bq, bk):
    table = []
    for b in range(own_ids.shape[0] // bq):
        low, high = own_ids[b * bq], own_ids[b * bq + bq - 1]
        start = jnp.sum((id_row < low).astype(jnp.int32)) - window_start
        end = jnp.sum((id_row <= high).astype(jnp.int32)) - window_start
        first, last = start // bk, (end + bk - 1) // bk
        full_first, full_last = (start + bk - 1) // bk, end // bk
        whole = jnp.logical_and(low == high, full_first < full_last)
        table += [first, jnp.where(whole, full_first, first), jnp.where(whole, full_last, first), last]
    return jnp.stack(table).astype(jnp.int32)


def normalize(hidden, gain, shift):
    centre = jnp.mean(hidden, axis=-1, keepdims=True)
    centred = hidden - centre
    spread = jnp.mean(centred * centred, axis=-1, keepdims=True)
    return centred * lax.rsqrt(spread + NORM_EPS) * gain + shift


def gelu_exact(values):
    return jax.nn.gelu(values, approximate=False)


def column_sums(matrix):
    return jnp.sum(matrix.astype(F32), axis=0)


def on_device(dps, seqs, tokens, doc_ids, memory, qkv_weight, query_bias, value_bias, out_weight, out_bias, norm1_gain, norm1_bias, up_weight, up_bias, down_weight, down_bias, norm2_gain, norm2_bias, out_grad):
    rows = tokens.shape[1]
    width = qkv_weight.shape[2]
    heads = width // HEAD_DIM
    bq, bk = rows, 256
    own = REACH * rows
    pieces = 2 * REACH + 1
    s = lax.axis_index("seq")
    id_row = doc_ids[0]
    edge = jnp.full((own,), -1, jnp.int32)
    window_start = s * rows - own
    slots = memory_slots(id_row)
    window_slots = lax.dynamic_slice_in_dim(jnp.concatenate([edge, slots, edge]), s * rows, pieces * rows, 0)
    window_ids = lax.dynamic_slice_in_dim(jnp.concatenate([edge, id_row, edge]), s * rows, pieces * rows, 0)
    own_ids = window_ids[own:own + rows]
    blocks = document_blocks(id_row, own_ids, window_start, bq, bk)
    ids = jnp.broadcast_to(window_ids.astype(F32)[None], (8, pieces * rows))

    weight = qkv_weight.transpose(1, 0, 2)
    slots_row = jnp.broadcast_to(window_slots[None], (8, pieces * rows))
    memory_pad = jnp.pad(memory, ((0, 32 - memory.shape[0]), (0, 0)))
    query, key, value, source = project_window(
        tokens[0], slots_row, memory_pad, weight, query_bias[None], value_bias[None], seqs, 1)
    own_slots = window_slots[own:own + rows]

    mixed_low, logsums = attention_forward(blocks, query, key, value, ids, rows, own, bq, bk)

    def both(part):
        low = part.astype(BF16)
        return low.astype(F32) + lax.ppermute(low, "tensor", [(0, 1), (1, 0)]).astype(F32)

    branch = both(jnp.einsum("tf,of->to", mixed_low, out_weight, preferred_element_type=F32)) + out_bias
    first_input = source.astype(F32) + branch
    first_out, first_pull = jax.vjp(normalize, first_input, norm1_gain, norm1_bias)
    first_low = first_out.astype(BF16)
    up_proj = jnp.dot(first_low, up_weight, preferred_element_type=F32) + up_bias
    act_full, gelu_pull = jax.vjp(gelu_exact, up_proj)
    act_low = act_full.astype(BF16)
    down_out = both(jnp.einsum("tf,of->to", act_low, down_weight, preferred_element_type=F32)) + down_bias
    result, second_pull = jax.vjp(normalize, first_out + down_out, norm2_gain, norm2_bias)
    output = result.astype(BF16)[None]
    grad_second, grad_gain2, grad_shift2 = second_pull(out_grad[0].astype(F32))
    down_grad = grad_second.astype(BF16)
    grad_down_weight = jnp.einsum("to,tf->of", down_grad, act_low, preferred_element_type=F32)
    act_grad = jnp.einsum("to,of->tf", down_grad, down_weight, preferred_element_type=F32)
    up_grad = gelu_pull(act_grad)[0].astype(BF16)
    grad_up_weight = jnp.einsum("td,tf->df", first_low, up_grad, preferred_element_type=F32)
    grad_first = grad_second + both(jnp.einsum("tf,df->td", up_grad, up_weight, preferred_element_type=F32))
    grad_input1, grad_gain1, grad_shift1 = first_pull(grad_first)
    branch_grad = grad_input1.astype(BF16)
    grad_out_weight = jnp.einsum("to,tf->of", branch_grad, mixed_low, preferred_element_type=F32)
    mixed_grad = jnp.einsum("to,of->tf", branch_grad, out_weight, preferred_element_type=F32).astype(BF16)
    grads_window, stats_window, along_cols = gather_grads(mixed_grad, mixed_low, logsums, seqs, 2)
    proj_grad = attention_backward(blocks, query, key, value, grads_window, ids, logsums, along_cols, stats_window, rows, own, bq, bk)

    select = (own_slots[:, None] == jnp.arange(32, dtype=jnp.int32)[None, :]).astype(BF16)
    small = jnp.concatenate([
        jnp.stack([grad_gain1, grad_shift1, grad_gain2, grad_shift2, column_sums(branch_grad), column_sums(down_grad)]),
        column_sums(up_grad).reshape(2, -1), jnp.zeros((24, 2 * width), F32)])
    up_sum, down_sum, out_sum, qkv_sum, input_grad, small = tail(
        grad_up_weight.astype(BF16), grad_down_weight.astype(BF16), grad_out_weight.astype(BF16), proj_grad, source,
        weight, grad_input1, select, small.reshape(4, 8, 2 * width), dps, seqs)
    small = small.reshape(32, 2 * width)
    input_grad = input_grad[None]
    piece = small.shape[1] // seqs
    vectors = lax.dynamic_slice_in_dim(small[:6], s * piece, piece, 1)
    memory_grad = small[9:29]
    return (
        output, input_grad, memory_grad,
        qkv_sum.transpose(1, 0, 2), small[8, :width], small[8, width:],
        out_sum, vectors[4], vectors[0], vectors[1],
        up_sum, small[6:8].reshape(-1), down_sum, vectors[5], vectors[2], vectors[3],
    )


def solution(mesh):
    in_specs = (
        P("dp", "seq", None), P("dp", None), P(), P(None, None, "tensor"), P("tensor"), P("tensor"), P(None, "tensor"), P(), P(), P(),
        P(None, "tensor"), P("tensor"), P(None, "tensor"), P(), P(), P(), P("dp", "seq", None),
    )
    out_specs = (
        P("dp", "seq", None), P("dp", "seq", None), P(), P("seq", None, "tensor"), P("tensor"), P("tensor"), P("seq", "tensor"), P("seq"), P("seq"), P("seq"),
        P("seq", "tensor"), P("tensor"), P("seq", "tensor"), P("seq"), P("seq"), P("seq"),
    )
    step = functools.partial(on_device, mesh.shape["dp"], mesh.shape["seq"])
    return jax.shard_map(step, mesh=mesh, in_specs=in_specs, out_specs=out_specs, check_vma=False)
```

```python
import functools

import jax
import jax.numpy as jnp
from jax import lax
from jax.experimental import pallas as pl
from jax.experimental.pallas import tpu as pltpu
from jax.sharding import PartitionSpec as P

HEAD_DIM = 64
READ_ROWS = 10
REACH = 3
NORM_EPS = 1e-05
F32, BF16 = jnp.float32, jnp.bfloat16
NT = (((1,), (1,)), ((), ()))
NN = (((1,), (0,)), ((), ()))
NEG = -1e30
FLOOR = -1e29
VMEM = pl.BlockSpec(memory_space=pltpu.VMEM)
SMEM = pl.BlockSpec(memory_space=pltpu.SMEM)


def remote(source, target, send_sem, recv_sem, **where):
    return pltpu.make_async_remote_copy(
        source, target, send_sem, recv_sem, device_id=where, device_id_type=pl.DeviceIdType.MESH
    )


def greet(partners):
    barrier = pltpu.get_barrier_semaphore()
    total = 0
    for present, where in partners:
        total = total + present.astype(jnp.int32)

        @pl.when(present)
        def _():
            pl.semaphore_signal(barrier, inc=1, device_id=where, device_id_type=pl.DeviceIdType.MESH)

    pl.semaphore_wait(barrier, total)


def dot(a, b, dims=NN):
    return lax.dot_general(a, b, dims, preferred_element_type=F32)

def low_half(shape):
    return lax.broadcasted_iota(jnp.int32, shape, len(shape) - 1) < 64

def id_columns(ids_ref, start, count):
    row = jnp.broadcast_to(ids_ref[0:1, pl.ds(start, count)], (128, count))
    return jnp.transpose(row)

def wide(x, count):
    return jnp.concatenate([x] * (count // 128), axis=1)

def split_heads(source_ref, rows, target_ref, pairs, keep):
    for pair in range(pairs):
        block = source_ref[rows, pair * 128:pair * 128 + 128]
        target_ref[2 * pair] = jnp.where(keep, block, jnp.zeros_like(block))
        target_ref[2 * pair + 1] = jnp.where(keep, jnp.zeros_like(block), block)

def sweep(rng_ref, b, body):
    first, full_first, full_last, last = (rng_ref[4 * b + i] for i in range(4))
    lax.fori_loop(full_first, full_last, lambda j, c: body(j, False, c), 0)

    def edge(i, c):
        j = first + i
        return body(jnp.where(j < full_first, j, j + full_last - full_first), True, c)

    lax.fori_loop(0, last - first - (full_last - full_first), edge, 0)

def fwd_kernel(bq, bk, own, rng_ref, q_ref, k_ref, v_ref, ids_ref, o_ref, lse_ref, acc_ref, max_ref, q_heads, cols_ref):
    pairs = q_ref.shape[1] // 128
    rows = o_ref.shape[0]
    low_q, low_k = low_half((bq, 128)), low_half((bk, 128))

    def block(qb, carry):
        mine = pl.ds(pl.multiple_of(qb * bq, bq), bq)
        cols_ref[...] = id_columns(ids_ref, pl.multiple_of(own + qb * bq, bq), bq)
        split_heads(q_ref, pl.ds(pl.multiple_of(own + qb * bq, bq), bq), q_heads, pairs, low_q)
        acc_ref[...] = jnp.zeros_like(acc_ref)
        max_ref[...] = jnp.full_like(max_ref, FLOOR)

        def step(j, masked, carry):
            there = pl.ds(pl.multiple_of(j * bk, bk), bk)
            def pair_step(pair, carry):
                lanes = pl.ds(pair * 128, 128)
                key = k_ref[there, lanes]
                value = v_ref[there, lanes]
                for odd in range(2):
                    head = 2 * pair + odd
                    scores = dot(q_heads[head], key, NT)
                    if masked:
                        scores = jnp.where(wide(cols_ref[...], bk) == ids_ref[0:1, there], scores, NEG)
                    old = max_ref[head]
                    new = jnp.maximum(old, jnp.max(scores, axis=1, keepdims=True))
                    probs = jnp.exp(scores - wide(new, bk)).astype(BF16)
                    ones = jnp.where(low_k if odd == 0 else ~low_k, value, jnp.ones_like(value))
                    acc_ref[head] = acc_ref[head] * jnp.exp(old - new) + dot(probs, ones)
                    max_ref[head] = new
                return carry
            for pair in range(pairs):
                pair_step(pair, carry)
            return carry

        sweep(rng_ref, qb, step)
        stats = jnp.zeros((bq, 128), F32)
        lane = lax.broadcasted_iota(jnp.int32, (bq, 128), 1)
        for pair in range(pairs):
            even, odd = acc_ref[2 * pair], acc_ref[2 * pair + 1]
            total_even, total_odd = even[:, 64:65], odd[:, 0:1]
            mixed = jnp.where(low_q, even / total_even, odd / total_odd)
            o_ref[mine, pair * 128:pair * 128 + 128] = mixed.astype(BF16)
            stats = jnp.where(lane == 2 * pair, max_ref[2 * pair] + jnp.log(total_even), stats)
            stats = jnp.where(lane == 2 * pair + 1, max_ref[2 * pair + 1] + jnp.log(total_odd), stats)
        lse_ref[mine, :] = stats
        return carry

    lax.fori_loop(0, rows // bq, block, 0)

def attention_forward(rng, query, key, value, ids, rows, own, bq=256, bk=256):
    width = query.shape[1]
    heads = width // 64
    return pl.pallas_call(
        functools.partial(fwd_kernel, bq, bk, own),
        out_shape=(jax.ShapeDtypeStruct((rows, width), BF16), jax.ShapeDtypeStruct((rows, 128), F32)),
        in_specs=[pl.BlockSpec(memory_space=pltpu.SMEM)] + [pl.BlockSpec(memory_space=pltpu.VMEM)] * 4,
        out_specs=(pl.BlockSpec(memory_space=pltpu.VMEM),) * 2,
        scratch_shapes=[pltpu.VMEM((heads, bq, 128), F32), pltpu.VMEM((heads, bq, 128), F32), pltpu.VMEM((heads, bq, 128), BF16), pltpu.VMEM((bq, 128), F32)],
        compiler_params=pltpu.CompilerParams(vmem_limit_bytes=24 << 20),
        name="attention_forward",
    )(rng, query, key, value, ids)

def bwd_kernel(bq, bk, own, rng_ref, q_ref, k_ref, v_ref, g_ref, ids_ref, lse_ref, along_ref, rows_ref, out_ref, dq_acc, dk_acc, dv_acc, q_heads, k_heads, v_heads, g_heads, lse_cols, along_cols, cols_ref):
    rows, width = out_ref.shape[0], q_ref.shape[1]
    pairs = width // 128
    heads = 2 * pairs
    low_q = low_half((bq, 128))

    def block(b, carry):
        start = pl.multiple_of(b * bq, bq)
        mine = pl.ds(start, bq)
        here = pl.ds(pl.multiple_of(own + start, bq), bq)
        cols_ref[...] = id_columns(ids_ref, pl.multiple_of(own + start, bq), bq)
        for source, target in ((q_ref, q_heads), (k_ref, k_heads), (v_ref, v_heads), (g_ref, g_heads)):
            split_heads(source, here, target, pairs, low_q)
        for head in range(heads):
            lse_cols[head] = jnp.broadcast_to(lse_ref[mine, head:head + 1], (bq, 128))
            along_cols[head] = jnp.broadcast_to(along_ref[mine, head:head + 1], (bq, 128))
        for acc in (dq_acc, dk_acc, dv_acc):
            acc[...] = jnp.zeros_like(acc)

        def step(j, masked, carry):
            there = pl.ds(pl.multiple_of(j * bk, bk), bk)
            def pair_step(pair, carry):
                lanes = pl.ds(pair * 128, 128)
                q_far, k_far, v_far, g_far = (r[there, lanes] for r in (q_ref, k_ref, v_ref, g_ref))
                def hide(x):
                    return jnp.where(wide(cols_ref[...], bk) == ids_ref[0:1, there], x, 0.0) if masked else x
                for odd in range(2):
                    head = 2 * pair + odd
                    scores = dot(q_heads[head], k_far, NT)
                    probs = hide(jnp.exp(scores - wide(lse_cols[head], bk)))
                    slope = dot(g_heads[head], v_far, NT)
                    grad = (probs * (slope - wide(along_cols[head], bk))).astype(BF16)
                    dq_acc[head] += dot(grad, k_far)
                    scores = dot(k_heads[head], q_far, NT)
                    probs = hide(jnp.exp(scores - rows_ref[pl.ds(head, 1), there]))
                    slope = dot(v_heads[head], g_far, NT)
                    grad = (probs * (slope - rows_ref[pl.ds(8 + head, 1), there])).astype(BF16)
                    dv_acc[head] += dot(probs.astype(BF16), g_far)
                    dk_acc[head] += dot(grad, q_far)
                return carry
            for pair in range(pairs):
                pair_step(pair, carry)
            return carry

        sweep(rng_ref, b, step)
        for which, (acc, factor) in enumerate(((dq_acc, 0.125), (dk_acc, 1.0), (dv_acc, 1.0))):
            for pair in range(pairs):
                both = jnp.where(low_q, acc[2 * pair], acc[2 * pair + 1]) * factor
                out_ref[mine, which * width + pair * 128:which * width + pair * 128 + 128] = both.astype(BF16)
        return carry

    lax.fori_loop(0, rows // bq, block, 0)

def attention_backward(rng, query, key, value, grads, ids, lse, along, stat_rows, rows, own, bq=256, bk=256):
    width = query.shape[1]
    heads = width // 64
    return pl.pallas_call(
        functools.partial(bwd_kernel, bq, bk, own),
        out_shape=jax.ShapeDtypeStruct((rows, 3 * width), BF16),
        in_specs=[pl.BlockSpec(memory_space=pltpu.SMEM)] + [pl.BlockSpec(memory_space=pltpu.VMEM)] * 8,
        out_specs=pl.BlockSpec(memory_space=pltpu.VMEM),
        scratch_shapes=[pltpu.VMEM((heads, bq, 128), F32)] * 3 + [pltpu.VMEM((heads, bq, 128), BF16)] * 4 + [pltpu.VMEM((heads, bq, 128), F32)] * 2 + [pltpu.VMEM((bq, 128), F32)],
        compiler_params=pltpu.CompilerParams(vmem_limit_bytes=40 << 20),
        name="attention_backward",
    )(rng, query, key, value, grads, ids, lse, along, stat_rows)

class Halo:
    def __init__(self, count, pieces, send_sem, recv_sem):
        self.count, self.pieces, self.send_sem, self.recv_sem = count, pieces, send_sem, recv_sem
        s = self.s = lax.axis_index("seq")
        self.core = lax.rem(s, 2)
        self.sibling = s + 1 - 2 * self.core
        self.left, self.right = s >= 2, s < count - 2

    def greet(self):
        s, count = self.s, self.count
        greet([(s >= k, {"seq": s - k}) for k in (1, 2)] + [(s < count - k, {"seq": s + k}) for k in (1, 2)])

    def own(self, part, kind, slot, target):
        source, window = self.pieces[part]
        return remote(source, window(slot), self.send_sem.at[kind, part], self.recv_sem.at[slot, part], seq=target)

    def moved(self, part, kind, held, slot, target):
        window = self.pieces[part][1]
        return remote(window(held), window(slot), self.send_sem.at[kind, part], self.recv_sem.at[slot, part], seq=target)

    def first_copies(self, part):
        s, core = self.s, self.core
        return (
            (self.right, self.own(part, 0, 1, s + 2)),
            (self.left, self.own(part, 1, 5, s - 2)),
            (core == 0, self.own(part, 2, 2, self.sibling)),
            (core == 1, self.own(part, 2, 4, self.sibling)),
        )

    def from_left(self, part):
        s, core, left, right = self.s, self.core, self.left, self.right
        return (
            (jnp.logical_and(left, jnp.logical_and(core == 1, right)), self.moved(part, 3, 1, 0, s + 1)),
            (jnp.logical_and(left, core == 0), self.moved(part, 4, 1, 0, self.sibling)),
            (jnp.logical_and(left, core == 1), self.moved(part, 4, 1, 2, self.sibling)),
        )

    def from_right(self, part):
        s, core, left, right = self.s, self.core, self.left, self.right
        return (
            (jnp.logical_and(right, jnp.logical_and(core == 0, left)), self.moved(part, 5, 5, 6, s - 1)),
            (jnp.logical_and(right, core == 0), self.moved(part, 6, 5, 4, self.sibling)),
            (jnp.logical_and(right, core == 1), self.moved(part, 6, 5, 6, self.sibling)),
        )

    def each(self, copies, act):
        for present, copy in copies:
            pl.when(present)(functools.partial(act, copy))

    def send(self, part):
        self.each(self.first_copies(part), lambda copy: copy.start())

    def arrived(self, slot, part):
        self.own(part, 0, slot, self.s).wait_recv()

    def relay(self, part):
        pl.when(self.left)(functools.partial(self.arrived, 1, part))
        self.each(self.from_left(part), lambda copy: copy.start())
        pl.when(self.right)(functools.partial(self.arrived, 5, part))
        self.each(self.from_right(part), lambda copy: copy.start())

    def present(self, slot):
        block = self.s + slot - REACH
        return jnp.logical_and(block >= 0, block < self.count)

    def receive(self, slot):
        for part in range(len(self.pieces)):
            pl.when(self.present(slot))(functools.partial(self.arrived, slot, part))

    def finish(self):
        for part in range(len(self.pieces)):
            self.each(self.first_copies(part) + self.from_left(part) + self.from_right(part), lambda copy: copy.wait_send())


def project_kernel(count, parts, own_ref, slots_ref, memory_ref, weight_ref, query_bias_ref, value_bias_ref,
                   q_ref, k_ref, v_ref, source_ref, window_ref, send_sem, recv_sem):
    block = own_ref.shape[0]
    rows = block // parts
    tile = 256
    tiles = block // tile

    def piece(part):
        return own_ref.at[pl.ds(part * rows, rows)], lambda slot: window_ref.at[pl.ds(slot * block + part * rows, rows)]

    halo = Halo(count, [piece(part) for part in range(parts)], send_sem, recv_sem)
    halo.greet()
    for part in range(parts):
        halo.send(part)

    def project(load, start, keep):
        hot = (lax.broadcasted_iota(jnp.int32, (32, tile), 0) == slots_ref[0:1, pl.ds(start, tile)]).astype(F32).astype(BF16)
        tn = (((0,), (0,)), ((), ()))
        chosen = dot(hot, memory_ref[...], tn)
        inside = wide(dot(hot, jnp.ones((32, 128), BF16), tn), chosen.shape[1])
        source = jnp.where(inside > 0.5, chosen, load().astype(F32)).astype(BF16)
        keep(source)
        out = pl.ds(start, tile)
        q_ref[out, :] = (dot(source, weight_ref[0]) + query_bias_ref[...]).astype(BF16) * 0.125
        k_ref[out, :] = dot(source, weight_ref[1]).astype(BF16)
        v_ref[out, :] = (dot(source, weight_ref[2]) + value_bias_ref[...]).astype(BF16)

    def own_tile(i, carry):
        at = pl.ds(pl.multiple_of(i * tile, tile), tile)

        def keep(source):
            source_ref[at, :] = source

        project(lambda: own_ref[at, :], pl.multiple_of(REACH * block + i * tile, tile), keep)
        return carry

    lax.fori_loop(0, tiles, own_tile, 0)
    for part in range(parts):
        halo.relay(part)

    def two_blocks(low, high):
        def step(i, carry):
            slot = low + (high - low) * (i // tiles)

            @pl.when(halo.present(slot))
            def _():
                start = pl.multiple_of(slot * block + lax.rem(i, tiles) * tile, tile)
                project(lambda: window_ref[pl.ds(start, tile), :], start, lambda source: None)

            return carry

        lax.fori_loop(0, 2 * tiles, step, 0)

    two_blocks(1, 5)
    for slots in ((2, 4), (0, 6)):
        for slot in slots:
            halo.receive(slot)
        two_blocks(*slots)
    halo.finish()


def project_window(own, slots, memory, weight, query_bias, value_bias, count, collective_id, parts=2):
    rows, dim = own.shape
    width = weight.shape[2]
    total = (2 * REACH + 1) * rows
    wide_out = jax.ShapeDtypeStruct((total, width), BF16)
    return pl.pallas_call(
        functools.partial(project_kernel, count, parts),
        out_shape=(wide_out, wide_out, wide_out, jax.ShapeDtypeStruct((rows, dim), BF16)),
        in_specs=[VMEM] * 6,
        out_specs=(VMEM,) * 4,
        scratch_shapes=[
            pltpu.VMEM((total, dim), BF16),
            pltpu.SemaphoreType.DMA((7, parts)),
            pltpu.SemaphoreType.DMA((7, parts)),
        ],
        compiler_params=pltpu.CompilerParams(collective_id=collective_id, has_side_effects=True, vmem_limit_bytes=40 << 20),
        name="project_window",
    )(own, slots, memory, weight, query_bias, value_bias)


def grads_kernel(count, parts, grad_ref, mixed_ref, lse_ref, window_ref, stats_ref, along_ref, own_stats, send_sem, recv_sem):
    block, width = grad_ref.shape
    rows = block // parts

    def piece(part):
        return grad_ref.at[pl.ds(part * rows, rows)], lambda slot: window_ref.at[pl.ds(slot * block + part * rows, rows)]

    stats_piece = own_stats, lambda slot: stats_ref.at[:, pl.ds(slot * block, block)]
    halo = Halo(count, [piece(part) for part in range(parts)] + [stats_piece], send_sem, recv_sem)
    halo.greet()
    for part in range(parts):
        halo.send(part)
    window_ref[REACH * block:(REACH + 1) * block, :] = grad_ref[...]
    lane = lax.broadcasted_iota(jnp.int32, (block, 128), 1)
    along = jnp.zeros((block, 128), F32)
    for pair in range(width // 128):
        lanes = slice(pair * 128, pair * 128 + 128)
        product = grad_ref[:, lanes].astype(F32) * mixed_ref[:, lanes].astype(F32)
        even = jnp.sum(jnp.where(lane < 64, product, 0.0), axis=1, keepdims=True)
        odd = jnp.sum(jnp.where(lane < 64, 0.0, product), axis=1, keepdims=True)
        along = jnp.where(lane == 2 * pair, even, jnp.where(lane == 2 * pair + 1, odd, along))
    along_ref[...] = along
    own_stats[0:8, :] = jnp.transpose(lse_ref[...])[0:8, :]
    own_stats[8:16, :] = jnp.transpose(along)[0:8, :]
    stats_ref[:, REACH * block:(REACH + 1) * block] = own_stats[...]
    halo.send(parts)
    for part in range(parts + 1):
        halo.relay(part)
    for slot in (0, 2, 4, 6):
        halo.receive(slot)
    halo.finish()


def gather_grads(grad, mixed, lse, count, collective_id, parts=2):
    rows, width = grad.shape
    total = (2 * REACH + 1) * rows
    return pl.pallas_call(
        functools.partial(grads_kernel, count, parts),
        out_shape=(
            jax.ShapeDtypeStruct((total, width), BF16),
            jax.ShapeDtypeStruct((16, total), F32),
            jax.ShapeDtypeStruct((rows, 128), F32),
        ),
        in_specs=[VMEM] * 3,
        out_specs=(VMEM,) * 3,
        scratch_shapes=[
            pltpu.VMEM((16, rows), F32),
            pltpu.SemaphoreType.DMA((7, parts + 1)),
            pltpu.SemaphoreType.DMA((7, parts + 1)),
        ],
        compiler_params=pltpu.CompilerParams(collective_id=collective_id, has_side_effects=True, vmem_limit_bytes=24 << 20),
        name="gather_grads",
    )(grad, mixed, lse)


def split_dot(left, right, dims):
    high = right.astype(BF16)
    low = (right - high.astype(F32)).astype(BF16)
    return dot(left, high, dims) + dot(left, low, dims)


def tail_kernel(dps, seqs, width, *refs):
    (early_refs, (out_grad_ref, proj_ref, source_ref, weight_ref, input1_ref, select_ref, small_ref),
     (up_out, down_out, out_out, qkv_out, input_out, small_out),
     (mix, y_send, y_recv, a_recv, parts, b_recv, small_in, small_recv, small_mine, small_dp),
     (mine, c_recv, last, d_recv), (y_sems, a_sems, b_sems, c_sems, d_sems, s_sems)) = (
        refs[:dps], refs[dps:dps + 7], refs[dps + 7:dps + 13], refs[dps + 13:dps + 23], refs[dps + 23:dps + 27], refs[dps + 27:])
    zs = seqs // 2
    bits = zs.bit_length() - 1
    t, d, s = lax.axis_index("tensor"), lax.axis_index("dp"), lax.axis_index("seq")
    z, core = s // 2, lax.rem(s, 2)
    sibling = s + 1 - 2 * core
    late, early = a_recv.shape[0], mine.shape[0] - a_recv.shape[0]
    chunk = a_recv.shape[3]
    shares = -(-chunk // width)
    owners = small_ref.shape[0]
    block, hidden = up_out.shape
    share_width = early * width
    rows, columns = proj_ref.shape
    third = columns // 3
    steps = y_send.shape[0]
    span = rows // steps
    true = s >= 0
    partners = [(true, {"seq": lax.rem(s + k, seqs)}) for k in range(1, seqs)]
    partners += [(true, {"dp": lax.rem(d + k, dps)}) for k in range(1, dps)]
    partners += [(true, {"tensor": 1 - t})]
    greet(partners)

    def active(c):
        return true if c < early else d < shares

    def a_copy(c, j):
        start = pl.multiple_of((2 * j + 1 - core) * block, 16)
        at = (c - early) * chunk
        i = c - early
        return remote(mix.at[pl.ds(start, block), pl.ds(at, chunk)], a_recv.at[i, j], a_sems.at[0, i, j], a_sems.at[1, i, j], seq=sibling)

    def b_copy(c, k):
        other = lax.rem(d + k, dps)
        i = c - early
        return other, remote(parts.at[i, other], b_recv.at[i, k], b_sems.at[0, i, k], b_sems.at[1, i, k], dp=other)

    def first_slot(b):
        return sum(zs // (2 << e) for e in range(b))

    def c_copies(c, b):
        size = 2 << b
        high = lax.rem(z // (1 << b), 2)
        partner = z + (1 << b) - (size * high)
        low = lax.rem(partner, size)
        return [
            remote(mine.at[c, i * size + low], c_recv.at[c, first_slot(b) + i], c_sems.at[0, c, first_slot(b) + i], c_sems.at[1, c, first_slot(b) + i], seq=2 * partner + core)
            for i in range(zs // size)
        ]

    def d_copy(c, k):
        return remote(last.at[c], d_recv.at[c, k], d_sems.at[0, c, k], d_sems.at[1, c, k], dp=lax.rem(d + k, dps))

    def start_a(c):
        for j in range(zs):
            a_copy(c, j).start()

    def start_early(c):
        lanes = slice(c * width, c * width + width)
        for j in range(zs):
            total = early_refs[0][j, :, lanes].astype(F32)
            for k in range(1, dps):
                total = total + early_refs[k][j, :, lanes].astype(F32)
            mine[c, j] = total.astype(BF16)
        for copy in c_copies(c, 0):
            copy.start()

    def end_a(c):
        i = c - early
        for j in range(zs):
            a_copy(c, j).wait()
            start = pl.multiple_of((2 * j + core) * block, 16)
            for p in range(shares):
                real = min(width, chunk - p * width)
                lanes = pl.ds(i * chunk + p * width, real)
                total = mix[pl.ds(start, block), lanes].astype(F32) + a_recv[i, j, :, p * width:p * width + real].astype(F32)
                parts[i, p, j, :, 0:real] = total.astype(BF16)
                if real < width:
                    parts[i, p, j, :, real:width] = jnp.zeros((block, width - real), BF16)
        for k in range(1, dps):
            other, copy = b_copy(c, k)
            pl.when(other < shares)(copy.start)

    def end_b(c):
        i = c - early
        for k in range(1, dps):
            other, copy = b_copy(c, k)
            pl.when(other < shares)(copy.wait_send)

        @pl.when(d < shares)
        def _():
            for k in range(1, dps):
                b_copy(c, k)[1].wait_recv()
            for j in range(zs):
                total = parts[i, d, j].astype(F32)
                for k in range(1, dps):
                    total = total + b_recv[i, k, j].astype(F32)
                mine[c, j] = total.astype(BF16)
            for copy in c_copies(c, 0):
                copy.start()

    def end_c(c, b):
        size = 2 << b
        kept = lax.rem(z, size)

        @pl.when(active(c))
        def _():
            for i, copy in enumerate(c_copies(c, b)):
                copy.wait()
                held = mine[c, i * size + kept].astype(F32) + c_recv[c, first_slot(b) + i].astype(F32)
                if b < bits - 1:
                    mine[c, i * size + kept] = held.astype(BF16)
                else:
                    last[c] = held.astype(BF16)
            if b < bits - 1:
                for copy in c_copies(c, b + 1):
                    copy.start()
            else:
                for k in range(1, dps):
                    d_copy(c, k).start()

    def put(c, share, value):
        count = dps if c < early else shares
        for p in range(count):

            @pl.when(share == p)
            def _():
                if c < early:
                    which, column = divmod(p * share_width + c * width, hidden)
                    (up_out, down_out)[which][:, column:column + width] = value.astype(F32)
                    return
                first = (c - early) * chunk + p * width
                for lane in range(0, min(width, chunk - p * width), 128):
                    which, column = divmod(first + lane, third)
                    part = value[:, lane:lane + 128].astype(F32)
                    if which == 0:
                        out_out[:, column:column + 128] = part
                    else:
                        qkv_out[which - 1, :, column:column + 128] = part

    def end_d(c):
        @pl.when(active(c))
        def _():
            put(c, d, last[c])
            for k in range(1, dps):
                d_copy(c, k).wait_send()

        for k in range(1, dps):
            share = lax.rem(d + dps - k, dps)

            @pl.when(true if c < early else share < shares)
            def _():
                d_copy(c, k).wait_recv()
                put(c, share, d_recv[c, k])

    def y_copy(i):
        return remote(y_send.at[i], y_recv.at[i], y_sems.at[0, i], y_sems.at[1, i], tensor=1 - t)

    for c in range(early):
        start_early(c)
    out_width = out_grad_ref.shape[1]
    mix[:, 0:out_width] = out_grad_ref[...]
    for i in range(3):
        part = lax.dot_general(source_ref[...], proj_ref[:, i * third:(i + 1) * third], (((0,), (0,)), ((), ())), preferred_element_type=F32)
        mix[:, out_width + i * third:out_width + (i + 1) * third] = part.astype(BF16)
    for c in range(early, early + late):
        start_a(c)
    for i in range(steps):
        at = slice(i * span, (i + 1) * span)
        y_send[i] = sum(dot(proj_ref[at, j * third:(j + 1) * third], weight_ref[j], NT) for j in range(3)).astype(BF16)
        y_copy(i).start()
    for i in range(owners):
        small_in[i] = small_ref[i]
    small_in[1, 0:1, 0:third] = jnp.sum(proj_ref[:, 0:third].astype(F32), axis=0, keepdims=True)
    small_in[1, 0:1, third:2 * third] = jnp.sum(proj_ref[:, 2 * third:3 * third].astype(F32), axis=0, keepdims=True)

    def end_y():
        memory = jnp.zeros((32, input_out.shape[1]), F32)
        for i in range(steps):
            y_copy(i).wait()
            at = slice(i * span, (i + 1) * span)
            total = input1_ref[at, :] + (y_send[i].astype(F32) + y_recv[i].astype(F32))
            select = select_ref[at, :]
            memory = memory + split_dot(select, total, (((0,), (0,)), ((), ())))
            inside = dot(select, jnp.ones((32, total.shape[1]), BF16))
            input_out[at, :] = jnp.where(inside > 0.5, 0.0, total).astype(BF16)
        small_in[1, 1:8, :] = memory[0:7]
        small_in[2] = memory[7:15]
        small_in[3, 0:5, :] = memory[15:20]
        for hop in range(1, seqs):
            owner = lax.rem(s + hop, seqs)
            pl.when(owner < owners)(to_owner(hop, owner).start)

    def to_owner(hop, owner):
        return remote(small_in.at[owner], small_recv.at[hop], s_sems.at[0, 0, hop], s_sems.at[1, 0, hop], seq=owner)

    def across(k):
        return remote(small_mine, small_dp.at[k], s_sems.at[0, 1, k], s_sems.at[1, 1, k], dp=lax.rem(d + k, dps))

    def back(hop, owner, target):
        return remote(small_out.at[owner], small_out.at[owner], s_sems.at[0, 2, hop], s_sems.at[1, 2, hop], seq=target)

    def small_one():
        @pl.when(s < owners)
        def _():
            total = small_in[s]
            for hop in range(1, seqs):
                to_owner(hop, s).wait_recv()
                total = total + small_recv[hop]
            small_mine[...] = total
            for k in range(1, dps):
                across(k).start()

    def small_two():
        @pl.when(s < owners)
        def _():
            small_dp[0] = small_mine[...]
            for k in range(1, dps):
                across(k).wait()
            ordered = jnp.zeros(small_mine.shape, F32)
            for index in range(dps):
                ordered = ordered + small_dp[lax.rem(d + dps - index, dps)]
            small_out[s] = ordered
            for hop in range(1, seqs):
                back(hop, s, lax.rem(s + hop, seqs)).start()

    def small_three():
        for hop in range(1, seqs):
            owner = lax.rem(s + hop, seqs)
            pl.when(owner < owners)(to_owner(hop, owner).wait_send)
        for hop in range(1, seqs):
            pl.when(lax.rem(s + seqs - hop, seqs) < owners)(back(hop, 0, s).wait_recv)
            pl.when(s < owners)(back(hop, 0, s).wait_send)

    zed = [functools.partial(end_c, b=b) for b in range(bits)]
    lates = list(range(early, early + late))
    for c in lates:
        end_a(c)
    for c in range(early):
        zed[0](c)
    for c in lates:
        end_b(c)
    end_y()
    for b in range(1, bits):
        for c in range(early):
            zed[b](c)
        for c in lates:
            zed[b - 1](c)
        if b == 1:
            small_one()
    for c in range(early):
        end_d(c)
    small_two()
    for c in lates:
        zed[bits - 1](c)
    for c in lates:
        end_d(c)
    small_three()


def tail(early, out, proj, source, weight, input1, select, small, dps, seqs):
    zs = seqs // 2
    dim = source.shape[1]
    hidden = early[0].shape[2] * dps // 2
    rows = proj.shape[0]
    block = dim // seqs
    mixed = out.shape[1] + proj.shape[1]
    late = 2
    chunk = mixed // late
    width = -(-chunk // (128 * dps)) * 128
    width = early[0].shape[2] if early[0].shape[2] % width else width
    chunks = early[0].shape[2] // width + late
    steps = 4
    dma = pltpu.SemaphoreType.DMA
    return pl.pallas_call(
        functools.partial(tail_kernel, dps, seqs, width),
        out_shape=(
            jax.ShapeDtypeStruct((block, hidden), F32),
            jax.ShapeDtypeStruct((block, hidden), F32),
            jax.ShapeDtypeStruct((block, out.shape[1]), F32),
            jax.ShapeDtypeStruct((3, block, out.shape[1]), F32),
            jax.ShapeDtypeStruct((rows, dim), BF16),
            jax.ShapeDtypeStruct(small.shape, F32),
        ),
        in_specs=[VMEM] * (dps + 7),
        out_specs=(VMEM,) * 6,
        scratch_shapes=[
            pltpu.VMEM((dim, mixed), BF16),
            pltpu.VMEM((steps, rows // steps, dim), BF16),
            pltpu.VMEM((steps, rows // steps, dim), BF16),
            pltpu.VMEM((late, zs, block, chunk), BF16),
            pltpu.VMEM((late, dps, zs, block, width), BF16),
            pltpu.VMEM((late, dps, zs, block, width), BF16),
            pltpu.VMEM(small.shape, F32),
            pltpu.VMEM((seqs,) + small.shape[1:], F32),
            pltpu.VMEM(small.shape[1:], F32),
            pltpu.VMEM((dps,) + small.shape[1:], F32),
            pltpu.VMEM((chunks, zs, block, width), BF16),
            pltpu.VMEM((chunks, zs - 1, block, width), BF16),
            pltpu.VMEM((chunks, block, width), BF16),
            pltpu.VMEM((chunks, dps, block, width), BF16),
            dma((2, steps)),
            dma((2, late, zs)),
            dma((2, late, dps)),
            dma((2, chunks, zs)),
            dma((2, chunks, dps)),
            dma((2, 3, max(seqs, dps))),
        ],
        compiler_params=pltpu.CompilerParams(collective_id=7, has_side_effects=True, vmem_limit_bytes=48 << 20),
        name="tail",
    )(*early, out, proj, source, weight, input1, select, small)


def pair_and_dp_sums(up, down, dps, seqs):
    s, d = lax.axis_index("seq"), lax.axis_index("dp")
    core = lax.rem(s, 2)
    zs = seqs // 2
    pair = [(i, i + 1 - 2 * (i % 2)) for i in range(seqs)]
    sums = []
    for grad in (up, down):
        split = grad.astype(BF16).reshape(zs, 2, -1, grad.shape[1])
        theirs = lax.ppermute(lax.dynamic_index_in_dim(split, 1 - core, 1, False), "seq", pair)
        sums.append((lax.dynamic_index_in_dim(split, core, 1, False).astype(F32) + theirs.astype(F32)).astype(BF16))
    pieces = [piece for total in sums for piece in jnp.split(total, max(dps // 2, 1), axis=2)]

    def share(index):
        return functools.reduce(lambda kept, k: jnp.where(index == k, pieces[k], kept), range(1, dps), pieces[0])

    result = [share(d)]
    for k in range(1, dps):
        result.append(lax.ppermute(share(lax.rem(d + k, dps)), "dp", [(i, (i + k) % dps) for i in range(dps)]))
    return result


def memory_slots(id_row):
    count = id_row.shape[0]
    edge = jnp.full((READ_ROWS,), -1, jnp.int32)
    padded = jnp.concatenate([edge, id_row, edge])
    before = sum((padded[READ_ROWS - k:READ_ROWS - k + count] == id_row).astype(jnp.int32) for k in range(1, READ_ROWS + 1))
    behind = sum((padded[READ_ROWS + k:READ_ROWS + k + count] == id_row).astype(jnp.int32) for k in range(1, READ_ROWS + 1))
    return jnp.where(before < READ_ROWS, before, jnp.where(behind < READ_ROWS, 2 * READ_ROWS - 1 - behind, -1))


def document_blocks(id_row, own_ids, window_start, bq, bk):
    table = []
    for b in range(own_ids.shape[0] // bq):
        low, high = own_ids[b * bq], own_ids[b * bq + bq - 1]
        start = jnp.sum((id_row < low).astype(jnp.int32)) - window_start
        end = jnp.sum((id_row <= high).astype(jnp.int32)) - window_start
        first, last = start // bk, (end + bk - 1) // bk
        full_first, full_last = (start + bk - 1) // bk, end // bk
        whole = jnp.logical_and(low == high, full_first < full_last)
        table += [first, jnp.where(whole, full_first, first), jnp.where(whole, full_last, first), last]
    return jnp.stack(table).astype(jnp.int32)


def normalize(hidden, gain, shift):
    centre = jnp.mean(hidden, axis=-1, keepdims=True)
    centred = hidden - centre
    spread = jnp.mean(centred * centred, axis=-1, keepdims=True)
    return centred * lax.rsqrt(spread + NORM_EPS) * gain + shift


def gelu_exact(values):
    return jax.nn.gelu(values, approximate=False)


def column_sums(matrix):
    return jnp.sum(matrix.astype(F32), axis=0)


def on_device(dps, seqs, tokens, doc_ids, memory, qkv_weight, query_bias, value_bias, out_weight, out_bias, norm1_gain, norm1_bias, up_weight, up_bias, down_weight, down_bias, norm2_gain, norm2_bias, out_grad):
    rows = tokens.shape[1]
    width = qkv_weight.shape[2]
    heads = width // HEAD_DIM
    bq, bk = rows, 256
    own = REACH * rows
    pieces = 2 * REACH + 1
    s = lax.axis_index("seq")
    id_row = doc_ids[0]
    edge = jnp.full((own,), -1, jnp.int32)
    window_start = s * rows - own
    slots = memory_slots(id_row)
    window_slots = lax.dynamic_slice_in_dim(jnp.concatenate([edge, slots, edge]), s * rows, pieces * rows, 0)
    window_ids = lax.dynamic_slice_in_dim(jnp.concatenate([edge, id_row, edge]), s * rows, pieces * rows, 0)
    own_ids = window_ids[own:own + rows]
    blocks = document_blocks(id_row, own_ids, window_start, bq, bk)
    ids = jnp.broadcast_to(window_ids.astype(F32)[None], (8, pieces * rows))

    weight = qkv_weight.transpose(1, 0, 2)
    slots_row = jnp.broadcast_to(window_slots[None], (8, pieces * rows))
    memory_pad = jnp.pad(memory, ((0, 32 - memory.shape[0]), (0, 0)))
    query, key, value, source = project_window(
        tokens[0], slots_row, memory_pad, weight, query_bias[None], value_bias[None], seqs, 1)
    own_slots = window_slots[own:own + rows]

    mixed_low, logsums = attention_forward(blocks, query, key, value, ids, rows, own, bq, bk)

    def both(part):
        low = part.astype(BF16)
        return low.astype(F32) + lax.ppermute(low, "tensor", [(0, 1), (1, 0)]).astype(F32)

    branch = both(jnp.einsum("tf,of->to", mixed_low, out_weight, preferred_element_type=F32)) + out_bias
    first_input = source.astype(F32) + branch
    first_out, first_pull = jax.vjp(normalize, first_input, norm1_gain, norm1_bias)
    first_low = first_out.astype(BF16)
    up_proj = jnp.dot(first_low, up_weight, preferred_element_type=F32) + up_bias
    act_full, gelu_pull = jax.vjp(gelu_exact, up_proj)
    act_low = act_full.astype(BF16)
    down_out = both(jnp.einsum("tf,of->to", act_low, down_weight, preferred_element_type=F32)) + down_bias
    result, second_pull = jax.vjp(normalize, first_out + down_out, norm2_gain, norm2_bias)
    output = result.astype(BF16)[None]
    grad_second, grad_gain2, grad_shift2 = second_pull(out_grad[0].astype(F32))
    down_grad = grad_second.astype(BF16)
    grad_down_weight = jnp.einsum("to,tf->of", down_grad, act_low, preferred_element_type=F32)
    act_grad = jnp.einsum("to,of->tf", down_grad, down_weight, preferred_element_type=F32)
    up_grad = gelu_pull(act_grad)[0].astype(BF16)
    grad_up_weight = jnp.einsum("td,tf->df", first_low, up_grad, preferred_element_type=F32)
    grad_first = grad_second + both(jnp.einsum("tf,df->td", up_grad, up_weight, preferred_element_type=F32))
    grad_input1, grad_gain1, grad_shift1 = first_pull(grad_first)
    branch_grad = grad_input1.astype(BF16)
    grad_out_weight = jnp.einsum("to,tf->of", branch_grad, mixed_low, preferred_element_type=F32)
    mixed_grad = jnp.einsum("to,of->tf", branch_grad, out_weight, preferred_element_type=F32).astype(BF16)
    early = pair_and_dp_sums(grad_up_weight, grad_down_weight, dps, seqs)
    grads_window, stats_window, along_cols = gather_grads(mixed_grad, mixed_low, logsums, seqs, 2)
    proj_grad = attention_backward(blocks, query, key, value, grads_window, ids, logsums, along_cols, stats_window, rows, own, bq, bk)

    select = (own_slots[:, None] == jnp.arange(32, dtype=jnp.int32)[None, :]).astype(BF16)
    small = jnp.concatenate([
        jnp.stack([grad_gain1, grad_shift1, grad_gain2, grad_shift2, column_sums(branch_grad), column_sums(down_grad)]),
        column_sums(up_grad).reshape(2, -1), jnp.zeros((24, 2 * width), F32)])
    up_sum, down_sum, out_sum, qkv_sum, input_grad, small = tail(
        early, grad_out_weight.astype(BF16), proj_grad, source,
        weight, grad_input1, select, small.reshape(4, 8, 2 * width), dps, seqs)
    small = small.reshape(32, 2 * width)
    input_grad = input_grad[None]
    piece = small.shape[1] // seqs
    vectors = lax.dynamic_slice_in_dim(small[:6], s * piece, piece, 1)
    memory_grad = small[9:29]
    return (
        output, input_grad, memory_grad,
        qkv_sum.transpose(1, 0, 2), small[8, :width], small[8, width:],
        out_sum, vectors[4], vectors[0], vectors[1],
        up_sum, small[6:8].reshape(-1), down_sum, vectors[5], vectors[2], vectors[3],
    )


def solution(mesh):
    in_specs = (
        P("dp", "seq", None), P("dp", None), P(), P(None, None, "tensor"), P("tensor"), P("tensor"), P(None, "tensor"), P(), P(), P(),
        P(None, "tensor"), P("tensor"), P(None, "tensor"), P(), P(), P(), P("dp", "seq", None),
    )
    out_specs = (
        P("dp", "seq", None), P("dp", "seq", None), P(), P("seq", None, "tensor"), P("tensor"), P("tensor"), P("seq", "tensor"), P("seq"), P("seq"), P("seq"),
        P("seq", "tensor"), P("tensor"), P("seq", "tensor"), P("seq"), P("seq"), P("seq"),
    )
    step = functools.partial(on_device, mesh.shape["dp"], mesh.shape["seq"])
    return jax.shard_map(step, mesh=mesh, in_specs=in_specs, out_specs=out_specs, check_vma=False)
```

```python
import functools

import jax
import jax.numpy as jnp
from jax import lax
from jax.experimental import pallas as pl
from jax.experimental.pallas import tpu as pltpu
from jax.sharding import PartitionSpec as P

HEAD_DIM = 64
READ_ROWS = 10
REACH = 3
NORM_EPS = 1e-05
OWNERS = 4
F32, BF16 = jnp.float32, jnp.bfloat16
NT = (((1,), (1,)), ((), ()))
NN = (((1,), (0,)), ((), ()))
NEG = -1e30
FLOOR = -1e29
VMEM = pl.BlockSpec(memory_space=pltpu.VMEM)
SMEM = pl.BlockSpec(memory_space=pltpu.SMEM)


def remote(source, target, send_sem, recv_sem, **where):
    return pltpu.make_async_remote_copy(
        source, target, send_sem, recv_sem, device_id=where, device_id_type=pl.DeviceIdType.MESH
    )


def greet(partners):
    barrier = pltpu.get_barrier_semaphore()
    total = 0
    for present, where in partners:
        total = total + present.astype(jnp.int32)

        @pl.when(present)
        def _():
            pl.semaphore_signal(barrier, inc=1, device_id=where, device_id_type=pl.DeviceIdType.MESH)

    pl.semaphore_wait(barrier, total)


def dot(a, b, dims=NN):
    return lax.dot_general(a, b, dims, preferred_element_type=F32)

def low_half(shape):
    return lax.broadcasted_iota(jnp.int32, shape, len(shape) - 1) < 64

def id_columns(ids_ref, start, count):
    row = jnp.broadcast_to(ids_ref[0:1, pl.ds(start, count)], (128, count))
    return jnp.transpose(row)

def wide(x, count):
    return jnp.concatenate([x] * (count // 128), axis=1)

def split_heads(source_ref, rows, target_ref, pairs, keep):
    for pair in range(pairs):
        block = source_ref[rows, pair * 128:pair * 128 + 128]
        target_ref[2 * pair] = jnp.where(keep, block, jnp.zeros_like(block))
        target_ref[2 * pair + 1] = jnp.where(keep, jnp.zeros_like(block), block)

def sweep(rng_ref, b, body):
    first, full_first, full_last, last = (rng_ref[4 * b + i] for i in range(4))
    lax.fori_loop(full_first, full_last, lambda j, c: body(j, False, c), 0)

    def edge(i, c):
        j = first + i
        return body(jnp.where(j < full_first, j, j + full_last - full_first), True, c)

    lax.fori_loop(0, last - first - (full_last - full_first), edge, 0)

def fwd_kernel(bq, bk, own, rng_ref, q_ref, k_ref, v_ref, ids_ref, o_ref, lse_ref, acc_ref, max_ref, q_heads, cols_ref):
    pairs = q_ref.shape[1] // 128
    rows = o_ref.shape[0]
    low_q, low_k = low_half((bq, 128)), low_half((bk, 128))

    def block(qb, carry):
        mine = pl.ds(pl.multiple_of(qb * bq, bq), bq)
        cols_ref[...] = id_columns(ids_ref, pl.multiple_of(own + qb * bq, bq), bq)
        split_heads(q_ref, pl.ds(pl.multiple_of(own + qb * bq, bq), bq), q_heads, pairs, low_q)
        acc_ref[...] = jnp.zeros_like(acc_ref)
        max_ref[...] = jnp.full_like(max_ref, FLOOR)

        def step(j, masked, carry):
            there = pl.ds(pl.multiple_of(j * bk, bk), bk)
            def pair_step(pair, carry):
                lanes = pl.ds(pair * 128, 128)
                key = k_ref[there, lanes]
                value = v_ref[there, lanes]
                for odd in range(2):
                    head = 2 * pair + odd
                    scores = dot(q_heads[head], key, NT)
                    if masked:
                        scores = jnp.where(wide(cols_ref[...], bk) == ids_ref[0:1, there], scores, NEG)
                    old = max_ref[head]
                    new = jnp.maximum(old, jnp.max(scores, axis=1, keepdims=True))
                    probs = jnp.exp(scores - wide(new, bk)).astype(BF16)
                    ones = jnp.where(low_k if odd == 0 else ~low_k, value, jnp.ones_like(value))
                    acc_ref[head] = acc_ref[head] * jnp.exp(old - new) + dot(probs, ones)
                    max_ref[head] = new
                return carry
            for pair in range(pairs):
                pair_step(pair, carry)
            return carry

        sweep(rng_ref, qb, step)
        stats = jnp.zeros((bq, 128), F32)
        lane = lax.broadcasted_iota(jnp.int32, (bq, 128), 1)
        for pair in range(pairs):
            even, odd = acc_ref[2 * pair], acc_ref[2 * pair + 1]
            total_even, total_odd = even[:, 64:65], odd[:, 0:1]
            mixed = jnp.where(low_q, even / total_even, odd / total_odd)
            o_ref[mine, pair * 128:pair * 128 + 128] = mixed.astype(BF16)
            stats = jnp.where(lane == 2 * pair, max_ref[2 * pair] + jnp.log(total_even), stats)
            stats = jnp.where(lane == 2 * pair + 1, max_ref[2 * pair + 1] + jnp.log(total_odd), stats)
        lse_ref[mine, :] = stats
        return carry

    lax.fori_loop(0, rows // bq, block, 0)

def attention_forward(rng, query, key, value, ids, rows, own, bq=256, bk=256):
    width = query.shape[1]
    heads = width // 64
    return pl.pallas_call(
        functools.partial(fwd_kernel, bq, bk, own),
        out_shape=(jax.ShapeDtypeStruct((rows, width), BF16), jax.ShapeDtypeStruct((rows, 128), F32)),
        in_specs=[pl.BlockSpec(memory_space=pltpu.SMEM)] + [pl.BlockSpec(memory_space=pltpu.VMEM)] * 4,
        out_specs=(pl.BlockSpec(memory_space=pltpu.VMEM),) * 2,
        scratch_shapes=[pltpu.VMEM((heads, bq, 128), F32), pltpu.VMEM((heads, bq, 128), F32), pltpu.VMEM((heads, bq, 128), BF16), pltpu.VMEM((bq, 128), F32)],
        compiler_params=pltpu.CompilerParams(vmem_limit_bytes=24 << 20),
        name="attention_forward",
    )(rng, query, key, value, ids)

def bwd_kernel(bq, bk, own, rng_ref, q_ref, k_ref, v_ref, g_ref, ids_ref, lse_ref, along_ref, rows_ref, out_ref, dq_acc, dk_acc, dv_acc, q_heads, k_heads, v_heads, g_heads, lse_cols, along_cols, cols_ref):
    rows, width = out_ref.shape[0], q_ref.shape[1]
    pairs = width // 128
    heads = 2 * pairs
    low_q = low_half((bq, 128))

    def block(b, carry):
        start = pl.multiple_of(b * bq, bq)
        mine = pl.ds(start, bq)
        here = pl.ds(pl.multiple_of(own + start, bq), bq)
        cols_ref[...] = id_columns(ids_ref, pl.multiple_of(own + start, bq), bq)
        for source, target in ((q_ref, q_heads), (k_ref, k_heads), (v_ref, v_heads), (g_ref, g_heads)):
            split_heads(source, here, target, pairs, low_q)
        for head in range(heads):
            lse_cols[head] = jnp.broadcast_to(lse_ref[mine, head:head + 1], (bq, 128))
            along_cols[head] = jnp.broadcast_to(along_ref[mine, head:head + 1], (bq, 128))
        for acc in (dq_acc, dk_acc, dv_acc):
            acc[...] = jnp.zeros_like(acc)

        def step(j, masked, carry):
            there = pl.ds(pl.multiple_of(j * bk, bk), bk)
            def pair_step(pair, carry):
                lanes = pl.ds(pair * 128, 128)
                q_far, k_far, v_far, g_far = (r[there, lanes] for r in (q_ref, k_ref, v_ref, g_ref))
                def hide(x):
                    return jnp.where(wide(cols_ref[...], bk) == ids_ref[0:1, there], x, 0.0) if masked else x
                for odd in range(2):
                    head = 2 * pair + odd
                    scores = dot(q_heads[head], k_far, NT)
                    probs = hide(jnp.exp(scores - wide(lse_cols[head], bk)))
                    slope = dot(g_heads[head], v_far, NT)
                    grad = (probs * (slope - wide(along_cols[head], bk))).astype(BF16)
                    dq_acc[head] += dot(grad, k_far)
                    scores = dot(k_heads[head], q_far, NT)
                    probs = hide(jnp.exp(scores - rows_ref[pl.ds(head, 1), there]))
                    slope = dot(v_heads[head], g_far, NT)
                    grad = (probs * (slope - rows_ref[pl.ds(8 + head, 1), there])).astype(BF16)
                    dv_acc[head] += dot(probs.astype(BF16), g_far)
                    dk_acc[head] += dot(grad, q_far)
                return carry
            for pair in range(pairs):
                pair_step(pair, carry)
            return carry

        sweep(rng_ref, b, step)
        for which, (acc, factor) in enumerate(((dq_acc, 0.125), (dk_acc, 1.0), (dv_acc, 1.0))):
            for pair in range(pairs):
                both = jnp.where(low_q, acc[2 * pair], acc[2 * pair + 1]) * factor
                out_ref[mine, which * width + pair * 128:which * width + pair * 128 + 128] = both.astype(BF16)
        return carry

    lax.fori_loop(0, rows // bq, block, 0)

def attention_backward(rng, query, key, value, grads, ids, lse, along, stat_rows, rows, own, bq=256, bk=256):
    width = query.shape[1]
    heads = width // 64
    return pl.pallas_call(
        functools.partial(bwd_kernel, bq, bk, own),
        out_shape=jax.ShapeDtypeStruct((rows, 3 * width), BF16),
        in_specs=[pl.BlockSpec(memory_space=pltpu.SMEM)] + [pl.BlockSpec(memory_space=pltpu.VMEM)] * 8,
        out_specs=pl.BlockSpec(memory_space=pltpu.VMEM),
        scratch_shapes=[pltpu.VMEM((heads, bq, 128), F32)] * 3 + [pltpu.VMEM((heads, bq, 128), BF16)] * 4 + [pltpu.VMEM((heads, bq, 128), F32)] * 2 + [pltpu.VMEM((bq, 128), F32)],
        compiler_params=pltpu.CompilerParams(vmem_limit_bytes=40 << 20),
        name="attention_backward",
    )(rng, query, key, value, grads, ids, lse, along, stat_rows)

class Halo:
    def __init__(self, count, pieces, send_sem, recv_sem):
        self.count, self.pieces, self.send_sem, self.recv_sem = count, pieces, send_sem, recv_sem
        s = self.s = lax.axis_index("seq")
        self.core = lax.rem(s, 2)
        self.sibling = s + 1 - 2 * self.core
        self.left, self.right = s >= 2, s < count - 2

    def greet(self):
        s, count = self.s, self.count
        greet([(s >= k, {"seq": s - k}) for k in (1, 2)] + [(s < count - k, {"seq": s + k}) for k in (1, 2)])

    def own(self, part, kind, slot, target):
        source, window = self.pieces[part]
        return remote(source, window(slot), self.send_sem.at[kind, part], self.recv_sem.at[slot, part], seq=target)

    def moved(self, part, kind, held, slot, target):
        window = self.pieces[part][1]
        return remote(window(held), window(slot), self.send_sem.at[kind, part], self.recv_sem.at[slot, part], seq=target)

    def first_copies(self, part):
        s, core = self.s, self.core
        return (
            (self.right, self.own(part, 0, 1, s + 2)),
            (self.left, self.own(part, 1, 5, s - 2)),
            (core == 0, self.own(part, 2, 2, self.sibling)),
            (core == 1, self.own(part, 2, 4, self.sibling)),
        )

    def from_left(self, part):
        s, core, left, right = self.s, self.core, self.left, self.right
        return (
            (jnp.logical_and(left, jnp.logical_and(core == 1, right)), self.moved(part, 3, 1, 0, s + 1)),
            (jnp.logical_and(left, core == 0), self.moved(part, 4, 1, 0, self.sibling)),
            (jnp.logical_and(left, core == 1), self.moved(part, 4, 1, 2, self.sibling)),
        )

    def from_right(self, part):
        s, core, left, right = self.s, self.core, self.left, self.right
        return (
            (jnp.logical_and(right, jnp.logical_and(core == 0, left)), self.moved(part, 5, 5, 6, s - 1)),
            (jnp.logical_and(right, core == 0), self.moved(part, 6, 5, 4, self.sibling)),
            (jnp.logical_and(right, core == 1), self.moved(part, 6, 5, 6, self.sibling)),
        )

    def each(self, copies, act):
        for present, copy in copies:
            pl.when(present)(functools.partial(act, copy))

    def send(self, part):
        self.each(self.first_copies(part), lambda copy: copy.start())

    def arrived(self, slot, part):
        self.own(part, 0, slot, self.s).wait_recv()

    def relay(self, part):
        pl.when(self.left)(functools.partial(self.arrived, 1, part))
        self.each(self.from_left(part), lambda copy: copy.start())
        pl.when(self.right)(functools.partial(self.arrived, 5, part))
        self.each(self.from_right(part), lambda copy: copy.start())

    def present(self, slot):
        block = self.s + slot - REACH
        return jnp.logical_and(block >= 0, block < self.count)

    def receive(self, slot):
        for part in range(len(self.pieces)):
            pl.when(self.present(slot))(functools.partial(self.arrived, slot, part))

    def finish(self):
        for part in range(len(self.pieces)):
            self.each(self.first_copies(part) + self.from_left(part) + self.from_right(part), lambda copy: copy.wait_send())


def project_kernel(count, parts, own_ref, slots_ref, memory_ref, weight_ref, query_bias_ref, value_bias_ref,
                   q_ref, k_ref, v_ref, source_ref, window_ref, send_sem, recv_sem):
    block = own_ref.shape[0]
    rows = block // parts
    tile = 256
    tiles = block // tile

    def piece(part):
        return own_ref.at[pl.ds(part * rows, rows)], lambda slot: window_ref.at[pl.ds(slot * block + part * rows, rows)]

    halo = Halo(count, [piece(part) for part in range(parts)], send_sem, recv_sem)
    halo.greet()
    for part in range(parts):
        halo.send(part)

    def project(load, start, keep):
        hot = (lax.broadcasted_iota(jnp.int32, (32, tile), 0) == slots_ref[0:1, pl.ds(start, tile)]).astype(F32).astype(BF16)
        tn = (((0,), (0,)), ((), ()))
        chosen = dot(hot, memory_ref[...], tn)
        inside = wide(dot(hot, jnp.ones((32, 128), BF16), tn), chosen.shape[1])
        source = jnp.where(inside > 0.5, chosen, load().astype(F32)).astype(BF16)
        keep(source)
        out = pl.ds(start, tile)
        q_ref[out, :] = (dot(source, weight_ref[0]) + query_bias_ref[...]).astype(BF16) * 0.125
        k_ref[out, :] = dot(source, weight_ref[1]).astype(BF16)
        v_ref[out, :] = (dot(source, weight_ref[2]) + value_bias_ref[...]).astype(BF16)

    def own_tile(i, carry):
        at = pl.ds(pl.multiple_of(i * tile, tile), tile)

        def keep(source):
            source_ref[at, :] = source

        project(lambda: own_ref[at, :], pl.multiple_of(REACH * block + i * tile, tile), keep)
        return carry

    lax.fori_loop(0, tiles, own_tile, 0)
    for part in range(parts):
        halo.relay(part)

    def two_blocks(low, high):
        def step(i, carry):
            slot = low + (high - low) * (i // tiles)

            @pl.when(halo.present(slot))
            def _():
                start = pl.multiple_of(slot * block + lax.rem(i, tiles) * tile, tile)
                project(lambda: window_ref[pl.ds(start, tile), :], start, lambda source: None)

            return carry

        lax.fori_loop(0, 2 * tiles, step, 0)

    two_blocks(1, 5)
    for slots in ((2, 4), (0, 6)):
        for slot in slots:
            halo.receive(slot)
        two_blocks(*slots)
    halo.finish()


def project_window(own, slots, memory, weight, query_bias, value_bias, count, collective_id, parts=2):
    rows, dim = own.shape
    width = weight.shape[2]
    total = (2 * REACH + 1) * rows
    wide_out = jax.ShapeDtypeStruct((total, width), BF16)
    return pl.pallas_call(
        functools.partial(project_kernel, count, parts),
        out_shape=(wide_out, wide_out, wide_out, jax.ShapeDtypeStruct((rows, dim), BF16)),
        in_specs=[VMEM] * 6,
        out_specs=(VMEM,) * 4,
        scratch_shapes=[
            pltpu.VMEM((total, dim), BF16),
            pltpu.SemaphoreType.DMA((7, parts)),
            pltpu.SemaphoreType.DMA((7, parts)),
        ],
        compiler_params=pltpu.CompilerParams(collective_id=collective_id, has_side_effects=True, vmem_limit_bytes=40 << 20),
        name="project_window",
    )(own, slots, memory, weight, query_bias, value_bias)


def grads_kernel(count, parts, grad_ref, mixed_ref, lse_ref, low_ref, window_ref, stats_ref, along_ref, out_grad_ref, own_stats, send_sem, recv_sem):
    block, width = grad_ref.shape
    rows = block // parts

    def piece(part):
        return grad_ref.at[pl.ds(part * rows, rows)], lambda slot: window_ref.at[pl.ds(slot * block + part * rows, rows)]

    stats_piece = own_stats, lambda slot: stats_ref.at[:, pl.ds(slot * block, block)]
    halo = Halo(count, [piece(part) for part in range(parts)] + [stats_piece], send_sem, recv_sem)
    halo.greet()
    for part in range(parts):
        halo.send(part)
    window_ref[REACH * block:(REACH + 1) * block, :] = grad_ref[...]
    lane = lax.broadcasted_iota(jnp.int32, (block, 128), 1)
    along = jnp.zeros((block, 128), F32)
    for pair in range(width // 128):
        lanes = slice(pair * 128, pair * 128 + 128)
        product = grad_ref[:, lanes].astype(F32) * mixed_ref[:, lanes].astype(F32)
        even = jnp.sum(jnp.where(lane < 64, product, 0.0), axis=1, keepdims=True)
        odd = jnp.sum(jnp.where(lane < 64, 0.0, product), axis=1, keepdims=True)
        along = jnp.where(lane == 2 * pair, even, jnp.where(lane == 2 * pair + 1, odd, along))
    along_ref[...] = along
    own_stats[0:8, :] = jnp.transpose(lse_ref[...])[0:8, :]
    own_stats[8:16, :] = jnp.transpose(along)[0:8, :]
    stats_ref[:, REACH * block:(REACH + 1) * block] = own_stats[...]
    halo.send(parts)
    out_grad_ref[...] = dot(low_ref[...], mixed_ref[...], (((0,), (0,)), ((), ()))).astype(BF16)
    for part in range(parts + 1):
        halo.relay(part)
    for slot in (0, 2, 4, 6):
        halo.receive(slot)
    halo.finish()


def gather_grads(grad, mixed, lse, low, count, collective_id, parts=2):
    rows, width = grad.shape
    total = (2 * REACH + 1) * rows
    return pl.pallas_call(
        functools.partial(grads_kernel, count, parts),
        out_shape=(
            jax.ShapeDtypeStruct((total, width), BF16),
            jax.ShapeDtypeStruct((16, total), F32),
            jax.ShapeDtypeStruct((rows, 128), F32),
            jax.ShapeDtypeStruct((low.shape[1], width), BF16),
        ),
        in_specs=[VMEM] * 4,
        out_specs=(VMEM,) * 4,
        scratch_shapes=[
            pltpu.VMEM((16, rows), F32),
            pltpu.SemaphoreType.DMA((7, parts + 1)),
            pltpu.SemaphoreType.DMA((7, parts + 1)),
        ],
        compiler_params=pltpu.CompilerParams(collective_id=collective_id, has_side_effects=True, vmem_limit_bytes=24 << 20),
        name="gather_grads",
    )(grad, mixed, lse, low)


def split_dot(left, right, dims):
    high = right.astype(BF16)
    low = (right - high.astype(F32)).astype(BF16)
    return dot(left, high, dims) + dot(left, low, dims)


def tail_kernel(dps, seqs, width, *refs):
    (early_refs, (out_grad_ref, proj_ref, source_ref, weight_ref, input1_ref, select_ref, small_ref),
     (up_out, down_out, out_out, qkv_out, input_out, small_out),
     (mix, y_send, y_recv, a_recv, parts, b_recv, small_in, small_recv, small_mine, small_dp),
     (mine, c_recv, last, d_recv), (y_sems, a_sems, b_sems, c_sems, d_sems, s_sems)) = (
        refs[:dps], refs[dps:dps + 7], refs[dps + 7:dps + 13], refs[dps + 13:dps + 23], refs[dps + 23:dps + 27], refs[dps + 27:])
    zs = seqs // 2
    bits = zs.bit_length() - 1
    t, d, s = lax.axis_index("tensor"), lax.axis_index("dp"), lax.axis_index("seq")
    z, core = s // 2, lax.rem(s, 2)
    sibling = s + 1 - 2 * core
    late, early = a_recv.shape[0], mine.shape[0] - a_recv.shape[0]
    chunk = a_recv.shape[3]
    shares = -(-chunk // width)
    owners = small_out.shape[0]
    block, hidden = up_out.shape
    share_width = early * width
    rows, columns = proj_ref.shape
    third = columns // 3
    steps = y_send.shape[0]
    span = rows // steps
    true = s >= 0
    partners = [(true, {"seq": lax.rem(s + k, seqs)}) for k in range(1, seqs)]
    partners += [(true, {"dp": lax.rem(d + k, dps)}) for k in range(1, dps)]
    partners += [(true, {"tensor": 1 - t})]
    greet(partners)

    def active(c):
        return true if c < early else d < shares

    def a_copy(c, j):
        start = pl.multiple_of((2 * j + 1 - core) * block, 16)
        at = (c - early) * chunk
        i = c - early
        return remote(mix.at[pl.ds(start, block), pl.ds(at, chunk)], a_recv.at[i, j], a_sems.at[0, i, j], a_sems.at[1, i, j], seq=sibling)

    def b_copy(c, k):
        other = lax.rem(d + k, dps)
        i = c - early
        return other, remote(parts.at[i, other], b_recv.at[i, k], b_sems.at[0, i, k], b_sems.at[1, i, k], dp=other)

    def first_slot(b):
        return sum(zs // (2 << e) for e in range(b))

    def c_copies(c, b):
        size = 2 << b
        high = lax.rem(z // (1 << b), 2)
        partner = z + (1 << b) - (size * high)
        low = lax.rem(partner, size)
        return [
            remote(mine.at[c, i * size + low], c_recv.at[c, first_slot(b) + i], c_sems.at[0, c, first_slot(b) + i], c_sems.at[1, c, first_slot(b) + i], seq=2 * partner + core)
            for i in range(zs // size)
        ]

    def d_copy(c, k):
        return remote(last.at[c], d_recv.at[c, k], d_sems.at[0, c, k], d_sems.at[1, c, k], dp=lax.rem(d + k, dps))

    def start_a(c):
        for j in range(zs):
            a_copy(c, j).start()

    def start_early(c):
        lanes = slice(c * width, c * width + width)
        for j in range(zs):
            total = early_refs[0][0, j, :, lanes].astype(F32)
            for k in range(1, dps):
                total = total + early_refs[k][j, :, lanes].astype(F32)
            mine[c, j] = total.astype(BF16)
        for copy in c_copies(c, 0):
            copy.start()

    def end_a(c):
        i = c - early
        for j in range(zs):
            a_copy(c, j).wait()
            start = pl.multiple_of((2 * j + core) * block, 16)
            for p in range(shares):
                real = min(width, chunk - p * width)
                lanes = pl.ds(i * chunk + p * width, real)
                total = mix[pl.ds(start, block), lanes].astype(F32) + a_recv[i, j, :, p * width:p * width + real].astype(F32)
                parts[i, p, j, :, 0:real] = total.astype(BF16)
                if real < width:
                    parts[i, p, j, :, real:width] = jnp.zeros((block, width - real), BF16)
        for k in range(1, dps):
            other, copy = b_copy(c, k)
            pl.when(other < shares)(copy.start)

    def end_b(c):
        i = c - early
        for k in range(1, dps):
            other, copy = b_copy(c, k)
            pl.when(other < shares)(copy.wait_send)

        @pl.when(d < shares)
        def _():
            for k in range(1, dps):
                b_copy(c, k)[1].wait_recv()
            for j in range(zs):
                total = parts[i, d, j].astype(F32)
                for k in range(1, dps):
                    total = total + b_recv[i, k, j].astype(F32)
                mine[c, j] = total.astype(BF16)
            for copy in c_copies(c, 0):
                copy.start()

    def end_c(c, b):
        size = 2 << b
        kept = lax.rem(z, size)

        @pl.when(active(c))
        def _():
            for i, copy in enumerate(c_copies(c, b)):
                copy.wait()
                held = mine[c, i * size + kept].astype(F32) + c_recv[c, first_slot(b) + i].astype(F32)
                if b < bits - 1:
                    mine[c, i * size + kept] = held.astype(BF16)
                else:
                    last[c] = held.astype(BF16)
            if b < bits - 1:
                for copy in c_copies(c, b + 1):
                    copy.start()
            else:
                for k in range(1, dps):
                    d_copy(c, k).start()

    def put(c, share, value):
        count = dps if c < early else shares
        for p in range(count):

            @pl.when(share == p)
            def _():
                if c < early:
                    which, column = divmod(p * share_width + c * width, hidden)
                    (up_out, down_out)[which][:, column:column + width] = value.astype(F32)
                    return
                first = (c - early) * chunk + p * width
                for lane in range(0, min(width, chunk - p * width), 128):
                    which, column = divmod(first + lane, third)
                    part = value[:, lane:lane + 128].astype(F32)
                    if which == 0:
                        out_out[:, column:column + 128] = part
                    else:
                        qkv_out[which - 1, :, column:column + 128] = part

    def end_d(c):
        @pl.when(active(c))
        def _():
            put(c, d, last[c])
            for k in range(1, dps):
                d_copy(c, k).wait_send()

        for k in range(1, dps):
            share = lax.rem(d + dps - k, dps)

            @pl.when(true if c < early else share < shares)
            def _():
                d_copy(c, k).wait_recv()
                put(c, share, d_recv[c, k])

    def y_copy(i):
        return remote(y_send.at[i], y_recv.at[i], y_sems.at[0, i], y_sems.at[1, i], tensor=1 - t)

    for c in range(early):
        start_early(c)
    out_width = out_grad_ref.shape[1]
    mix[:, 0:out_width] = out_grad_ref[...]
    for i in range(3):
        part = lax.dot_general(source_ref[...], proj_ref[:, i * third:(i + 1) * third], (((0,), (0,)), ((), ())), preferred_element_type=F32)
        mix[:, out_width + i * third:out_width + (i + 1) * third] = part.astype(BF16)
    for c in range(early, early + late):
        start_a(c)
    for i in range(steps):
        at = slice(i * span, (i + 1) * span)
        y_send[i] = sum(dot(proj_ref[at, j * third:(j + 1) * third], weight_ref[j], NT) for j in range(3)).astype(BF16)
        y_copy(i).start()
    small_in[0] = small_ref[...]
    for i in range(1, owners):
        small_in[i] = jnp.zeros_like(small_ref)
    small_in[1, 0:1, 0:third] = jnp.sum(proj_ref[:, 0:third].astype(F32), axis=0, keepdims=True)
    small_in[1, 0:1, third:2 * third] = jnp.sum(proj_ref[:, 2 * third:3 * third].astype(F32), axis=0, keepdims=True)

    def end_y():
        memory = jnp.zeros((32, input_out.shape[1]), F32)
        for i in range(steps):
            y_copy(i).wait()
            at = slice(i * span, (i + 1) * span)
            total = input1_ref[at, :] + (y_send[i].astype(F32) + y_recv[i].astype(F32))
            select = select_ref[at, :]
            memory = memory + split_dot(select, total, (((0,), (0,)), ((), ())))
            inside = dot(select, jnp.ones((32, total.shape[1]), BF16))
            input_out[at, :] = jnp.where(inside > 0.5, 0.0, total).astype(BF16)
        small_in[1, 1:8, :] = memory[0:7]
        small_in[2] = memory[7:15]
        small_in[3, 0:5, :] = memory[15:20]
        for hop in range(1, seqs):
            owner = lax.rem(s + hop, seqs)
            pl.when(owner < owners)(to_owner(hop, owner).start)

    def to_owner(hop, owner):
        return remote(small_in.at[owner], small_recv.at[hop], s_sems.at[0, 0, hop], s_sems.at[1, 0, hop], seq=owner)

    def across(k):
        return remote(small_mine, small_dp.at[k], s_sems.at[0, 1, k], s_sems.at[1, 1, k], dp=lax.rem(d + k, dps))

    def back(hop, owner, target):
        return remote(small_out.at[owner], small_out.at[owner], s_sems.at[0, 2, hop], s_sems.at[1, 2, hop], seq=target)

    def small_one():
        @pl.when(s < owners)
        def _():
            total = small_in[s]
            for hop in range(1, seqs):
                to_owner(hop, s).wait_recv()
                total = total + small_recv[hop]
            small_mine[...] = total
            for k in range(1, dps):
                across(k).start()

    def small_two():
        @pl.when(s < owners)
        def _():
            small_dp[0] = small_mine[...]
            for k in range(1, dps):
                across(k).wait()
            ordered = jnp.zeros(small_mine.shape, F32)
            for index in range(dps):
                ordered = ordered + small_dp[lax.rem(d + dps - index, dps)]
            small_out[s] = ordered
            for hop in range(1, seqs):
                back(hop, s, lax.rem(s + hop, seqs)).start()

    def small_three():
        for hop in range(1, seqs):
            owner = lax.rem(s + hop, seqs)
            pl.when(owner < owners)(to_owner(hop, owner).wait_send)
        for hop in range(1, seqs):
            pl.when(lax.rem(s + seqs - hop, seqs) < owners)(back(hop, 0, s).wait_recv)
            pl.when(s < owners)(back(hop, 0, s).wait_send)

    zed = [functools.partial(end_c, b=b) for b in range(bits)]
    lates = list(range(early, early + late))
    for c in lates:
        end_a(c)
    for c in range(early):
        zed[0](c)
    for c in lates:
        end_b(c)
    end_y()
    for b in range(1, bits):
        for c in range(early):
            zed[b](c)
        for c in lates:
            zed[b - 1](c)
        if b == 1:
            small_one()
    for c in range(early):
        end_d(c)
    small_two()
    for c in lates:
        zed[bits - 1](c)
    for c in lates:
        end_d(c)
    small_three()


def tail(early, out, proj, source, weight, input1, select, small, dps, seqs):
    zs = seqs // 2
    dim = source.shape[1]
    hidden = early[0].shape[3] * dps // 2
    rows = proj.shape[0]
    block = dim // seqs
    mixed = out.shape[1] + proj.shape[1]
    late = 2
    chunk = mixed // late
    width = -(-chunk // (128 * dps)) * 128
    width = early[0].shape[3] if early[0].shape[3] % width else width
    chunks = early[0].shape[3] // width + late
    steps = 4
    table = (OWNERS,) + small.shape
    dma = pltpu.SemaphoreType.DMA
    return pl.pallas_call(
        functools.partial(tail_kernel, dps, seqs, width),
        out_shape=(
            jax.ShapeDtypeStruct((block, hidden), F32),
            jax.ShapeDtypeStruct((block, hidden), F32),
            jax.ShapeDtypeStruct((block, out.shape[1]), F32),
            jax.ShapeDtypeStruct((3, block, out.shape[1]), F32),
            jax.ShapeDtypeStruct((rows, dim), BF16),
            jax.ShapeDtypeStruct(table, F32),
        ),
        in_specs=[VMEM] * (dps + 7),
        out_specs=(VMEM,) * 6,
        scratch_shapes=[
            pltpu.VMEM((dim, mixed), BF16),
            pltpu.VMEM((steps, rows // steps, dim), BF16),
            pltpu.VMEM((steps, rows // steps, dim), BF16),
            pltpu.VMEM((late, zs, block, chunk), BF16),
            pltpu.VMEM((late, dps, zs, block, width), BF16),
            pltpu.VMEM((late, dps, zs, block, width), BF16),
            pltpu.VMEM(table, F32),
            pltpu.VMEM((seqs,) + small.shape, F32),
            pltpu.VMEM(small.shape, F32),
            pltpu.VMEM((dps,) + small.shape, F32),
            pltpu.VMEM((chunks, zs, block, width), BF16),
            pltpu.VMEM((chunks, zs - 1, block, width), BF16),
            pltpu.VMEM((chunks, block, width), BF16),
            pltpu.VMEM((chunks, dps, block, width), BF16),
            dma((2, steps)),
            dma((2, late, zs)),
            dma((2, late, dps)),
            dma((2, chunks, zs)),
            dma((2, chunks, dps)),
            dma((2, 3, max(seqs, dps))),
        ],
        compiler_params=pltpu.CompilerParams(collective_id=7, has_side_effects=True, vmem_limit_bytes=48 << 20),
        name="tail",
    )(*early, out, proj, source, weight, input1, select, small)


def feed_kernel(dps, seqs, span, mixed_ref, out_ref, other_ref, source_ref, up_ref, down_ref, vec_ref, grad_ref,
                y_ref, input1_ref, low_ref, mixed_grad_ref, shares_ref, small_ref,
                out_all, mixed_all, first_ref, hat_ref, scale_ref, first_low, act_ref, slope_ref, second_ref, down_grad, up_grad,
                y_send, y_recv, z_send, z_recv, grads, a_recv, m_sems, y_sems, z_sems, a_sems):
    rows, dim = source_ref.shape
    width, hidden = mixed_ref.shape[1], up_ref.shape[1]
    zs, block = seqs // 2, dim // seqs
    t, d, s = lax.axis_index("tensor"), lax.axis_index("dp"), lax.axis_index("seq")
    core = lax.rem(s, 2)
    sibling = s + 1 - 2 * core
    spans = rows // span
    true = s >= 0
    greet([(true, {"tensor": 1 - t}), (true, {"seq": sibling})])
    tn = (((0,), (0,)), ((), ()))

    def at(i):
        return pl.ds(pl.multiple_of(i * span, span), span)

    mine = pl.ds(pl.multiple_of(t * width, 128), width)
    theirs = pl.ds(pl.multiple_of((1 - t) * width, 128), width)

    def m_copy(i):
        return remote(mixed_ref.at[at(i)], mixed_all.at[at(i), mine], m_sems.at[0, i], m_sems.at[1, i], tensor=1 - t)

    def y_copy(i):
        return remote(y_send.at[at(i)], y_recv.at[at(i)], y_sems.at[0, i], y_sems.at[1, i], tensor=1 - t)

    def z_copy(i):
        return remote(z_send.at[at(i)], z_recv.at[at(i)], z_sems.at[0, i], z_sems.at[1, i], tensor=1 - t)

    def a_copy(which, j):
        start = pl.multiple_of((2 * j + 1 - core) * block, 16)
        return remote(grads.at[which, pl.ds(start, block)], a_recv.at[which, j], a_sems.at[0, which, j], a_sems.at[1, which, j], seq=sibling)

    def mean(x):
        return jnp.mean(x, axis=1, keepdims=True)

    def norm(x):
        centred = x - mean(x)
        scale = lax.rsqrt(mean(centred * centred) + NORM_EPS)
        return centred * scale, scale

    def norm_back(grad, hat, scale, gain):
        grad = grad * gain
        return scale * (grad - mean(grad) - hat * mean(grad * hat))

    def add_rows(row, x):
        small_ref[row:row + 1, :] += jnp.sum(x, axis=0, keepdims=True)

    out_bias, gain1, shift1, down_bias, gain2, shift2 = (vec_ref[i:i + 1, :] for i in range(6))

    for i in range(spans):
        m_copy(i).start()
    out_all[:, mine] = out_ref[...]
    out_all[:, theirs] = other_ref[...]
    mixed_all[:, mine] = mixed_ref[...]
    small_ref[...] = jnp.zeros_like(small_ref)

    def forward(i, carry):
        m_copy(i).wait()
        branch = dot(mixed_all[at(i), :], out_all[...], NT) + out_bias
        hat, scale = norm(source_ref[at(i), :].astype(F32) + branch)
        first = hat * gain1 + shift1
        low = first.astype(BF16)
        hat_ref[at(i), :] = hat
        scale_ref[at(i), :] = jnp.broadcast_to(scale, (span, 128))
        first_ref[at(i), :] = first
        first_low[at(i), :] = low
        part = jnp.zeros((span, dim), F32)
        for k in range(2):
            cols = slice(k * dim, (k + 1) * dim)
            up = dot(low, up_ref[:, cols]) + vec_ref[6 + k:7 + k, :]
            below = 0.5 + 0.5 * lax.erf(up * 0.7071067811865476)
            act = (up * below).astype(BF16)
            slope_ref[at(i), cols] = below + up * jnp.exp(-0.5 * up * up) * 0.3989422804014327
            act_ref[at(i), cols] = act
            part = part + dot(act, down_ref[:, cols], NT)
        y_send[at(i), :] = part.astype(BF16)
        y_copy(i).start()
        return carry

    lax.fori_loop(0, spans, forward, 0)

    def turn(i, carry):
        y_copy(i).wait()
        down = y_send[at(i), :].astype(F32) + y_recv[at(i), :].astype(F32) + down_bias
        hat, scale = norm(first_ref[at(i), :] + down)
        y_ref[at(i), :] = (hat * gain2 + shift2).astype(BF16)
        grad = grad_ref[at(i), :].astype(F32)
        add_rows(2, grad * hat)
        add_rows(3, grad)
        second = norm_back(grad, hat, scale, gain2)
        low = second.astype(BF16)
        second_ref[at(i), :] = second
        down_grad[at(i), :] = low
        add_rows(5, low.astype(F32))
        part = jnp.zeros((span, dim), F32)
        for k in range(2):
            cols = slice(k * dim, (k + 1) * dim)
            up = (slope_ref[at(i), cols] * dot(low, down_ref[:, cols])).astype(BF16)
            up_grad[at(i), cols] = up
            add_rows(6 + k, up.astype(F32))
            part = part + dot(up, up_ref[:, cols], NT)
        z_send[at(i), :] = part.astype(BF16)
        z_copy(i).start()
        return carry

    lax.fori_loop(0, spans, turn, 0)

    def products(j, carry):
        cols = pl.ds(pl.multiple_of(j * 512, 512), 512)
        grads[0, :, cols] = dot(first_low[...], up_grad[:, cols], tn).astype(BF16)
        grads[1, :, cols] = dot(down_grad[...], act_ref[:, cols], tn).astype(BF16)
        return carry

    lax.fori_loop(0, hidden // 512, products, 0)
    for which in range(2):
        for j in range(zs):
            a_copy(which, j).start()

    def back(i, carry):
        z_copy(i).wait()
        grad = second_ref[at(i), :] + (z_send[at(i), :].astype(F32) + z_recv[at(i), :].astype(F32))
        hat = hat_ref[at(i), :]
        add_rows(0, grad * hat)
        add_rows(1, grad)
        total = norm_back(grad, hat, scale_ref[at(i), 0:1], gain1)
        low = total.astype(BF16)
        input1_ref[at(i), :] = total
        low_ref[at(i), :] = low
        add_rows(4, low.astype(F32))
        mixed_grad_ref[at(i), :] = dot(low, out_ref[...]).astype(BF16)
        return carry

    lax.fori_loop(0, spans, back, 0)
    share = 2 * hidden // dps
    for which in range(2):
        for j in range(zs):
            a_copy(which, j).wait()
            own = pl.ds(pl.multiple_of((2 * j + core) * block, 16), block)
            for p in range(dps):
                if p * share // hidden <= which <= ((p + 1) * share - 1) // hidden:
                    first, last = max(p * share, which * hidden), min((p + 1) * share, (which + 1) * hidden)
                    cols = slice(first - which * hidden, last - which * hidden)
                    total = grads[which, own, cols].astype(F32) + a_recv[which, j, :, cols].astype(F32)
                    shares_ref[lax.rem(p - d + dps, dps), j, :, first - p * share:last - p * share] = total.astype(BF16)


def feed_forward(mixed, out_weight, out_other, source, up, down, vectors, grad, dps, seqs, span=256):
    rows, dim = source.shape
    width, hidden = mixed.shape[1], up.shape[1]
    zs, block = seqs // 2, dim // seqs
    spans = rows // span
    dma = pltpu.SemaphoreType.DMA
    return pl.pallas_call(
        functools.partial(feed_kernel, dps, seqs, span),
        out_shape=(
            jax.ShapeDtypeStruct((rows, dim), BF16),
            jax.ShapeDtypeStruct((rows, dim), F32),
            jax.ShapeDtypeStruct((rows, dim), BF16),
            jax.ShapeDtypeStruct((rows, width), BF16),
            jax.ShapeDtypeStruct((dps, zs, block, 2 * hidden // dps), BF16),
            jax.ShapeDtypeStruct((8, dim), F32),
        ),
        in_specs=[VMEM] * 8,
        out_specs=(VMEM,) * 6,
        scratch_shapes=[
            pltpu.VMEM((dim, 2 * width), BF16),
            pltpu.VMEM((rows, 2 * width), BF16),
            pltpu.VMEM((rows, dim), F32),
            pltpu.VMEM((rows, dim), F32),
            pltpu.VMEM((rows, 128), F32),
            pltpu.VMEM((rows, dim), BF16),
            pltpu.VMEM((rows, hidden), BF16),
            pltpu.VMEM((rows, hidden), F32),
            pltpu.VMEM((rows, dim), F32),
            pltpu.VMEM((rows, dim), BF16),
            pltpu.VMEM((rows, hidden), BF16),
            pltpu.VMEM((rows, dim), BF16),
            pltpu.VMEM((rows, dim), BF16),
            pltpu.VMEM((rows, dim), BF16),
            pltpu.VMEM((rows, dim), BF16),
            pltpu.VMEM((2, dim, hidden), BF16),
            pltpu.VMEM((2, zs, block, hidden), BF16),
            dma((2, spans)),
            dma((2, spans)),
            dma((2, spans)),
            dma((2, 2, zs)),
        ],
        compiler_params=pltpu.CompilerParams(collective_id=3, has_side_effects=True, vmem_limit_bytes=56 << 20),
        name="feed_forward",
    )(mixed, out_weight, out_other, source, up, down, vectors, grad)


def memory_slots(id_row):
    count = id_row.shape[0]
    edge = jnp.full((READ_ROWS,), -1, jnp.int32)
    padded = jnp.concatenate([edge, id_row, edge])
    before = sum((padded[READ_ROWS - k:READ_ROWS - k + count] == id_row).astype(jnp.int32) for k in range(1, READ_ROWS + 1))
    behind = sum((padded[READ_ROWS + k:READ_ROWS + k + count] == id_row).astype(jnp.int32) for k in range(1, READ_ROWS + 1))
    return jnp.where(before < READ_ROWS, before, jnp.where(behind < READ_ROWS, 2 * READ_ROWS - 1 - behind, -1))


def document_blocks(id_row, own_ids, window_start, bk):
    bounds = jnp.stack([own_ids[0], own_ids[-1] + 1])
    start_end = jnp.sum((id_row[None, :] < bounds[:, None]).astype(jnp.int32), axis=1) - window_start
    shift = bk.bit_length() - 1
    floor, ceil = start_end >> shift, (start_end + bk - 1) >> shift
    first, last = floor[0], ceil[1]
    whole = jnp.logical_and(bounds[0] + 1 == bounds[1], ceil[0] < floor[1])
    inside = jnp.where(whole, jnp.stack([ceil[0], floor[1]]), first)
    return jnp.concatenate([floor[:1], inside, ceil[1:]]).astype(jnp.int32)


def on_device(dps, seqs, tokens, doc_ids, memory, qkv_weight, query_bias, value_bias, out_weight, out_bias, norm1_gain, norm1_bias, up_weight, up_bias, down_weight, down_bias, norm2_gain, norm2_bias, out_grad):
    rows = tokens.shape[1]
    width = qkv_weight.shape[2]
    heads = width // HEAD_DIM
    bq, bk = rows, 256
    own = REACH * rows
    pieces = 2 * REACH + 1
    s = lax.axis_index("seq")
    id_row = doc_ids[0]
    edge = jnp.full((own,), -1, jnp.int32)
    window_start = s * rows - own
    slots = memory_slots(id_row)
    window_slots = lax.dynamic_slice_in_dim(jnp.concatenate([edge, slots, edge]), s * rows, pieces * rows, 0)
    window_ids = lax.dynamic_slice_in_dim(jnp.concatenate([edge, id_row, edge]), s * rows, pieces * rows, 0)
    own_ids = window_ids[own:own + rows]
    blocks = document_blocks(id_row, own_ids, window_start, bk)
    ids = jnp.broadcast_to(window_ids.astype(F32)[None], (8, pieces * rows))

    out_other = lax.ppermute(out_weight, "tensor", [(0, 1), (1, 0)])
    weight = qkv_weight.transpose(1, 0, 2)
    slots_row = jnp.broadcast_to(window_slots[None], (8, pieces * rows))
    memory_pad = jnp.pad(memory, ((0, 32 - memory.shape[0]), (0, 0)))
    query, key, value, source = project_window(
        tokens[0], slots_row, memory_pad, weight, query_bias[None], value_bias[None], seqs, 1)
    own_slots = window_slots[own:own + rows]

    mixed_low, logsums = attention_forward(blocks, query, key, value, ids, rows, own, bq, bk)

    vectors = jnp.stack([out_bias, norm1_gain, norm1_bias, down_bias, norm2_gain, norm2_bias, up_bias[:2 * width], up_bias[2 * width:]])
    output, grad_input1, branch_grad, mixed_grad, shares, small = feed_forward(
        mixed_low, out_weight, out_other, source, up_weight, down_weight, vectors, out_grad[0], dps, seqs)
    early = [shares] + [
        lax.ppermute(shares[k], "dp", [(i, (i + k) % dps) for i in range(dps)]) for k in range(1, dps)]
    grads_window, stats_window, along_cols, grad_out_weight = gather_grads(mixed_grad, mixed_low, logsums, branch_grad, seqs, 2)
    proj_grad = attention_backward(blocks, query, key, value, grads_window, ids, logsums, along_cols, stats_window, rows, own, bq, bk)

    select = (own_slots[:, None] == jnp.arange(32, dtype=jnp.int32)[None, :]).astype(BF16)
    up_sum, down_sum, out_sum, qkv_sum, input_grad, small = tail(
        early, grad_out_weight, proj_grad, source, weight, grad_input1, select, small, dps, seqs)
    small = small.reshape(32, 2 * width)
    input_grad = input_grad[None]
    piece = small.shape[1] // seqs
    vectors = lax.dynamic_slice_in_dim(small[:6], s * piece, piece, 1)
    memory_grad = small[9:29]
    return (
        output[None], input_grad, memory_grad,
        qkv_sum.transpose(1, 0, 2), small[8, :width], small[8, width:],
        out_sum, vectors[4], vectors[0], vectors[1],
        up_sum, small[6:8].reshape(-1), down_sum, vectors[5], vectors[2], vectors[3],
    )


def solution(mesh):
    in_specs = (
        P("dp", "seq", None), P("dp", None), P(), P(None, None, "tensor"), P("tensor"), P("tensor"), P(None, "tensor"), P(), P(), P(),
        P(None, "tensor"), P("tensor"), P(None, "tensor"), P(), P(), P(), P("dp", "seq", None),
    )
    out_specs = (
        P("dp", "seq", None), P("dp", "seq", None), P(), P("seq", None, "tensor"), P("tensor"), P("tensor"), P("seq", "tensor"), P("seq"), P("seq"), P("seq"),
        P("seq", "tensor"), P("tensor"), P("seq", "tensor"), P("seq"), P("seq"), P("seq"),
    )
    step = functools.partial(on_device, mesh.shape["dp"], mesh.shape["seq"])
    return jax.shard_map(step, mesh=mesh, in_specs=in_specs, out_specs=out_specs, check_vma=False)
```

```python
import functools

import jax
import jax.numpy as jnp
from jax import lax
from jax.experimental import pallas as pl
from jax.experimental.pallas import tpu as pltpu
from jax.sharding import PartitionSpec as P

HEAD_DIM = 64
READ_ROWS = 10
REACH = 3
NORM_EPS = 1e-05
OWNERS = 4
F32, BF16 = jnp.float32, jnp.bfloat16
NT = (((1,), (1,)), ((), ()))
NN = (((1,), (0,)), ((), ()))
NEG = -1e30
FLOOR = -1e29
VMEM = pl.BlockSpec(memory_space=pltpu.VMEM)
HBM = pl.BlockSpec(memory_space=pltpu.HBM)


def remote(source, target, send_sem, recv_sem, **where):
    return pltpu.make_async_remote_copy(
        source, target, send_sem, recv_sem, device_id=where, device_id_type=pl.DeviceIdType.MESH
    )


def greet(partners):
    barrier = pltpu.get_barrier_semaphore()
    total = 0
    for present, where in partners:
        total = total + present.astype(jnp.int32)

        @pl.when(present)
        def _():
            pl.semaphore_signal(barrier, inc=1, device_id=where, device_id_type=pl.DeviceIdType.MESH)

    pl.semaphore_wait(barrier, total)


def dot(a, b, dims=NN):
    return lax.dot_general(a, b, dims, preferred_element_type=F32)

def low_half(shape):
    return lax.broadcasted_iota(jnp.int32, shape, len(shape) - 1) < 64

def id_columns(ids_ref, start, count):
    row = jnp.broadcast_to(ids_ref[0:1, pl.ds(start, count)], (128, count))
    return jnp.transpose(row)

def wide(x, count):
    return jnp.concatenate([x] * (count // 128), axis=1)

def split_heads(source_ref, rows, target_ref, pairs, keep):
    for pair in range(pairs):
        block = source_ref[rows, pair * 128:pair * 128 + 128]
        target_ref[2 * pair] = jnp.where(keep, block, jnp.zeros_like(block))
        target_ref[2 * pair + 1] = jnp.where(keep, jnp.zeros_like(block), block)

def sweep(ids_ref, start, count, bk, body):
    mine, every = ids_ref[0:1, pl.ds(start, count)], ids_ref[0:1, :]
    low, high = jnp.min(mine), jnp.max(mine)
    begin = jnp.sum(jnp.where(every < low, 1.0, 0.0)).astype(jnp.int32)
    end = jnp.sum(jnp.where(every <= high, 1.0, 0.0)).astype(jnp.int32)
    shift = bk.bit_length() - 1
    first, last = begin >> shift, (end + bk - 1) >> shift
    full_first, full_last = (begin + bk - 1) >> shift, end >> shift
    whole = jnp.logical_and(low == high, full_first < full_last)
    full_first, full_last = jnp.where(whole, full_first, first), jnp.where(whole, full_last, first)
    lax.fori_loop(full_first, full_last, lambda j, c: body(j, False, c), 0)

    def edge(i, c):
        j = first + i
        return body(jnp.where(j < full_first, j, j + full_last - full_first), True, c)

    lax.fori_loop(0, last - first - (full_last - full_first), edge, 0)

def fwd_kernel(bq, bk, own, q_ref, k_ref, v_ref, ids_ref, o_ref, lse_ref, acc_ref, max_ref, q_heads, cols_ref):
    pairs = q_ref.shape[1] // 128
    rows = o_ref.shape[0]
    low_q, low_k = low_half((bq, 128)), low_half((bk, 128))

    def block(qb, carry):
        mine = pl.ds(pl.multiple_of(qb * bq, bq), bq)
        cols_ref[...] = id_columns(ids_ref, pl.multiple_of(own + qb * bq, bq), bq)
        split_heads(q_ref, pl.ds(pl.multiple_of(own + qb * bq, bq), bq), q_heads, pairs, low_q)
        acc_ref[...] = jnp.zeros_like(acc_ref)
        max_ref[...] = jnp.full_like(max_ref, FLOOR)

        def step(j, masked, carry):
            there = pl.ds(pl.multiple_of(j * bk, bk), bk)
            def pair_step(pair, carry):
                lanes = pl.ds(pair * 128, 128)
                key = k_ref[there, lanes]
                value = v_ref[there, lanes]
                for odd in range(2):
                    head = 2 * pair + odd
                    scores = dot(q_heads[head], key, NT)
                    if masked:
                        scores = jnp.where(wide(cols_ref[...], bk) == ids_ref[0:1, there], scores, NEG)
                    old = max_ref[head]
                    new = jnp.maximum(old, jnp.max(scores, axis=1, keepdims=True))
                    probs = jnp.exp(scores - wide(new, bk)).astype(BF16)
                    ones = jnp.where(low_k if odd == 0 else ~low_k, value, jnp.ones_like(value))
                    acc_ref[head] = acc_ref[head] * jnp.exp(old - new) + dot(probs, ones)
                    max_ref[head] = new
                return carry
            for pair in range(pairs):
                pair_step(pair, carry)
            return carry

        sweep(ids_ref, pl.multiple_of(own + qb * bq, bq), bq, bk, step)
        stats = jnp.zeros((bq, 128), F32)
        lane = lax.broadcasted_iota(jnp.int32, (bq, 128), 1)
        for pair in range(pairs):
            even, odd = acc_ref[2 * pair], acc_ref[2 * pair + 1]
            total_even, total_odd = even[:, 64:65], odd[:, 0:1]
            mixed = jnp.where(low_q, even / total_even, odd / total_odd)
            o_ref[mine, pair * 128:pair * 128 + 128] = mixed.astype(BF16)
            stats = jnp.where(lane == 2 * pair, max_ref[2 * pair] + jnp.log(total_even), stats)
            stats = jnp.where(lane == 2 * pair + 1, max_ref[2 * pair + 1] + jnp.log(total_odd), stats)
        lse_ref[mine, :] = stats
        return carry

    lax.fori_loop(0, rows // bq, block, 0)

def attention_forward(query, key, value, ids, rows, own, bq=256, bk=256):
    width = query.shape[1]
    heads = width // 64
    return pl.pallas_call(
        functools.partial(fwd_kernel, bq, bk, own),
        out_shape=(jax.ShapeDtypeStruct((rows, width), BF16), jax.ShapeDtypeStruct((rows, 128), F32)),
        in_specs=[VMEM] * 4,
        out_specs=(pl.BlockSpec(memory_space=pltpu.VMEM),) * 2,
        scratch_shapes=[pltpu.VMEM((heads, bq, 128), F32), pltpu.VMEM((heads, bq, 128), F32), pltpu.VMEM((heads, bq, 128), BF16), pltpu.VMEM((bq, 128), F32)],
        compiler_params=pltpu.CompilerParams(vmem_limit_bytes=24 << 20),
        name="attention_forward",
    )(query, key, value, ids)

def bwd_kernel(bq, bk, own, q_ref, k_ref, v_ref, g_ref, ids_ref, lse_ref, along_ref, rows_ref, out_ref, dq_acc, dk_acc, dv_acc, q_heads, k_heads, v_heads, g_heads, lse_cols, along_cols, cols_ref):
    rows, width = out_ref.shape[0], q_ref.shape[1]
    pairs = width // 128
    heads = 2 * pairs
    low_q = low_half((bq, 128))

    def block(b, carry):
        start = pl.multiple_of(b * bq, bq)
        mine = pl.ds(start, bq)
        here = pl.ds(pl.multiple_of(own + start, bq), bq)
        cols_ref[...] = id_columns(ids_ref, pl.multiple_of(own + start, bq), bq)
        for source, target in ((q_ref, q_heads), (k_ref, k_heads), (v_ref, v_heads), (g_ref, g_heads)):
            split_heads(source, here, target, pairs, low_q)
        for head in range(heads):
            lse_cols[head] = jnp.broadcast_to(lse_ref[mine, head:head + 1], (bq, 128))
            along_cols[head] = jnp.broadcast_to(along_ref[mine, head:head + 1], (bq, 128))
        for acc in (dq_acc, dk_acc, dv_acc):
            acc[...] = jnp.zeros_like(acc)

        def step(j, masked, carry):
            there = pl.ds(pl.multiple_of(j * bk, bk), bk)
            def pair_step(pair, carry):
                lanes = pl.ds(pair * 128, 128)
                q_far, k_far, v_far, g_far = (r[there, lanes] for r in (q_ref, k_ref, v_ref, g_ref))
                def hide(x):
                    return jnp.where(wide(cols_ref[...], bk) == ids_ref[0:1, there], x, 0.0) if masked else x
                for odd in range(2):
                    head = 2 * pair + odd
                    scores = dot(q_heads[head], k_far, NT)
                    probs = hide(jnp.exp(scores - wide(lse_cols[head], bk)))
                    slope = dot(g_heads[head], v_far, NT)
                    grad = (probs * (slope - wide(along_cols[head], bk))).astype(BF16)
                    dq_acc[head] += dot(grad, k_far)
                    scores = dot(k_heads[head], q_far, NT)
                    probs = hide(jnp.exp(scores - rows_ref[pl.ds(head, 1), there]))
                    slope = dot(v_heads[head], g_far, NT)
                    grad = (probs * (slope - rows_ref[pl.ds(8 + head, 1), there])).astype(BF16)
                    dv_acc[head] += dot(probs.astype(BF16), g_far)
                    dk_acc[head] += dot(grad, q_far)
                return carry
            for pair in range(pairs):
                pair_step(pair, carry)
            return carry

        sweep(ids_ref, pl.multiple_of(own + start, bq), bq, bk, step)
        for which, (acc, factor) in enumerate(((dq_acc, 0.125), (dk_acc, 1.0), (dv_acc, 1.0))):
            for pair in range(pairs):
                both = jnp.where(low_q, acc[2 * pair], acc[2 * pair + 1]) * factor
                out_ref[mine, which * width + pair * 128:which * width + pair * 128 + 128] = both.astype(BF16)
        return carry

    lax.fori_loop(0, rows // bq, block, 0)

def attention_backward(query, key, value, grads, ids, lse, along, stat_rows, rows, own, bq=256, bk=256):
    width = query.shape[1]
    heads = width // 64
    return pl.pallas_call(
        functools.partial(bwd_kernel, bq, bk, own),
        out_shape=jax.ShapeDtypeStruct((rows, 3 * width), BF16),
        in_specs=[VMEM] * 8,
        out_specs=pl.BlockSpec(memory_space=pltpu.VMEM),
        scratch_shapes=[pltpu.VMEM((heads, bq, 128), F32)] * 3 + [pltpu.VMEM((heads, bq, 128), BF16)] * 4 + [pltpu.VMEM((heads, bq, 128), F32)] * 2 + [pltpu.VMEM((bq, 128), F32)],
        compiler_params=pltpu.CompilerParams(vmem_limit_bytes=40 << 20),
        name="attention_backward",
    )(query, key, value, grads, ids, lse, along, stat_rows)

class Halo:
    def __init__(self, count, pieces, send_sem, recv_sem):
        self.count, self.pieces, self.send_sem, self.recv_sem = count, pieces, send_sem, recv_sem
        s = self.s = lax.axis_index("seq")
        self.core = lax.rem(s, 2)
        self.sibling = s + 1 - 2 * self.core
        self.left, self.right = s >= 2, s < count - 2

    def greet(self):
        s, count = self.s, self.count
        greet([(s >= k, {"seq": s - k}) for k in (1, 2)] + [(s < count - k, {"seq": s + k}) for k in (1, 2)])

    def own(self, part, kind, slot, target):
        source, window = self.pieces[part]
        return remote(source, window(slot), self.send_sem.at[kind, part], self.recv_sem.at[slot, part], seq=target)

    def moved(self, part, kind, held, slot, target):
        window = self.pieces[part][1]
        return remote(window(held), window(slot), self.send_sem.at[kind, part], self.recv_sem.at[slot, part], seq=target)

    def first_copies(self, part):
        s, core = self.s, self.core
        return (
            (self.right, self.own(part, 0, 1, s + 2)),
            (self.left, self.own(part, 1, 5, s - 2)),
            (core == 0, self.own(part, 2, 2, self.sibling)),
            (core == 1, self.own(part, 2, 4, self.sibling)),
        )

    def from_left(self, part):
        s, core, left, right = self.s, self.core, self.left, self.right
        return (
            (jnp.logical_and(left, jnp.logical_and(core == 1, right)), self.moved(part, 3, 1, 0, s + 1)),
            (jnp.logical_and(left, core == 0), self.moved(part, 4, 1, 0, self.sibling)),
            (jnp.logical_and(left, core == 1), self.moved(part, 4, 1, 2, self.sibling)),
        )

    def from_right(self, part):
        s, core, left, right = self.s, self.core, self.left, self.right
        return (
            (jnp.logical_and(right, jnp.logical_and(core == 0, left)), self.moved(part, 5, 5, 6, s - 1)),
            (jnp.logical_and(right, core == 0), self.moved(part, 6, 5, 4, self.sibling)),
            (jnp.logical_and(right, core == 1), self.moved(part, 6, 5, 6, self.sibling)),
        )

    def each(self, copies, act):
        for present, copy in copies:
            pl.when(present)(functools.partial(act, copy))

    def send(self, part):
        self.each(self.first_copies(part), lambda copy: copy.start())

    def arrived(self, slot, part):
        self.own(part, 0, slot, self.s).wait_recv()

    def relay(self, part):
        pl.when(self.left)(functools.partial(self.arrived, 1, part))
        self.each(self.from_left(part), lambda copy: copy.start())
        pl.when(self.right)(functools.partial(self.arrived, 5, part))
        self.each(self.from_right(part), lambda copy: copy.start())

    def present(self, slot):
        block = self.s + slot - REACH
        return jnp.logical_and(block >= 0, block < self.count)

    def receive(self, slot):
        for part in range(len(self.pieces)):
            pl.when(self.present(slot))(functools.partial(self.arrived, slot, part))

    def finish(self):
        for part in range(len(self.pieces)):
            self.each(self.first_copies(part) + self.from_left(part) + self.from_right(part), lambda copy: copy.wait_send())


def project_kernel(count, parts, own_ref, slots_ref, memory_ref, weight_ref, query_bias_ref, value_bias_ref,
                   q_ref, k_ref, v_ref, source_ref, window_ref, weight, send_sem, recv_sem, local_sem):
    block = own_ref.shape[0]
    rows = block // parts
    tile = 256
    tiles = block // tile

    def piece(part):
        return own_ref.at[pl.ds(part * rows, rows)], lambda slot: window_ref.at[pl.ds(slot * block + part * rows, rows)]

    halo = Halo(count, [piece(part) for part in range(parts)], send_sem, recv_sem)
    halo.greet()
    for part in range(parts):
        halo.send(part)
    local = [
        pltpu.make_async_copy(own_ref, window_ref.at[pl.ds(REACH * block, block)], local_sem.at[0]),
        pltpu.make_async_copy(weight_ref, weight, local_sem.at[1]),
    ]
    for copy in local:
        copy.start()
    query_bias, value_bias = query_bias_ref[...].reshape(1, -1), value_bias_ref[...].reshape(1, -1)

    def project(load, start, keep):
        hot = (lax.broadcasted_iota(jnp.int32, (32, tile), 0) == slots_ref[0:1, pl.ds(start, tile)]).astype(F32).astype(BF16)
        tn = (((0,), (0,)), ((), ()))
        chosen = dot(hot, memory_ref[...], tn)
        inside = wide(dot(hot, jnp.ones((32, 128), BF16), tn), chosen.shape[1])
        source = jnp.where(inside > 0.5, chosen, load().astype(F32)).astype(BF16)
        keep(source)
        out = pl.ds(start, tile)
        q_ref[out, :] = (dot(source, weight[0]) + query_bias).astype(BF16) * 0.125
        k_ref[out, :] = dot(source, weight[1]).astype(BF16)
        v_ref[out, :] = (dot(source, weight[2]) + value_bias).astype(BF16)

    def own_tile(i, carry):
        at = pl.ds(pl.multiple_of(i * tile, tile), tile)

        def keep(source):
            source_ref[at, :] = source

        start = pl.multiple_of(REACH * block + i * tile, tile)
        project(lambda: window_ref[pl.ds(start, tile), :], start, keep)
        return carry

    for copy in local:
        copy.wait()
    lax.fori_loop(0, tiles, own_tile, 0)
    for part in range(parts):
        halo.relay(part)

    def two_blocks(low, high):
        def step(i, carry):
            slot = low + (high - low) * (i // tiles)

            @pl.when(halo.present(slot))
            def _():
                start = pl.multiple_of(slot * block + lax.rem(i, tiles) * tile, tile)
                project(lambda: window_ref[pl.ds(start, tile), :], start, lambda source: None)

            return carry

        lax.fori_loop(0, 2 * tiles, step, 0)

    two_blocks(1, 5)
    for slots in ((2, 4), (0, 6)):
        for slot in slots:
            halo.receive(slot)
        two_blocks(*slots)
    halo.finish()


def project_window(own, slots, memory, weight, query_bias, value_bias, count, collective_id, parts=2):
    rows, dim = own.shape
    width = weight.shape[2]
    total = (2 * REACH + 1) * rows
    wide_out = jax.ShapeDtypeStruct((total, width), BF16)
    return pl.pallas_call(
        functools.partial(project_kernel, count, parts),
        out_shape=(wide_out, wide_out, wide_out, jax.ShapeDtypeStruct((rows, dim), BF16)),
        in_specs=[HBM, VMEM, VMEM, HBM, VMEM, VMEM],
        out_specs=(VMEM,) * 4,
        scratch_shapes=[
            pltpu.VMEM((total, dim), BF16),
            pltpu.VMEM(weight.shape, BF16),
            pltpu.SemaphoreType.DMA((7, parts)),
            pltpu.SemaphoreType.DMA((7, parts)),
            pltpu.SemaphoreType.DMA((2,)),
        ],
        compiler_params=pltpu.CompilerParams(collective_id=collective_id, has_side_effects=True, vmem_limit_bytes=40 << 20),
        name="project_window",
    )(own, slots, memory, weight, query_bias, value_bias)


def grads_kernel(count, parts, grad_ref, mixed_ref, lse_ref, low_ref, window_ref, stats_ref, along_ref, out_grad_ref, own_stats, send_sem, recv_sem):
    block, width = grad_ref.shape
    rows = block // parts

    def piece(part):
        return grad_ref.at[pl.ds(part * rows, rows)], lambda slot: window_ref.at[pl.ds(slot * block + part * rows, rows)]

    stats_piece = own_stats, lambda slot: stats_ref.at[:, pl.ds(slot * block, block)]
    halo = Halo(count, [piece(part) for part in range(parts)] + [stats_piece], send_sem, recv_sem)
    halo.greet()
    for part in range(parts):
        halo.send(part)
    window_ref[REACH * block:(REACH + 1) * block, :] = grad_ref[...]
    lane = lax.broadcasted_iota(jnp.int32, (block, 128), 1)
    along = jnp.zeros((block, 128), F32)
    for pair in range(width // 128):
        lanes = slice(pair * 128, pair * 128 + 128)
        product = grad_ref[:, lanes].astype(F32) * mixed_ref[:, lanes].astype(F32)
        even = jnp.sum(jnp.where(lane < 64, product, 0.0), axis=1, keepdims=True)
        odd = jnp.sum(jnp.where(lane < 64, 0.0, product), axis=1, keepdims=True)
        along = jnp.where(lane == 2 * pair, even, jnp.where(lane == 2 * pair + 1, odd, along))
    along_ref[...] = along
    own_stats[0:8, :] = jnp.transpose(lse_ref[...])[0:8, :]
    own_stats[8:16, :] = jnp.transpose(along)[0:8, :]
    stats_ref[:, REACH * block:(REACH + 1) * block] = own_stats[...]
    halo.send(parts)
    out_grad_ref[...] = dot(low_ref[...], mixed_ref[...], (((0,), (0,)), ((), ()))).astype(BF16)
    for part in range(parts + 1):
        halo.relay(part)
    for slot in (0, 2, 4, 6):
        halo.receive(slot)
    halo.finish()


def gather_grads(grad, mixed, lse, low, count, collective_id, parts=2):
    rows, width = grad.shape
    total = (2 * REACH + 1) * rows
    return pl.pallas_call(
        functools.partial(grads_kernel, count, parts),
        out_shape=(
            jax.ShapeDtypeStruct((total, width), BF16),
            jax.ShapeDtypeStruct((16, total), F32),
            jax.ShapeDtypeStruct((rows, 128), F32),
            jax.ShapeDtypeStruct((low.shape[1], width), BF16),
        ),
        in_specs=[VMEM] * 4,
        out_specs=(VMEM,) * 4,
        scratch_shapes=[
            pltpu.VMEM((16, rows), F32),
            pltpu.SemaphoreType.DMA((7, parts + 1)),
            pltpu.SemaphoreType.DMA((7, parts + 1)),
        ],
        compiler_params=pltpu.CompilerParams(collective_id=collective_id, has_side_effects=True, vmem_limit_bytes=24 << 20),
        name="gather_grads",
    )(grad, mixed, lse, low)


def split_dot(left, right, dims):
    high = right.astype(BF16)
    low = (right - high.astype(F32)).astype(BF16)
    return dot(left, high, dims) + dot(left, low, dims)


def tail_kernel(dps, seqs, width, *refs):
    (early_refs, (out_grad_ref, proj_ref, source_ref, weight_ref, input1_ref, select_ref, small_ref),
     (up_out, down_out, out_out, qkv_out, input_out, small_out),
     (mix, y_send, y_recv, a_recv, parts, b_recv, small_in, small_recv, small_mine, small_dp),
     (mine, c_recv, last, d_recv), (y_sems, a_sems, b_sems, c_sems, d_sems, s_sems)) = (
        refs[:dps], refs[dps:dps + 7], refs[dps + 7:dps + 13], refs[dps + 13:dps + 23], refs[dps + 23:dps + 27], refs[dps + 27:])
    zs = seqs // 2
    bits = zs.bit_length() - 1
    t, d, s = lax.axis_index("tensor"), lax.axis_index("dp"), lax.axis_index("seq")
    z, core = s // 2, lax.rem(s, 2)
    sibling = s + 1 - 2 * core
    late, early = a_recv.shape[0], mine.shape[0] - a_recv.shape[0]
    chunk = a_recv.shape[3]
    shares = -(-chunk // width)
    owners = small_out.shape[0]
    block, hidden = up_out.shape
    share_width = early * width
    rows, columns = proj_ref.shape
    third = columns // 3
    steps = y_send.shape[0]
    span = rows // steps
    true = s >= 0
    partners = [(true, {"seq": lax.rem(s + k, seqs)}) for k in range(1, seqs)]
    partners += [(true, {"dp": lax.rem(d + k, dps)}) for k in range(1, dps)]
    partners += [(true, {"tensor": 1 - t})]
    greet(partners)

    def active(c):
        return true if c < early else d < shares

    def a_copy(c, j):
        start = pl.multiple_of((2 * j + 1 - core) * block, 16)
        at = (c - early) * chunk
        i = c - early
        return remote(mix.at[pl.ds(start, block), pl.ds(at, chunk)], a_recv.at[i, j], a_sems.at[0, i, j], a_sems.at[1, i, j], seq=sibling)

    def b_copy(c, k):
        other = lax.rem(d + k, dps)
        i = c - early
        return other, remote(parts.at[i, other], b_recv.at[i, k], b_sems.at[0, i, k], b_sems.at[1, i, k], dp=other)

    def first_slot(b):
        return sum(zs // (2 << e) for e in range(b))

    def c_copies(c, b):
        size = 2 << b
        high = lax.rem(z // (1 << b), 2)
        partner = z + (1 << b) - (size * high)
        low = lax.rem(partner, size)
        return [
            remote(mine.at[c, i * size + low], c_recv.at[c, first_slot(b) + i], c_sems.at[0, c, first_slot(b) + i], c_sems.at[1, c, first_slot(b) + i], seq=2 * partner + core)
            for i in range(zs // size)
        ]

    def d_copy(c, k):
        return remote(last.at[c], d_recv.at[c, k], d_sems.at[0, c, k], d_sems.at[1, c, k], dp=lax.rem(d + k, dps))

    def start_a(c):
        for j in range(zs):
            a_copy(c, j).start()

    def start_early(c):
        lanes = slice(c * width, c * width + width)
        for j in range(zs):
            total = early_refs[0][j, :, lanes].astype(F32)
            for k in range(1, dps):
                total = total + early_refs[k][j, :, lanes].astype(F32)
            mine[c, j] = total.astype(BF16)
        for copy in c_copies(c, 0):
            copy.start()

    def end_a(c):
        i = c - early
        for j in range(zs):
            a_copy(c, j).wait()
            start = pl.multiple_of((2 * j + core) * block, 16)
            for p in range(shares):
                real = min(width, chunk - p * width)
                lanes = pl.ds(i * chunk + p * width, real)
                total = mix[pl.ds(start, block), lanes].astype(F32) + a_recv[i, j, :, p * width:p * width + real].astype(F32)
                parts[i, p, j, :, 0:real] = total.astype(BF16)
                if real < width:
                    parts[i, p, j, :, real:width] = jnp.zeros((block, width - real), BF16)
        for k in range(1, dps):
            other, copy = b_copy(c, k)
            pl.when(other < shares)(copy.start)

    def end_b(c):
        i = c - early
        for k in range(1, dps):
            other, copy = b_copy(c, k)
            pl.when(other < shares)(copy.wait_send)

        @pl.when(d < shares)
        def _():
            for k in range(1, dps):
                b_copy(c, k)[1].wait_recv()
            for j in range(zs):
                total = parts[i, d, j].astype(F32)
                for k in range(1, dps):
                    total = total + b_recv[i, k, j].astype(F32)
                mine[c, j] = total.astype(BF16)
            for copy in c_copies(c, 0):
                copy.start()

    def end_c(c, b):
        size = 2 << b
        kept = lax.rem(z, size)

        @pl.when(active(c))
        def _():
            for i, copy in enumerate(c_copies(c, b)):
                copy.wait()
                held = mine[c, i * size + kept].astype(F32) + c_recv[c, first_slot(b) + i].astype(F32)
                if b < bits - 1:
                    mine[c, i * size + kept] = held.astype(BF16)
                else:
                    last[c] = held.astype(BF16)
            if b < bits - 1:
                for copy in c_copies(c, b + 1):
                    copy.start()
            else:
                for k in range(1, dps):
                    d_copy(c, k).start()

    def put(c, share, value):
        count = dps if c < early else shares
        for p in range(count):

            @pl.when(share == p)
            def _():
                if c < early:
                    which, column = divmod(p * share_width + c * width, hidden)
                    (up_out, down_out)[which][:, column:column + width] = value.astype(F32)
                    return
                first = (c - early) * chunk + p * width
                for lane in range(0, min(width, chunk - p * width), 128):
                    which, column = divmod(first + lane, third)
                    part = value[:, lane:lane + 128].astype(F32)
                    if which == 0:
                        out_out[:, column:column + 128] = part
                    else:
                        qkv_out[which - 1, :, column:column + 128] = part

    def end_d(c):
        @pl.when(active(c))
        def _():
            put(c, d, last[c])
            for k in range(1, dps):
                d_copy(c, k).wait_send()

        for k in range(1, dps):
            share = lax.rem(d + dps - k, dps)

            @pl.when(true if c < early else share < shares)
            def _():
                d_copy(c, k).wait_recv()
                put(c, share, d_recv[c, k])

    def y_copy(i):
        return remote(y_send.at[i], y_recv.at[i], y_sems.at[0, i], y_sems.at[1, i], tensor=1 - t)

    for c in range(early):
        start_early(c)
    out_width = out_grad_ref.shape[1]
    mix[:, 0:out_width] = out_grad_ref[...]
    for i in range(3):
        part = lax.dot_general(source_ref[...], proj_ref[:, i * third:(i + 1) * third], (((0,), (0,)), ((), ())), preferred_element_type=F32)
        mix[:, out_width + i * third:out_width + (i + 1) * third] = part.astype(BF16)
    for c in range(early, early + late):
        start_a(c)
    for i in range(steps):
        at = slice(i * span, (i + 1) * span)
        y_send[i] = sum(dot(proj_ref[at, j * third:(j + 1) * third], weight_ref[j], NT) for j in range(3)).astype(BF16)
        y_copy(i).start()
    small_in[0] = small_ref[...]
    for i in range(1, owners):
        small_in[i] = jnp.zeros_like(small_ref)
    small_in[1, 0:1, 0:third] = jnp.sum(proj_ref[:, 0:third].astype(F32), axis=0, keepdims=True)
    small_in[1, 0:1, third:2 * third] = jnp.sum(proj_ref[:, 2 * third:3 * third].astype(F32), axis=0, keepdims=True)

    def end_y():
        memory = jnp.zeros((32, input_out.shape[1]), F32)
        for i in range(steps):
            y_copy(i).wait()
            at = slice(i * span, (i + 1) * span)
            total = input1_ref[at, :] + (y_send[i].astype(F32) + y_recv[i].astype(F32))
            select = select_ref[at, :]
            memory = memory + split_dot(select, total, (((0,), (0,)), ((), ())))
            inside = dot(select, jnp.ones((32, total.shape[1]), BF16))
            input_out[at, :] = jnp.where(inside > 0.5, 0.0, total).astype(BF16)
        small_in[1, 1:8, :] = memory[0:7]
        small_in[2] = memory[7:15]
        small_in[3, 0:5, :] = memory[15:20]
        for hop in range(1, seqs):
            owner = lax.rem(s + hop, seqs)
            pl.when(owner < owners)(to_owner(hop, owner).start)

    def to_owner(hop, owner):
        return remote(small_in.at[owner], small_recv.at[hop], s_sems.at[0, 0, hop], s_sems.at[1, 0, hop], seq=owner)

    def across(k):
        return remote(small_mine, small_dp.at[k], s_sems.at[0, 1, k], s_sems.at[1, 1, k], dp=lax.rem(d + k, dps))

    def back(hop, owner, target):
        return remote(small_out.at[owner], small_out.at[owner], s_sems.at[0, 2, hop], s_sems.at[1, 2, hop], seq=target)

    def small_one():
        @pl.when(s < owners)
        def _():
            total = small_in[s]
            for hop in range(1, seqs):
                to_owner(hop, s).wait_recv()
                total = total + small_recv[hop]
            small_mine[...] = total
            for k in range(1, dps):
                across(k).start()

    def small_two():
        @pl.when(s < owners)
        def _():
            small_dp[0] = small_mine[...]
            for k in range(1, dps):
                across(k).wait()
            ordered = jnp.zeros(small_mine.shape, F32)
            for index in range(dps):
                ordered = ordered + small_dp[lax.rem(d + dps - index, dps)]
            small_out[s] = ordered
            for hop in range(1, seqs):
                back(hop, s, lax.rem(s + hop, seqs)).start()

    def small_three():
        for hop in range(1, seqs):
            owner = lax.rem(s + hop, seqs)
            pl.when(owner < owners)(to_owner(hop, owner).wait_send)
        for hop in range(1, seqs):
            pl.when(lax.rem(s + seqs - hop, seqs) < owners)(back(hop, 0, s).wait_recv)
            pl.when(s < owners)(back(hop, 0, s).wait_send)

    zed = [functools.partial(end_c, b=b) for b in range(bits)]
    lates = list(range(early, early + late))
    for c in lates:
        end_a(c)
    for c in range(early):
        zed[0](c)
    for c in lates:
        end_b(c)
    end_y()
    for b in range(1, bits):
        for c in range(early):
            zed[b](c)
        for c in lates:
            zed[b - 1](c)
        if b == 1:
            small_one()
    for c in range(early):
        end_d(c)
    small_two()
    for c in lates:
        zed[bits - 1](c)
    for c in lates:
        end_d(c)
    small_three()


def tail(early, out, proj, source, weight, input1, select, small, dps, seqs):
    zs = seqs // 2
    dim = source.shape[1]
    hidden = early[0].shape[2] * dps // 2
    rows = proj.shape[0]
    block = dim // seqs
    mixed = out.shape[1] + proj.shape[1]
    late = 2
    chunk = mixed // late
    width = -(-chunk // (128 * dps)) * 128
    width = early[0].shape[2] if early[0].shape[2] % width else width
    chunks = early[0].shape[2] // width + late
    steps = 4
    table = (OWNERS,) + small.shape
    dma = pltpu.SemaphoreType.DMA
    return pl.pallas_call(
        functools.partial(tail_kernel, dps, seqs, width),
        out_shape=(
            jax.ShapeDtypeStruct((block, hidden), F32),
            jax.ShapeDtypeStruct((block, hidden), F32),
            jax.ShapeDtypeStruct((block, out.shape[1]), F32),
            jax.ShapeDtypeStruct((3, block, out.shape[1]), F32),
            jax.ShapeDtypeStruct((rows, dim), BF16),
            jax.ShapeDtypeStruct(table, F32),
        ),
        in_specs=[VMEM] * (dps + 7),
        out_specs=(VMEM,) * 6,
        scratch_shapes=[
            pltpu.VMEM((dim, mixed), BF16),
            pltpu.VMEM((steps, rows // steps, dim), BF16),
            pltpu.VMEM((steps, rows // steps, dim), BF16),
            pltpu.VMEM((late, zs, block, chunk), BF16),
            pltpu.VMEM((late, dps, zs, block, width), BF16),
            pltpu.VMEM((late, dps, zs, block, width), BF16),
            pltpu.VMEM(table, F32),
            pltpu.VMEM((seqs,) + small.shape, F32),
            pltpu.VMEM(small.shape, F32),
            pltpu.VMEM((dps,) + small.shape, F32),
            pltpu.VMEM((chunks, zs, block, width), BF16),
            pltpu.VMEM((chunks, zs - 1, block, width), BF16),
            pltpu.VMEM((chunks, block, width), BF16),
            pltpu.VMEM((chunks, dps, block, width), BF16),
            dma((2, steps)),
            dma((2, late, zs)),
            dma((2, late, dps)),
            dma((2, chunks, zs)),
            dma((2, chunks, dps)),
            dma((2, 3, max(seqs, dps))),
        ],
        compiler_params=pltpu.CompilerParams(collective_id=7, has_side_effects=True, vmem_limit_bytes=48 << 20),
        name="tail",
    )(*early, out, proj, source, weight, input1, select, small)


def feed_kernel(dps, seqs, span, *refs):
    (mixed_ref, out_ref, other_ref, source_ref, up_hbm, down_hbm, grad_ref), vectors = refs[:7], refs[7:14]
    share_refs = refs[14:14 + dps]
    feed_body(dps, seqs, span, mixed_ref, out_ref, other_ref, source_ref, up_hbm, down_hbm, grad_ref, vectors, share_refs, *refs[14 + dps:])


def feed_body(dps, seqs, span, mixed_ref, out_ref, other_ref, source_ref, up_hbm, down_hbm, grad_ref, vectors, share_refs,
                y_ref, input1_ref, low_ref, mixed_grad_ref, small_ref,
                up_ref, down_ref, w_sems, out_all, mixed_all, first_ref, hat_ref, scale_ref, first_low, act_ref, slope_ref, second_ref, down_grad, up_grad,
                y_send, y_recv, z_send, z_recv, grads, a_recv, m_sems, y_sems, z_sems, a_sems):
    rows, dim = source_ref.shape
    width, hidden = mixed_ref.shape[1], up_ref.shape[1]
    zs, block = seqs // 2, dim // seqs
    t, d, s = lax.axis_index("tensor"), lax.axis_index("dp"), lax.axis_index("seq")
    core = lax.rem(s, 2)
    sibling = s + 1 - 2 * core
    spans = rows // span
    true = s >= 0
    greet([(true, {"tensor": 1 - t}), (true, {"seq": sibling})])
    tn = (((0,), (0,)), ((), ()))

    def at(i):
        return pl.ds(pl.multiple_of(i * span, span), span)

    mine = pl.ds(pl.multiple_of(t * width, 128), width)
    theirs = pl.ds(pl.multiple_of((1 - t) * width, 128), width)

    def m_copy(i):
        return remote(mixed_ref.at[at(i)], mixed_all.at[at(i), mine], m_sems.at[0, i], m_sems.at[1, i], tensor=1 - t)

    def y_copy(i):
        return remote(y_send.at[at(i)], y_recv.at[at(i)], y_sems.at[0, i], y_sems.at[1, i], tensor=1 - t)

    def z_copy(i):
        return remote(z_send.at[at(i)], z_recv.at[at(i)], z_sems.at[0, i], z_sems.at[1, i], tensor=1 - t)

    def a_copy(which, j):
        start = pl.multiple_of((2 * j + 1 - core) * block, 16)
        return remote(grads.at[which, pl.ds(start, block)], a_recv.at[which, j], a_sems.at[0, which, j], a_sems.at[1, which, j], seq=sibling)

    def mean(x):
        return jnp.mean(x, axis=1, keepdims=True)

    def norm(x):
        centred = x - mean(x)
        scale = lax.rsqrt(mean(centred * centred) + NORM_EPS)
        return centred * scale, scale

    def norm_back(grad, hat, scale, gain):
        grad = grad * gain
        return scale * (grad - mean(grad) - hat * mean(grad * hat))

    def add_rows(row, x):
        small_ref[row:row + 1, :] += jnp.sum(x, axis=0, keepdims=True)

    out_bias, gain1, shift1, down_bias, gain2, shift2, up_bias = (ref[...].reshape(1, -1) for ref in vectors)

    for i in range(spans):
        m_copy(i).start()
    loads = [pltpu.make_async_copy(up_hbm, up_ref, w_sems.at[0]), pltpu.make_async_copy(down_hbm, down_ref, w_sems.at[1])]
    for copy in loads:
        copy.start()
    out_all[:, mine] = out_ref[...]
    out_all[:, theirs] = other_ref[...]
    mixed_all[:, mine] = mixed_ref[...]
    small_ref[...] = jnp.zeros_like(small_ref)
    for copy in loads:
        copy.wait()

    def forward(i, carry):
        m_copy(i).wait()
        branch = dot(mixed_all[at(i), :], out_all[...], NT) + out_bias
        hat, scale = norm(source_ref[at(i), :].astype(F32) + branch)
        first = hat * gain1 + shift1
        low = first.astype(BF16)
        hat_ref[at(i), :] = hat
        scale_ref[at(i), :] = jnp.broadcast_to(scale, (span, 128))
        first_ref[at(i), :] = first
        first_low[at(i), :] = low
        part = jnp.zeros((span, dim), F32)
        for k in range(2):
            cols = slice(k * dim, (k + 1) * dim)
            up = dot(low, up_ref[:, cols]) + up_bias[:, cols]
            below = 0.5 + 0.5 * lax.erf(up * 0.7071067811865476)
            act = (up * below).astype(BF16)
            slope_ref[at(i), cols] = below + up * jnp.exp(-0.5 * up * up) * 0.3989422804014327
            act_ref[at(i), cols] = act
            part = part + dot(act, down_ref[:, cols], NT)
        y_send[at(i), :] = part.astype(BF16)
        y_copy(i).start()
        return carry

    lax.fori_loop(0, spans, forward, 0)

    def turn(i, carry):
        y_copy(i).wait()
        down = y_send[at(i), :].astype(F32) + y_recv[at(i), :].astype(F32) + down_bias
        hat, scale = norm(first_ref[at(i), :] + down)
        y_ref[at(i), :] = (hat * gain2 + shift2).astype(BF16)
        grad = grad_ref[at(i), :].astype(F32)
        add_rows(2, grad * hat)
        add_rows(3, grad)
        second = norm_back(grad, hat, scale, gain2)
        low = second.astype(BF16)
        second_ref[at(i), :] = second
        down_grad[at(i), :] = low
        add_rows(5, low.astype(F32))
        part = jnp.zeros((span, dim), F32)
        for k in range(2):
            cols = slice(k * dim, (k + 1) * dim)
            up = (slope_ref[at(i), cols] * dot(low, down_ref[:, cols])).astype(BF16)
            up_grad[at(i), cols] = up
            add_rows(6 + k, up.astype(F32))
            part = part + dot(up, up_ref[:, cols], NT)
        z_send[at(i), :] = part.astype(BF16)
        z_copy(i).start()
        return carry

    lax.fori_loop(0, spans, turn, 0)

    def products(j, carry):
        cols = pl.ds(pl.multiple_of(j * 512, 512), 512)
        grads[0, :, cols] = dot(first_low[...], up_grad[:, cols], tn).astype(BF16)
        grads[1, :, cols] = dot(down_grad[...], act_ref[:, cols], tn).astype(BF16)
        return carry

    lax.fori_loop(0, hidden // 512, products, 0)
    for which in range(2):
        for j in range(zs):
            a_copy(which, j).start()

    def back(i, carry):
        z_copy(i).wait()
        grad = second_ref[at(i), :] + (z_send[at(i), :].astype(F32) + z_recv[at(i), :].astype(F32))
        hat = hat_ref[at(i), :]
        add_rows(0, grad * hat)
        add_rows(1, grad)
        total = norm_back(grad, hat, scale_ref[at(i), 0:1], gain1)
        low = total.astype(BF16)
        input1_ref[at(i), :] = total
        low_ref[at(i), :] = low
        add_rows(4, low.astype(F32))
        mixed_grad_ref[at(i), :] = dot(low, out_ref[...]).astype(BF16)
        return carry

    lax.fori_loop(0, spans, back, 0)
    share = 2 * hidden // dps
    for which in range(2):
        for j in range(zs):
            a_copy(which, j).wait()
            own = pl.ds(pl.multiple_of((2 * j + core) * block, 16), block)
            for p in range(dps):
                if p * share // hidden <= which <= ((p + 1) * share - 1) // hidden:
                    first, last = max(p * share, which * hidden), min((p + 1) * share, (which + 1) * hidden)
                    cols = slice(first - which * hidden, last - which * hidden)
                    total = grads[which, own, cols].astype(F32) + a_recv[which, j, :, cols].astype(F32)
                    for k in range(dps):

                        @pl.when(lax.rem(p - d + dps, dps) == k)
                        def _():
                            share_refs[k][j, :, first - p * share:last - p * share] = total.astype(BF16)


def feed_forward(mixed, out_weight, out_other, source, up, down, vectors, grad, dps, seqs, span=256):
    rows, dim = source.shape
    width, hidden = mixed.shape[1], up.shape[1]
    zs, block = seqs // 2, dim // seqs
    spans = rows // span
    dma = pltpu.SemaphoreType.DMA
    return pl.pallas_call(
        functools.partial(feed_kernel, dps, seqs, span),
        out_shape=(jax.ShapeDtypeStruct((zs, block, 2 * hidden // dps), BF16),) * dps + (
            jax.ShapeDtypeStruct((rows, dim), BF16),
            jax.ShapeDtypeStruct((rows, dim), F32),
            jax.ShapeDtypeStruct((rows, dim), BF16),
            jax.ShapeDtypeStruct((rows, width), BF16),
            jax.ShapeDtypeStruct((8, dim), F32),
        ),
        in_specs=[VMEM] * 4 + [HBM] * 2 + [VMEM] * 8,
        out_specs=(VMEM,) * (dps + 5),
        scratch_shapes=[
            pltpu.VMEM((dim, hidden), BF16),
            pltpu.VMEM((dim, hidden), BF16),
            dma((2,)),
            pltpu.VMEM((dim, 2 * width), BF16),
            pltpu.VMEM((rows, 2 * width), BF16),
            pltpu.VMEM((rows, dim), F32),
            pltpu.VMEM((rows, dim), F32),
            pltpu.VMEM((rows, 128), F32),
            pltpu.VMEM((rows, dim), BF16),
            pltpu.VMEM((rows, hidden), BF16),
            pltpu.VMEM((rows, hidden), F32),
            pltpu.VMEM((rows, dim), F32),
            pltpu.VMEM((rows, dim), BF16),
            pltpu.VMEM((rows, hidden), BF16),
            pltpu.VMEM((rows, dim), BF16),
            pltpu.VMEM((rows, dim), BF16),
            pltpu.VMEM((rows, dim), BF16),
            pltpu.VMEM((rows, dim), BF16),
            pltpu.VMEM((2, dim, hidden), BF16),
            pltpu.VMEM((2, zs, block, hidden), BF16),
            dma((2, spans)),
            dma((2, spans)),
            dma((2, spans)),
            dma((2, 2, zs)),
        ],
        compiler_params=pltpu.CompilerParams(collective_id=3, has_side_effects=True, vmem_limit_bytes=56 << 20),
        name="feed_forward",
    )(mixed, out_weight, out_other, source, up, down, grad, *vectors)


def memory_slots(id_row):
    count = id_row.shape[0]
    edge = jnp.full((READ_ROWS,), -1, jnp.int32)
    padded = jnp.concatenate([edge, id_row, edge])
    before = sum((padded[READ_ROWS - k:READ_ROWS - k + count] == id_row).astype(jnp.int32) for k in range(1, READ_ROWS + 1))
    behind = sum((padded[READ_ROWS + k:READ_ROWS + k + count] == id_row).astype(jnp.int32) for k in range(1, READ_ROWS + 1))
    return jnp.where(before < READ_ROWS, before, jnp.where(behind < READ_ROWS, 2 * READ_ROWS - 1 - behind, -1))


def on_device(dps, seqs, tokens, doc_ids, memory, qkv_weight, query_bias, value_bias, out_weight, out_bias, norm1_gain, norm1_bias, up_weight, up_bias, down_weight, down_bias, norm2_gain, norm2_bias, out_grad):
    rows = tokens.shape[1]
    width = qkv_weight.shape[2]
    heads = width // HEAD_DIM
    bq, bk = rows, 256
    own = REACH * rows
    pieces = 2 * REACH + 1
    s = lax.axis_index("seq")
    id_row = doc_ids[0]
    edge = jnp.full((own,), -1, jnp.int32)
    slots = memory_slots(id_row)
    window_slots = lax.dynamic_slice_in_dim(jnp.concatenate([edge, slots, edge]), s * rows, pieces * rows, 0)
    window_ids = lax.dynamic_slice_in_dim(jnp.concatenate([edge, id_row, jnp.full((own,), 1 << 20, jnp.int32)]), s * rows, pieces * rows, 0)
    ids = jnp.broadcast_to(window_ids.astype(F32)[None], (8, pieces * rows))

    out_other = lax.ppermute(out_weight, "tensor", [(0, 1), (1, 0)])
    weight = qkv_weight.transpose(1, 0, 2)
    slots_row = jnp.broadcast_to(window_slots[None], (8, pieces * rows))
    memory_pad = jnp.pad(memory, ((0, 32 - memory.shape[0]), (0, 0)))
    query, key, value, source = project_window(
        tokens[0], slots_row, memory_pad, weight, query_bias, value_bias, seqs, 1)
    own_slots = window_slots[own:own + rows]

    mixed_low, logsums = attention_forward(query, key, value, ids, rows, own, bq, bk)

    vectors = (out_bias, norm1_gain, norm1_bias, down_bias, norm2_gain, norm2_bias, up_bias)
    *shares, output, grad_input1, branch_grad, mixed_grad, small = feed_forward(
        mixed_low, out_weight, out_other, source, up_weight, down_weight, vectors, out_grad[0], dps, seqs)
    early = shares[:1] + [
        lax.ppermute(shares[k], "dp", [(i, (i + k) % dps) for i in range(dps)]) for k in range(1, dps)]
    grads_window, stats_window, along_cols, grad_out_weight = gather_grads(mixed_grad, mixed_low, logsums, branch_grad, seqs, 2)
    proj_grad = attention_backward(query, key, value, grads_window, ids, logsums, along_cols, stats_window, rows, own, bq, bk)

    select = (own_slots[:, None] == jnp.arange(32, dtype=jnp.int32)[None, :]).astype(BF16)
    up_sum, down_sum, out_sum, qkv_sum, input_grad, small = tail(
        early, grad_out_weight, proj_grad, source, weight, grad_input1, select, small, dps, seqs)
    small = small.reshape(32, 2 * width)
    input_grad = input_grad[None]
    piece = small.shape[1] // seqs
    vectors = lax.dynamic_slice_in_dim(small[:6], s * piece, piece, 1)
    memory_grad = small[9:29]
    return (
        output[None], input_grad, memory_grad,
        qkv_sum.transpose(1, 0, 2), small[8, :width], small[8, width:],
        out_sum, vectors[4], vectors[0], vectors[1],
        up_sum, small[6:8].reshape(-1), down_sum, vectors[5], vectors[2], vectors[3],
    )


def solution(mesh):
    in_specs = (
        P("dp", "seq", None), P("dp", None), P(), P(None, None, "tensor"), P("tensor"), P("tensor"), P(None, "tensor"), P(), P(), P(),
        P(None, "tensor"), P("tensor"), P(None, "tensor"), P(), P(), P(), P("dp", "seq", None),
    )
    out_specs = (
        P("dp", "seq", None), P("dp", "seq", None), P(), P("seq", None, "tensor"), P("tensor"), P("tensor"), P("seq", "tensor"), P("seq"), P("seq"), P("seq"),
        P("seq", "tensor"), P("tensor"), P("seq", "tensor"), P("seq"), P("seq"), P("seq"),
    )
    step = functools.partial(on_device, mesh.shape["dp"], mesh.shape["seq"])
    return jax.shard_map(step, mesh=mesh, in_specs=in_specs, out_specs=out_specs, check_vma=False)
```

```python
import functools

import jax
import jax.numpy as jnp
from jax import lax
from jax.experimental import pallas as pl
from jax.experimental.pallas import tpu as pltpu
from jax.sharding import PartitionSpec as P

HEAD_DIM = 64
READ_ROWS = 10
REACH = 3
NORM_EPS = 1e-05
OWNERS = 4
F32, BF16 = jnp.float32, jnp.bfloat16
NT = (((1,), (1,)), ((), ()))
NN = (((1,), (0,)), ((), ()))
NEG = -1e30
FLOOR = -1e29
VMEM = pl.BlockSpec(memory_space=pltpu.VMEM)
HBM = pl.BlockSpec(memory_space=pltpu.HBM)


def remote(source, target, send_sem, recv_sem, **where):
    return pltpu.make_async_remote_copy(
        source, target, send_sem, recv_sem, device_id=where, device_id_type=pl.DeviceIdType.MESH
    )


def greet(partners):
    barrier = pltpu.get_barrier_semaphore()
    total = 0
    for present, where in partners:
        total = total + present.astype(jnp.int32)

        @pl.when(present)
        def _():
            pl.semaphore_signal(barrier, inc=1, device_id=where, device_id_type=pl.DeviceIdType.MESH)

    pl.semaphore_wait(barrier, total)


def dot(a, b, dims=NN):
    return lax.dot_general(a, b, dims, preferred_element_type=F32)

def low_half(shape):
    return lax.broadcasted_iota(jnp.int32, shape, len(shape) - 1) < 64

def id_columns(ids_ref, start, count):
    row = jnp.broadcast_to(ids_ref[0:1, pl.ds(start, count)], (128, count))
    return jnp.transpose(row)

def wide(x, count):
    return jnp.concatenate([x] * (count // 128), axis=1)

def split_heads(source_ref, rows, target_ref, pairs, keep):
    for pair in range(pairs):
        block = source_ref[rows, pair * 128:pair * 128 + 128]
        target_ref[2 * pair] = jnp.where(keep, block, jnp.zeros_like(block))
        target_ref[2 * pair + 1] = jnp.where(keep, jnp.zeros_like(block), block)

def document_range(ids_ref, start, count, bk):
    mine, every = ids_ref[0:1, pl.ds(start, count)], ids_ref[0:1, :]
    low, high = jnp.min(mine), jnp.max(mine)
    begin = jnp.sum(jnp.where(every < low, 1.0, 0.0)).astype(jnp.int32)
    end = jnp.sum(jnp.where(every <= high, 1.0, 0.0)).astype(jnp.int32)
    shift = bk.bit_length() - 1
    first, last = begin >> shift, (end + bk - 1) >> shift
    full_first, full_last = (begin + bk - 1) >> shift, end >> shift
    whole = jnp.logical_and(low == high, full_first < full_last)
    return first, jnp.where(whole, full_first, first), jnp.where(whole, full_last, first), last


def sweep(span, body):
    first, full_first, full_last, last = span
    lax.fori_loop(full_first, full_last, lambda j, c: body(j, False, c), 0)

    def edge(i, c):
        j = first + i
        return body(jnp.where(j < full_first, j, j + full_last - full_first), True, c)

    lax.fori_loop(0, last - first - (full_last - full_first), edge, 0)

def fwd_kernel(bq, bk, own, q_ref, k_ref, v_ref, ids_ref, o_ref, lse_ref, acc_ref, max_ref, q_heads, cols_ref):
    pairs = q_ref.shape[1] // 128
    rows = o_ref.shape[0]
    low_q, low_k = low_half((bq, 128)), low_half((bk, 128))

    def block(qb, carry):
        mine = pl.ds(pl.multiple_of(qb * bq, bq), bq)
        cols_ref[...] = id_columns(ids_ref, pl.multiple_of(own + qb * bq, bq), bq)
        split_heads(q_ref, pl.ds(pl.multiple_of(own + qb * bq, bq), bq), q_heads, pairs, low_q)
        acc_ref[...] = jnp.zeros_like(acc_ref)
        max_ref[...] = jnp.full_like(max_ref, FLOOR)

        def step(j, masked, carry):
            there = pl.ds(pl.multiple_of(j * bk, bk), bk)
            def pair_step(pair, carry):
                lanes = pl.ds(pair * 128, 128)
                key = k_ref[there, lanes]
                value = v_ref[there, lanes]
                for odd in range(2):
                    head = 2 * pair + odd
                    scores = dot(q_heads[head], key, NT)
                    if masked:
                        scores = jnp.where(wide(cols_ref[...], bk) == ids_ref[0:1, there], scores, NEG)
                    old = max_ref[head]
                    new = jnp.maximum(old, jnp.max(scores, axis=1, keepdims=True))
                    probs = jnp.exp(scores - wide(new, bk)).astype(BF16)
                    ones = jnp.where(low_k if odd == 0 else ~low_k, value, jnp.ones_like(value))
                    acc_ref[head] = acc_ref[head] * jnp.exp(old - new) + dot(probs, ones)
                    max_ref[head] = new
                return carry
            for pair in range(pairs):
                pair_step(pair, carry)
            return carry

        sweep(document_range(ids_ref, pl.multiple_of(own + qb * bq, bq), bq, bk), step)
        stats = jnp.zeros((bq, 128), F32)
        lane = lax.broadcasted_iota(jnp.int32, (bq, 128), 1)
        for pair in range(pairs):
            even, odd = acc_ref[2 * pair], acc_ref[2 * pair + 1]
            total_even, total_odd = even[:, 64:65], odd[:, 0:1]
            mixed = jnp.where(low_q, even / total_even, odd / total_odd)
            o_ref[mine, pair * 128:pair * 128 + 128] = mixed.astype(BF16)
            stats = jnp.where(lane == 2 * pair, max_ref[2 * pair] + jnp.log(total_even), stats)
            stats = jnp.where(lane == 2 * pair + 1, max_ref[2 * pair + 1] + jnp.log(total_odd), stats)
        lse_ref[mine, :] = stats
        return carry

    lax.fori_loop(0, rows // bq, block, 0)

def attention_forward(query, key, value, ids, rows, own, bq=256, bk=256):
    width = query.shape[1]
    heads = width // 64
    return pl.pallas_call(
        functools.partial(fwd_kernel, bq, bk, own),
        out_shape=(jax.ShapeDtypeStruct((rows, width), BF16), jax.ShapeDtypeStruct((rows, 128), F32)),
        in_specs=[VMEM] * 4,
        out_specs=(pl.BlockSpec(memory_space=pltpu.VMEM),) * 2,
        scratch_shapes=[pltpu.VMEM((heads, bq, 128), F32), pltpu.VMEM((heads, bq, 128), F32), pltpu.VMEM((heads, bq, 128), BF16), pltpu.VMEM((bq, 128), F32)],
        compiler_params=pltpu.CompilerParams(vmem_limit_bytes=24 << 20),
        name="attention_forward",
    )(query, key, value, ids)

def bwd_kernel(bk, own, q_hbm, k_hbm, v_hbm, g_hbm, ids_ref, lse_ref, along_ref, rows_ref, out_ref, q_ref, k_ref, v_ref, g_ref, sems, dq_acc, dk_acc, dv_acc, q_heads, k_heads, v_heads, g_heads, lse_cols, along_cols, cols_ref):
    bq, width = out_ref.shape[0], q_ref.shape[1]
    pairs = width // 128
    heads = 2 * pairs
    low_q = low_half((bq, 128))

    blocks = document_range(ids_ref, own, bq, bk)
    first_own, last_own = own // bk, (own + bq) // bk

    def copies(j):
        there = pl.ds(pl.multiple_of(j * bk, bk), bk)
        pairs_of = ((q_hbm, q_ref), (k_hbm, k_ref), (v_hbm, v_ref), (g_hbm, g_ref))
        return [pltpu.make_async_copy(source.at[there], target.at[there], sems.at[i, j]) for i, (source, target) in enumerate(pairs_of)]

    def start_all(j, carry):
        @pl.when(jnp.logical_or(j < first_own, j >= last_own))
        def _():
            for copy in copies(j):
                copy.start()

        return carry

    for j in range(first_own, last_own):
        for copy in copies(j):
            copy.start()
    lax.fori_loop(blocks[0], blocks[3], start_all, 0)
    mine, here = pl.ds(0, bq), pl.ds(own, bq)
    cols_ref[...] = id_columns(ids_ref, own, bq)
    for acc in (dq_acc, dk_acc, dv_acc):
        acc[...] = jnp.zeros_like(acc)
    for head in range(heads):
        lse_cols[head] = jnp.broadcast_to(lse_ref[mine, head:head + 1], (bq, 128))
        along_cols[head] = jnp.broadcast_to(along_ref[mine, head:head + 1], (bq, 128))
    for j in range(first_own, last_own):
        for copy in copies(j):
            copy.wait()
    for source, target in ((q_ref, q_heads), (k_ref, k_heads), (v_ref, v_heads), (g_ref, g_heads)):
        split_heads(source, here, target, pairs, low_q)

    def step(j, masked, carry):
        there = pl.ds(pl.multiple_of(j * bk, bk), bk)

        @pl.when(jnp.logical_or(j < first_own, j >= last_own))
        def _():
            for copy in copies(j):
                copy.wait()

        def pair_step(pair, carry):
            lanes = pl.ds(pair * 128, 128)
            q_far, k_far, v_far, g_far = (r[there, lanes] for r in (q_ref, k_ref, v_ref, g_ref))
            def hide(x):
                return jnp.where(wide(cols_ref[...], bk) == ids_ref[0:1, there], x, 0.0) if masked else x
            for odd in range(2):
                head = 2 * pair + odd
                scores = dot(q_heads[head], k_far, NT)
                probs = hide(jnp.exp(scores - wide(lse_cols[head], bk)))
                slope = dot(g_heads[head], v_far, NT)
                grad = (probs * (slope - wide(along_cols[head], bk))).astype(BF16)
                dq_acc[head] += dot(grad, k_far)
                scores = dot(k_heads[head], q_far, NT)
                probs = hide(jnp.exp(scores - rows_ref[pl.ds(head, 1), there]))
                slope = dot(v_heads[head], g_far, NT)
                grad = (probs * (slope - rows_ref[pl.ds(8 + head, 1), there])).astype(BF16)
                dv_acc[head] += dot(probs.astype(BF16), g_far)
                dk_acc[head] += dot(grad, q_far)
            return carry
        for pair in range(pairs):
            pair_step(pair, carry)
        return carry

    sweep(blocks, step)
    for which, (acc, factor) in enumerate(((dq_acc, 0.125), (dk_acc, 1.0), (dv_acc, 1.0))):
        for pair in range(pairs):
            both = jnp.where(low_q, acc[2 * pair], acc[2 * pair + 1]) * factor
            out_ref[mine, which * width + pair * 128:which * width + pair * 128 + 128] = both.astype(BF16)

def attention_backward(query, key, value, grads, ids, lse, along, stat_rows, rows, own, bk=256):
    width = query.shape[1]
    heads, bq = width // 64, rows
    return pl.pallas_call(
        functools.partial(bwd_kernel, bk, own),
        out_shape=jax.ShapeDtypeStruct((rows, 3 * width), BF16),
        in_specs=[HBM] * 4 + [VMEM] * 4,
        out_specs=pl.BlockSpec(memory_space=pltpu.VMEM),
        scratch_shapes=[pltpu.VMEM(query.shape, BF16)] * 4 + [pltpu.SemaphoreType.DMA((4, query.shape[0] // bk))] + [pltpu.VMEM((heads, bq, 128), F32)] * 3 + [pltpu.VMEM((heads, bq, 128), BF16)] * 4 + [pltpu.VMEM((heads, bq, 128), F32)] * 2 + [pltpu.VMEM((bq, 128), F32)],
        compiler_params=pltpu.CompilerParams(vmem_limit_bytes=60 << 20),
        name="attention_backward",
    )(query, key, value, grads, ids, lse, along, stat_rows)

class Halo:
    def __init__(self, count, pieces, send_sem, recv_sem):
        self.count, self.pieces, self.send_sem, self.recv_sem = count, pieces, send_sem, recv_sem
        s = self.s = lax.axis_index("seq")
        self.core = lax.rem(s, 2)
        self.sibling = s + 1 - 2 * self.core
        self.left, self.right = s >= 2, s < count - 2

    def neighbours(self):
        s, count = self.s, self.count
        return [(s >= k, {"seq": s - k}) for k in (1, 2)] + [(s < count - k, {"seq": s + k}) for k in (1, 2)]

    def own(self, part, kind, slot, target):
        source, window = self.pieces[part]
        return remote(source, window(slot), self.send_sem.at[kind, part], self.recv_sem.at[slot, part], seq=target)

    def moved(self, part, kind, held, slot, target):
        window = self.pieces[part][1]
        return remote(window(held), window(slot), self.send_sem.at[kind, part], self.recv_sem.at[slot, part], seq=target)

    def first_copies(self, part):
        s, core = self.s, self.core
        return (
            (self.right, self.own(part, 0, 1, s + 2)),
            (self.left, self.own(part, 1, 5, s - 2)),
            (core == 0, self.own(part, 2, 2, self.sibling)),
            (core == 1, self.own(part, 2, 4, self.sibling)),
        )

    def from_left(self, part):
        s, core, left, right = self.s, self.core, self.left, self.right
        return (
            (jnp.logical_and(left, jnp.logical_and(core == 1, right)), self.moved(part, 3, 1, 0, s + 1)),
            (jnp.logical_and(left, core == 0), self.moved(part, 4, 1, 0, self.sibling)),
            (jnp.logical_and(left, core == 1), self.moved(part, 4, 1, 2, self.sibling)),
        )

    def from_right(self, part):
        s, core, left, right = self.s, self.core, self.left, self.right
        return (
            (jnp.logical_and(right, jnp.logical_and(core == 0, left)), self.moved(part, 5, 5, 6, s - 1)),
            (jnp.logical_and(right, core == 0), self.moved(part, 6, 5, 4, self.sibling)),
            (jnp.logical_and(right, core == 1), self.moved(part, 6, 5, 6, self.sibling)),
        )

    def each(self, copies, act):
        for present, copy in copies:
            pl.when(present)(functools.partial(act, copy))

    def send(self, part):
        self.each(self.first_copies(part), lambda copy: copy.start())

    def arrived(self, slot, part):
        self.own(part, 0, slot, self.s).wait_recv()

    def relay(self, part):
        pl.when(self.left)(functools.partial(self.arrived, 1, part))
        self.each(self.from_left(part), lambda copy: copy.start())
        pl.when(self.right)(functools.partial(self.arrived, 5, part))
        self.each(self.from_right(part), lambda copy: copy.start())

    def present(self, slot):
        block = self.s + slot - REACH
        return jnp.logical_and(block >= 0, block < self.count)

    def receive(self, slot):
        for part in range(len(self.pieces)):
            pl.when(self.present(slot))(functools.partial(self.arrived, slot, part))

    def finish(self):
        for part in range(len(self.pieces)):
            self.each(self.first_copies(part) + self.from_left(part) + self.from_right(part), lambda copy: copy.wait_send())


def project_kernel(count, parts, own_ref, slots_ref, memory_ref, weight_ref, query_bias_ref, value_bias_ref,
                   q_ref, k_ref, v_ref, source_ref, window_ref, weight, table, send_sem, recv_sem, local_sem):
    block = own_ref.shape[0]
    rows = block // parts
    tile = 256
    tiles = block // tile

    def piece(part):
        return own_ref.at[pl.ds(part * rows, rows)], lambda slot: window_ref.at[pl.ds(slot * block + part * rows, rows)]

    halo = Halo(count, [piece(part) for part in range(parts)], send_sem, recv_sem)
    greet(halo.neighbours())
    for part in range(parts):
        halo.send(part)
    local = [
        pltpu.make_async_copy(own_ref, window_ref.at[pl.ds(REACH * block, block)], local_sem.at[0]),
        pltpu.make_async_copy(weight_ref, weight, local_sem.at[1]),
    ]
    for copy in local:
        copy.start()
    table[...] = jnp.zeros_like(table)
    table[0:memory_ref.shape[0], :] = memory_ref[...]
    query_bias, value_bias = query_bias_ref[...].reshape(1, -1), value_bias_ref[...].reshape(1, -1)

    def project(load, start, keep):
        hot = (lax.broadcasted_iota(jnp.int32, (32, tile), 0) == slots_ref[0:1, pl.ds(start, tile)]).astype(F32).astype(BF16)
        tn = (((0,), (0,)), ((), ()))
        chosen = dot(hot, table[...], tn)
        inside = wide(dot(hot, jnp.ones((32, 128), BF16), tn), chosen.shape[1])
        source = jnp.where(inside > 0.5, chosen, load().astype(F32)).astype(BF16)
        keep(source)
        out = pl.ds(start, tile)
        q_ref[out, :] = (dot(source, weight[0]) + query_bias).astype(BF16) * 0.125
        k_ref[out, :] = dot(source, weight[1]).astype(BF16)
        v_ref[out, :] = (dot(source, weight[2]) + value_bias).astype(BF16)

    def own_tile(i, carry):
        at = pl.ds(pl.multiple_of(i * tile, tile), tile)

        def keep(source):
            source_ref[at, :] = source

        start = pl.multiple_of(REACH * block + i * tile, tile)
        project(lambda: window_ref[pl.ds(start, tile), :], start, keep)
        return carry

    for copy in local:
        copy.wait()
    lax.fori_loop(0, tiles, own_tile, 0)
    for part in range(parts):
        halo.relay(part)

    def two_blocks(low, high):
        def step(i, carry):
            slot = low + (high - low) * (i // tiles)

            @pl.when(halo.present(slot))
            def _():
                start = pl.multiple_of(slot * block + lax.rem(i, tiles) * tile, tile)
                project(lambda: window_ref[pl.ds(start, tile), :], start, lambda source: None)

            return carry

        lax.fori_loop(0, 2 * tiles, step, 0)

    two_blocks(1, 5)
    for slots in ((2, 4), (0, 6)):
        for slot in slots:
            halo.receive(slot)
        two_blocks(*slots)
    halo.finish()


def project_window(own, slots, memory, weight, query_bias, value_bias, count, collective_id, parts=2):
    rows, dim = own.shape
    width = weight.shape[2]
    total = (2 * REACH + 1) * rows
    wide_out = jax.ShapeDtypeStruct((total, width), BF16)
    return pl.pallas_call(
        functools.partial(project_kernel, count, parts),
        out_shape=(wide_out, wide_out, wide_out, jax.ShapeDtypeStruct((rows, dim), BF16)),
        in_specs=[HBM, VMEM, VMEM, HBM, VMEM, VMEM],
        out_specs=(VMEM,) * 4,
        scratch_shapes=[
            pltpu.VMEM((total, dim), BF16),
            pltpu.VMEM(weight.shape, BF16),
            pltpu.VMEM((32, dim), BF16),
            pltpu.SemaphoreType.DMA((7, parts)),
            pltpu.SemaphoreType.DMA((7, parts)),
            pltpu.SemaphoreType.DMA((2,)),
        ],
        compiler_params=pltpu.CompilerParams(collective_id=collective_id, has_side_effects=True, vmem_limit_bytes=40 << 20),
        name="project_window",
    )(own, slots, memory, weight, query_bias, value_bias)


def split_dot(left, right, dims):
    high = right.astype(BF16)
    low = (right - high.astype(F32)).astype(BF16)
    return dot(left, high, dims) + dot(left, low, dims)


def tail_kernel(dps, seqs, width, *refs):
    (early_refs, (out_grad_ref, proj_ref, source_ref, weight_ref, input1_ref, select_ref, small_ref),
     (up_out, down_out, out_out, qkv_out, input_out, small_out),
     (mix, y_send, y_recv, a_recv, parts, b_recv, small_in, small_recv, small_mine, small_dp),
     (mine, c_recv, last, d_recv), (y_sems, a_sems, b_sems, c_sems, d_sems, s_sems)) = (
        refs[:dps], refs[dps:dps + 7], refs[dps + 7:dps + 13], refs[dps + 13:dps + 23], refs[dps + 23:dps + 27], refs[dps + 27:])
    zs = seqs // 2
    bits = zs.bit_length() - 1
    t, d, s = lax.axis_index("tensor"), lax.axis_index("dp"), lax.axis_index("seq")
    z, core = s // 2, lax.rem(s, 2)
    sibling = s + 1 - 2 * core
    late, early = a_recv.shape[0], mine.shape[0] - a_recv.shape[0]
    chunk = a_recv.shape[3]
    shares = -(-chunk // width)
    owners = small_out.shape[0]
    block, hidden = up_out.shape
    share_width = early * width
    rows, columns = proj_ref.shape
    third = columns // 3
    steps = y_send.shape[0]
    span = rows // steps
    true = s >= 0
    partners = [(true, {"seq": lax.rem(s + k, seqs)}) for k in range(1, seqs)]
    partners += [(true, {"dp": lax.rem(d + k, dps)}) for k in range(1, dps)]
    partners += [(true, {"tensor": 1 - t})]
    greet(partners)

    def active(c):
        return true if c < early else d < shares

    def a_copy(c, j):
        start = pl.multiple_of((2 * j + 1 - core) * block, 16)
        at = (c - early) * chunk
        i = c - early
        return remote(mix.at[pl.ds(start, block), pl.ds(at, chunk)], a_recv.at[i, j], a_sems.at[0, i, j], a_sems.at[1, i, j], seq=sibling)

    def b_copy(c, k):
        other = lax.rem(d + k, dps)
        i = c - early
        return other, remote(parts.at[i, other], b_recv.at[i, k], b_sems.at[0, i, k], b_sems.at[1, i, k], dp=other)

    def first_slot(b):
        return sum(zs // (2 << e) for e in range(b))

    def c_copies(c, b):
        size = 2 << b
        high = lax.rem(z // (1 << b), 2)
        partner = z + (1 << b) - (size * high)
        low = lax.rem(partner, size)
        return [
            remote(mine.at[c, i * size + low], c_recv.at[c, first_slot(b) + i], c_sems.at[0, c, first_slot(b) + i], c_sems.at[1, c, first_slot(b) + i], seq=2 * partner + core)
            for i in range(zs // size)
        ]

    def d_copy(c, k):
        return remote(last.at[c], d_recv.at[c, k], d_sems.at[0, c, k], d_sems.at[1, c, k], dp=lax.rem(d + k, dps))

    def start_a(c):
        for j in range(zs):
            a_copy(c, j).start()

    def start_early(c):
        lanes = slice(c * width, c * width + width)
        for j in range(zs):
            total = early_refs[0][j, :, lanes].astype(F32)
            for k in range(1, dps):
                total = total + early_refs[k][j, :, lanes].astype(F32)
            mine[c, j] = total.astype(BF16)
        for copy in c_copies(c, 0):
            copy.start()

    def end_a(c):
        i = c - early
        for j in range(zs):
            a_copy(c, j).wait()
            start = pl.multiple_of((2 * j + core) * block, 16)
            for p in range(shares):
                real = min(width, chunk - p * width)
                lanes = pl.ds(i * chunk + p * width, real)
                total = mix[pl.ds(start, block), lanes].astype(F32) + a_recv[i, j, :, p * width:p * width + real].astype(F32)
                parts[i, p, j, :, 0:real] = total.astype(BF16)
                if real < width:
                    parts[i, p, j, :, real:width] = jnp.zeros((block, width - real), BF16)
        for k in range(1, dps):
            other, copy = b_copy(c, k)
            pl.when(other < shares)(copy.start)

    def end_b(c):
        i = c - early
        for k in range(1, dps):
            other, copy = b_copy(c, k)
            pl.when(other < shares)(copy.wait_send)

        @pl.when(d < shares)
        def _():
            for k in range(1, dps):
                b_copy(c, k)[1].wait_recv()
            for j in range(zs):
                total = parts[i, d, j].astype(F32)
                for k in range(1, dps):
                    total = total + b_recv[i, k, j].astype(F32)
                mine[c, j] = total.astype(BF16)
            for copy in c_copies(c, 0):
                copy.start()

    def end_c(c, b):
        size = 2 << b
        kept = lax.rem(z, size)

        @pl.when(active(c))
        def _():
            for i, copy in enumerate(c_copies(c, b)):
                copy.wait()
                held = mine[c, i * size + kept].astype(F32) + c_recv[c, first_slot(b) + i].astype(F32)
                if b < bits - 1:
                    mine[c, i * size + kept] = held.astype(BF16)
                else:
                    last[c] = held.astype(BF16)
            if b < bits - 1:
                for copy in c_copies(c, b + 1):
                    copy.start()
            else:
                for k in range(1, dps):
                    d_copy(c, k).start()

    def put(c, share, value):
        count = dps if c < early else shares
        for p in range(count):

            @pl.when(share == p)
            def _():
                if c < early:
                    which, column = divmod(p * share_width + c * width, hidden)
                    (up_out, down_out)[which][:, column:column + width] = value.astype(F32)
                    return
                first = (c - early) * chunk + p * width
                for lane in range(0, min(width, chunk - p * width), 128):
                    which, column = divmod(first + lane, third)
                    part = value[:, lane:lane + 128].astype(F32)
                    if which == 0:
                        out_out[:, column:column + 128] = part
                    else:
                        qkv_out[which - 1, :, column:column + 128] = part

    def end_d(c):
        @pl.when(active(c))
        def _():
            put(c, d, last[c])
            for k in range(1, dps):
                d_copy(c, k).wait_send()

        for k in range(1, dps):
            share = lax.rem(d + dps - k, dps)

            @pl.when(true if c < early else share < shares)
            def _():
                d_copy(c, k).wait_recv()
                put(c, share, d_recv[c, k])

    def y_copy(i):
        return remote(y_send.at[i], y_recv.at[i], y_sems.at[0, i], y_sems.at[1, i], tensor=1 - t)

    for c in range(early):
        start_early(c)
    out_width = out_grad_ref.shape[1]
    mix[:, 0:out_width] = out_grad_ref[...]
    for i in range(3):
        part = lax.dot_general(source_ref[...], proj_ref[:, i * third:(i + 1) * third], (((0,), (0,)), ((), ())), preferred_element_type=F32)
        mix[:, out_width + i * third:out_width + (i + 1) * third] = part.astype(BF16)
    for c in range(early, early + late):
        start_a(c)
    for i in range(steps):
        at = slice(i * span, (i + 1) * span)
        y_send[i] = sum(dot(proj_ref[at, j * third:(j + 1) * third], weight_ref[j], NT) for j in range(3)).astype(BF16)
        y_copy(i).start()
    small_in[0] = small_ref[...]
    for i in range(1, owners):
        small_in[i] = jnp.zeros_like(small_ref)
    small_in[1, 0:1, 0:third] = jnp.sum(proj_ref[:, 0:third].astype(F32), axis=0, keepdims=True)
    small_in[1, 0:1, third:2 * third] = jnp.sum(proj_ref[:, 2 * third:3 * third].astype(F32), axis=0, keepdims=True)

    def end_y():
        memory = jnp.zeros((32, input_out.shape[1]), F32)
        for i in range(steps):
            y_copy(i).wait()
            at = slice(i * span, (i + 1) * span)
            total = input1_ref[at, :] + (y_send[i].astype(F32) + y_recv[i].astype(F32))
            select = select_ref[at, :]
            memory = memory + split_dot(select, total, (((0,), (0,)), ((), ())))
            inside = dot(select, jnp.ones((32, total.shape[1]), BF16))
            input_out[at, :] = jnp.where(inside > 0.5, 0.0, total).astype(BF16)
        small_in[1, 1:8, :] = memory[0:7]
        small_in[2] = memory[7:15]
        small_in[3, 0:5, :] = memory[15:20]
        for hop in range(1, seqs):
            owner = lax.rem(s + hop, seqs)
            pl.when(owner < owners)(to_owner(hop, owner).start)

    def to_owner(hop, owner):
        return remote(small_in.at[owner], small_recv.at[hop], s_sems.at[0, 0, hop], s_sems.at[1, 0, hop], seq=owner)

    def across(k):
        return remote(small_mine, small_dp.at[k], s_sems.at[0, 1, k], s_sems.at[1, 1, k], dp=lax.rem(d + k, dps))

    def back(hop, owner, target):
        return remote(small_out.at[owner], small_out.at[owner], s_sems.at[0, 2, hop], s_sems.at[1, 2, hop], seq=target)

    def small_one():
        @pl.when(s < owners)
        def _():
            total = small_in[s]
            for hop in range(1, seqs):
                to_owner(hop, s).wait_recv()
                total = total + small_recv[hop]
            small_mine[...] = total
            for k in range(1, dps):
                across(k).start()

    def small_two():
        @pl.when(s < owners)
        def _():
            small_dp[0] = small_mine[...]
            for k in range(1, dps):
                across(k).wait()
            ordered = jnp.zeros(small_mine.shape, F32)
            for index in range(dps):
                ordered = ordered + small_dp[lax.rem(d + dps - index, dps)]
            small_out[s] = ordered
            for hop in range(1, seqs):
                back(hop, s, lax.rem(s + hop, seqs)).start()

    def small_three():
        for hop in range(1, seqs):
            owner = lax.rem(s + hop, seqs)
            pl.when(owner < owners)(to_owner(hop, owner).wait_send)
        for hop in range(1, seqs):
            pl.when(lax.rem(s + seqs - hop, seqs) < owners)(back(hop, 0, s).wait_recv)
            pl.when(s < owners)(back(hop, 0, s).wait_send)

    zed = [functools.partial(end_c, b=b) for b in range(bits)]
    lates = list(range(early, early + late))
    for c in lates:
        end_a(c)
    for c in range(early):
        zed[0](c)
    for c in lates:
        end_b(c)
    end_y()
    for b in range(1, bits):
        for c in range(early):
            zed[b](c)
        for c in lates:
            zed[b - 1](c)
        if b == 1:
            small_one()
    for c in range(early):
        end_d(c)
    small_two()
    for c in lates:
        zed[bits - 1](c)
    for c in lates:
        end_d(c)
    small_three()


def tail(early, out, proj, source, weight, input1, select, small, dps, seqs):
    zs = seqs // 2
    dim = source.shape[1]
    hidden = early[0].shape[2] * dps // 2
    rows = proj.shape[0]
    block = dim // seqs
    mixed = out.shape[1] + proj.shape[1]
    late = 2
    chunk = mixed // late
    width = -(-chunk // (128 * dps)) * 128
    width = early[0].shape[2] if early[0].shape[2] % width else width
    chunks = early[0].shape[2] // width + late
    steps = 4
    table = (OWNERS,) + small.shape
    dma = pltpu.SemaphoreType.DMA
    return pl.pallas_call(
        functools.partial(tail_kernel, dps, seqs, width),
        out_shape=(
            jax.ShapeDtypeStruct((block, hidden), F32),
            jax.ShapeDtypeStruct((block, hidden), F32),
            jax.ShapeDtypeStruct((block, out.shape[1]), F32),
            jax.ShapeDtypeStruct((3, block, out.shape[1]), F32),
            jax.ShapeDtypeStruct((rows, dim), BF16),
            jax.ShapeDtypeStruct(table, F32),
        ),
        in_specs=[VMEM] * (dps + 7),
        out_specs=(VMEM,) * 6,
        scratch_shapes=[
            pltpu.VMEM((dim, mixed), BF16),
            pltpu.VMEM((steps, rows // steps, dim), BF16),
            pltpu.VMEM((steps, rows // steps, dim), BF16),
            pltpu.VMEM((late, zs, block, chunk), BF16),
            pltpu.VMEM((late, dps, zs, block, width), BF16),
            pltpu.VMEM((late, dps, zs, block, width), BF16),
            pltpu.VMEM(table, F32),
            pltpu.VMEM((seqs,) + small.shape, F32),
            pltpu.VMEM(small.shape, F32),
            pltpu.VMEM((dps,) + small.shape, F32),
            pltpu.VMEM((chunks, zs, block, width), BF16),
            pltpu.VMEM((chunks, zs - 1, block, width), BF16),
            pltpu.VMEM((chunks, block, width), BF16),
            pltpu.VMEM((chunks, dps, block, width), BF16),
            dma((2, steps)),
            dma((2, late, zs)),
            dma((2, late, dps)),
            dma((2, chunks, zs)),
            dma((2, chunks, dps)),
            dma((2, 3, max(seqs, dps))),
        ],
        compiler_params=pltpu.CompilerParams(collective_id=7, has_side_effects=True, vmem_limit_bytes=48 << 20),
        name="tail",
    )(*early, out, proj, source, weight, input1, select, small)


def feed_kernel(dps, seqs, span, *refs):
    feed_body(dps, seqs, span, *refs[:8], refs[8:15], refs[15:15 + dps], *refs[15 + dps:])


def feed_body(dps, seqs, span, mixed_ref, out_ref, other_ref, source_ref, up_hbm, down_hbm, grad_ref, lse_ref, vectors, share_refs,
                y_ref, input1_ref, window_ref, stats_ref, along_ref, out_grad_ref, small_ref,
                low_ref, own_stats, h_send, h_recv,
                up_ref, down_ref, w_sems, out_all, mixed_all, first_ref, hat_ref, scale_ref, first_low, act_ref, slope_ref, second_ref, down_grad, up_grad,
                y_send, y_recv, z_send, z_recv, grads, a_recv, m_sems, y_sems, z_sems, a_sems):
    rows, dim = source_ref.shape
    width, hidden = mixed_ref.shape[1], up_ref.shape[1]
    zs, block = seqs // 2, dim // seqs
    t, d, s = lax.axis_index("tensor"), lax.axis_index("dp"), lax.axis_index("seq")
    core = lax.rem(s, 2)
    sibling = s + 1 - 2 * core
    spans = rows // span
    true = s >= 0

    def piece(part):
        return window_ref.at[pl.ds(REACH * rows + part * span, span)], lambda slot: window_ref.at[pl.ds(slot * rows + part * span, span)]

    stats_piece = own_stats, lambda slot: stats_ref.at[:, pl.ds(slot * rows, rows)]
    halo = Halo(seqs, [piece(part) for part in range(spans)] + [stats_piece], h_send, h_recv)
    greet([(true, {"tensor": 1 - t})] + halo.neighbours())
    tn = (((0,), (0,)), ((), ()))

    def at(i):
        return pl.ds(pl.multiple_of(i * span, span), span)

    mine = pl.ds(pl.multiple_of(t * width, 128), width)
    theirs = pl.ds(pl.multiple_of((1 - t) * width, 128), width)

    def m_copy(i):
        return remote(mixed_ref.at[at(i)], mixed_all.at[at(i), mine], m_sems.at[0, i], m_sems.at[1, i], tensor=1 - t)

    def y_copy(i):
        return remote(y_send.at[at(i)], y_recv.at[at(i)], y_sems.at[0, i], y_sems.at[1, i], tensor=1 - t)

    def z_copy(i):
        return remote(z_send.at[at(i)], z_recv.at[at(i)], z_sems.at[0, i], z_sems.at[1, i], tensor=1 - t)

    def a_copy(which, j):
        start = pl.multiple_of((2 * j + 1 - core) * block, 16)
        return remote(grads.at[which, pl.ds(start, block)], a_recv.at[which, j], a_sems.at[0, which, j], a_sems.at[1, which, j], seq=sibling)

    def mean(x):
        return jnp.mean(x, axis=1, keepdims=True)

    def norm(x):
        centred = x - mean(x)
        scale = lax.rsqrt(mean(centred * centred) + NORM_EPS)
        return centred * scale, scale

    def norm_back(grad, hat, scale, gain):
        grad = grad * gain
        return scale * (grad - mean(grad) - hat * mean(grad * hat))

    def add_rows(row, x):
        small_ref[row:row + 1, :] += jnp.sum(x, axis=0, keepdims=True)

    out_bias, gain1, shift1, down_bias, gain2, shift2, up_bias = (ref[...].reshape(1, -1) for ref in vectors)

    for i in range(spans):
        m_copy(i).start()
    loads = [pltpu.make_async_copy(up_hbm, up_ref, w_sems.at[0]), pltpu.make_async_copy(down_hbm, down_ref, w_sems.at[1])]
    for copy in loads:
        copy.start()
    out_all[:, mine] = out_ref[...]
    out_all[:, theirs] = other_ref[...]
    mixed_all[:, mine] = mixed_ref[...]
    small_ref[...] = jnp.zeros_like(small_ref)
    for copy in loads:
        copy.wait()

    def forward(i, carry):
        m_copy(i).wait()
        branch = dot(mixed_all[at(i), :], out_all[...], NT) + out_bias
        hat, scale = norm(source_ref[at(i), :].astype(F32) + branch)
        first = hat * gain1 + shift1
        low = first.astype(BF16)
        hat_ref[at(i), :] = hat
        scale_ref[at(i), :] = jnp.broadcast_to(scale, (span, 128))
        first_ref[at(i), :] = first
        first_low[at(i), :] = low
        part = jnp.zeros((span, dim), F32)
        for k in range(2):
            cols = slice(k * dim, (k + 1) * dim)
            up = dot(low, up_ref[:, cols]) + up_bias[:, cols]
            below = 0.5 + 0.5 * lax.erf(up * 0.7071067811865476)
            act = (up * below).astype(BF16)
            slope_ref[at(i), cols] = below + up * jnp.exp(-0.5 * up * up) * 0.3989422804014327
            act_ref[at(i), cols] = act
            part = part + dot(act, down_ref[:, cols], NT)
        y_send[at(i), :] = part.astype(BF16)
        y_copy(i).start()
        return carry

    lax.fori_loop(0, spans, forward, 0)

    def turn(i, carry):
        y_copy(i).wait()
        down = y_send[at(i), :].astype(F32) + y_recv[at(i), :].astype(F32) + down_bias
        hat, scale = norm(first_ref[at(i), :] + down)
        y_ref[at(i), :] = (hat * gain2 + shift2).astype(BF16)
        grad = grad_ref[at(i), :].astype(F32)
        add_rows(2, grad * hat)
        add_rows(3, grad)
        second = norm_back(grad, hat, scale, gain2)
        low = second.astype(BF16)
        second_ref[at(i), :] = second
        down_grad[at(i), :] = low
        add_rows(5, low.astype(F32))
        part = jnp.zeros((span, dim), F32)
        for k in range(2):
            cols = slice(k * dim, (k + 1) * dim)
            up = (slope_ref[at(i), cols] * dot(low, down_ref[:, cols])).astype(BF16)
            up_grad[at(i), cols] = up
            add_rows(6 + k, up.astype(F32))
            part = part + dot(up, up_ref[:, cols], NT)
        z_send[at(i), :] = part.astype(BF16)
        z_copy(i).start()
        return carry

    lax.fori_loop(0, spans, turn, 0)

    def products(j, carry):
        cols = pl.ds(pl.multiple_of(j * 512, 512), 512)
        grads[0, :, cols] = dot(first_low[...], up_grad[:, cols], tn).astype(BF16)
        grads[1, :, cols] = dot(down_grad[...], act_ref[:, cols], tn).astype(BF16)
        return carry

    lax.fori_loop(0, hidden // 512, products, 0)
    for which in range(2):
        for j in range(zs):
            a_copy(which, j).start()

    def back(i):
        z_copy(i).wait()
        grad = second_ref[at(i), :] + (z_send[at(i), :].astype(F32) + z_recv[at(i), :].astype(F32))
        hat = hat_ref[at(i), :]
        add_rows(0, grad * hat)
        add_rows(1, grad)
        total = norm_back(grad, hat, scale_ref[at(i), 0:1], gain1)
        low = total.astype(BF16)
        input1_ref[at(i), :] = total
        low_ref[at(i), :] = low
        add_rows(4, low.astype(F32))
        window_ref[REACH * rows + i * span:REACH * rows + (i + 1) * span, :] = dot(low, out_ref[...]).astype(BF16)
        halo.send(i)

    for i in range(spans):
        back(i)
    lane = lax.broadcasted_iota(jnp.int32, (rows, 128), 1)
    along = jnp.zeros((rows, 128), F32)
    for pair in range(width // 128):
        lanes = slice(pair * 128, pair * 128 + 128)
        product = window_ref[REACH * rows:(REACH + 1) * rows, lanes].astype(F32) * mixed_ref[:, lanes].astype(F32)
        even = jnp.sum(jnp.where(lane < 64, product, 0.0), axis=1, keepdims=True)
        odd = jnp.sum(jnp.where(lane < 64, 0.0, product), axis=1, keepdims=True)
        along = jnp.where(lane == 2 * pair, even, jnp.where(lane == 2 * pair + 1, odd, along))
    along_ref[...] = along
    own_stats[0:8, :] = jnp.transpose(lse_ref[...])[0:8, :]
    own_stats[8:16, :] = jnp.transpose(along)[0:8, :]
    stats_ref[:, REACH * rows:(REACH + 1) * rows] = own_stats[...]
    halo.send(spans)
    share = 2 * hidden // dps
    for which in range(2):
        for j in range(zs):
            a_copy(which, j).wait()
            own = pl.ds(pl.multiple_of((2 * j + core) * block, 16), block)
            for p in range(dps):
                if p * share // hidden <= which <= ((p + 1) * share - 1) // hidden:
                    first, last = max(p * share, which * hidden), min((p + 1) * share, (which + 1) * hidden)
                    cols = slice(first - which * hidden, last - which * hidden)
                    total = grads[which, own, cols].astype(F32) + a_recv[which, j, :, cols].astype(F32)
                    for k in range(dps):

                        @pl.when(lax.rem(p - d + dps, dps) == k)
                        def _():
                            share_refs[k][j, :, first - p * share:last - p * share] = total.astype(BF16)

    out_grad_ref[...] = dot(low_ref[...], mixed_ref[...], tn).astype(BF16)
    for part in range(spans + 1):
        halo.relay(part)
    for slot in (0, 2, 4, 6):
        halo.receive(slot)
    halo.finish()


def feed_forward(mixed, out_weight, out_other, source, up, down, grad, lse, vectors, dps, seqs, span=256):
    rows, dim = source.shape
    width, hidden = mixed.shape[1], up.shape[1]
    zs, block = seqs // 2, dim // seqs
    spans = rows // span
    total = (2 * REACH + 1) * rows
    dma = pltpu.SemaphoreType.DMA
    return pl.pallas_call(
        functools.partial(feed_kernel, dps, seqs, span),
        out_shape=(jax.ShapeDtypeStruct((zs, block, 2 * hidden // dps), BF16),) * dps + (
            jax.ShapeDtypeStruct((rows, dim), BF16),
            jax.ShapeDtypeStruct((rows, dim), F32),
            jax.ShapeDtypeStruct((total, width), BF16),
            jax.ShapeDtypeStruct((16, total), F32),
            jax.ShapeDtypeStruct((rows, 128), F32),
            jax.ShapeDtypeStruct((dim, width), BF16),
            jax.ShapeDtypeStruct((8, dim), F32),
        ),
        in_specs=[VMEM] * 4 + [HBM] * 2 + [VMEM] * 9,
        out_specs=(VMEM,) * (dps + 7),
        scratch_shapes=[
            pltpu.VMEM((rows, dim), BF16),
            pltpu.VMEM((16, rows), F32),
            dma((7, spans + 1)),
            dma((7, spans + 1)),
            pltpu.VMEM((dim, hidden), BF16),
            pltpu.VMEM((dim, hidden), BF16),
            dma((2,)),
            pltpu.VMEM((dim, 2 * width), BF16),
            pltpu.VMEM((rows, 2 * width), BF16),
            pltpu.VMEM((rows, dim), F32),
            pltpu.VMEM((rows, dim), F32),
            pltpu.VMEM((rows, 128), F32),
            pltpu.VMEM((rows, dim), BF16),
            pltpu.VMEM((rows, hidden), BF16),
            pltpu.VMEM((rows, hidden), F32),
            pltpu.VMEM((rows, dim), F32),
            pltpu.VMEM((rows, dim), BF16),
            pltpu.VMEM((rows, hidden), BF16),
            pltpu.VMEM((rows, dim), BF16),
            pltpu.VMEM((rows, dim), BF16),
            pltpu.VMEM((rows, dim), BF16),
            pltpu.VMEM((rows, dim), BF16),
            pltpu.VMEM((2, dim, hidden), BF16),
            pltpu.VMEM((2, zs, block, hidden), BF16),
            dma((2, spans)),
            dma((2, spans)),
            dma((2, spans)),
            dma((2, 2, zs)),
        ],
        compiler_params=pltpu.CompilerParams(collective_id=3, has_side_effects=True, vmem_limit_bytes=56 << 20),
        name="feed_forward",
    )(mixed, out_weight, out_other, source, up, down, grad, lse, *vectors)


def memory_slots(id_row):
    count = id_row.shape[0]
    edge = jnp.full((READ_ROWS,), -1, jnp.int32)
    padded = jnp.concatenate([edge, id_row, edge])
    before = sum((padded[READ_ROWS - k:READ_ROWS - k + count] == id_row).astype(jnp.int32) for k in range(1, READ_ROWS + 1))
    behind = sum((padded[READ_ROWS + k:READ_ROWS + k + count] == id_row).astype(jnp.int32) for k in range(1, READ_ROWS + 1))
    return jnp.where(before < READ_ROWS, before, jnp.where(behind < READ_ROWS, 2 * READ_ROWS - 1 - behind, -1))


def on_device(dps, seqs, tokens, doc_ids, memory, qkv_weight, query_bias, value_bias, out_weight, out_bias, norm1_gain, norm1_bias, up_weight, up_bias, down_weight, down_bias, norm2_gain, norm2_bias, out_grad):
    rows = tokens.shape[1]
    width = qkv_weight.shape[2]
    heads = width // HEAD_DIM
    bq, bk = rows, 256
    own = REACH * rows
    pieces = 2 * REACH + 1
    s = lax.axis_index("seq")
    id_row = doc_ids[0]
    edge = jnp.full((own,), -1, jnp.int32)
    slots = memory_slots(id_row)
    window_slots = lax.dynamic_slice_in_dim(jnp.concatenate([edge, slots, edge]), s * rows, pieces * rows, 0)
    window_ids = lax.dynamic_slice_in_dim(jnp.concatenate([edge, id_row, jnp.full((own,), 1 << 20, jnp.int32)]), s * rows, pieces * rows, 0)
    ids = jnp.broadcast_to(window_ids.astype(F32)[None], (8, pieces * rows))

    out_other = lax.ppermute(out_weight, "tensor", [(0, 1), (1, 0)])
    weight = qkv_weight.transpose(1, 0, 2)
    slots_row = jnp.broadcast_to(window_slots[None], (8, pieces * rows))
    query, key, value, source = project_window(
        tokens[0], slots_row, memory, weight, query_bias, value_bias, seqs, 1)
    own_slots = window_slots[own:own + rows]

    mixed_low, logsums = attention_forward(query, key, value, ids, rows, own, bq, bk)

    vectors = (out_bias, norm1_gain, norm1_bias, down_bias, norm2_gain, norm2_bias, up_bias)
    *shares, output, grad_input1, grads_window, stats_window, along_cols, grad_out_weight, small = feed_forward(
        mixed_low, out_weight, out_other, source, up_weight, down_weight, out_grad[0], logsums, vectors, dps, seqs)
    early = shares[:1] + [
        lax.ppermute(shares[k], "dp", [(i, (i + k) % dps) for i in range(dps)]) for k in range(1, dps)]
    proj_grad = attention_backward(query, key, value, grads_window, ids, logsums, along_cols, stats_window, rows, own, bk)

    select = (own_slots[:, None] == jnp.arange(32, dtype=jnp.int32)[None, :]).astype(BF16)
    up_sum, down_sum, out_sum, qkv_sum, input_grad, small = tail(
        early, grad_out_weight, proj_grad, source, weight, grad_input1, select, small, dps, seqs)
    small = small.reshape(32, 2 * width)
    input_grad = input_grad[None]
    piece = small.shape[1] // seqs
    vectors = lax.dynamic_slice_in_dim(small[:6], s * piece, piece, 1)
    memory_grad = small[9:29]
    return (
        output[None], input_grad, memory_grad,
        qkv_sum.transpose(1, 0, 2), small[8, :width], small[8, width:],
        out_sum, vectors[4], vectors[0], vectors[1],
        up_sum, small[6:8].reshape(-1), down_sum, vectors[5], vectors[2], vectors[3],
    )


def solution(mesh):
    in_specs = (
        P("dp", "seq", None), P("dp", None), P(), P(None, None, "tensor"), P("tensor"), P("tensor"), P(None, "tensor"), P(), P(), P(),
        P(None, "tensor"), P("tensor"), P(None, "tensor"), P(), P(), P(), P("dp", "seq", None),
    )
    out_specs = (
        P("dp", "seq", None), P("dp", "seq", None), P(), P("seq", None, "tensor"), P("tensor"), P("tensor"), P("seq", "tensor"), P("seq"), P("seq"), P("seq"),
        P("seq", "tensor"), P("tensor"), P("seq", "tensor"), P("seq"), P("seq"), P("seq"),
    )
    step = functools.partial(on_device, mesh.shape["dp"], mesh.shape["seq"])
    return jax.shard_map(step, mesh=mesh, in_specs=in_specs, out_specs=out_specs, check_vma=False)
```

```python
import functools

import jax
import jax.numpy as jnp
from jax import lax
from jax.experimental import pallas as pl
from jax.experimental.pallas import tpu as pltpu
from jax.sharding import PartitionSpec as P

HEAD_DIM = 64
READ_ROWS = 10
REACH = 3
NORM_EPS = 1e-05
OWNERS = 4
F32, BF16 = jnp.float32, jnp.bfloat16
NT = (((1,), (1,)), ((), ()))
NN = (((1,), (0,)), ((), ()))
NEG = -1e30
FLOOR = -1e29
VMEM = pl.BlockSpec(memory_space=pltpu.VMEM)
HBM = pl.BlockSpec(memory_space=pltpu.HBM)


def remote(source, target, send_sem, recv_sem, **where):
    return pltpu.make_async_remote_copy(
        source, target, send_sem, recv_sem, device_id=where, device_id_type=pl.DeviceIdType.MESH
    )


def greet(partners):
    barrier = pltpu.get_barrier_semaphore()
    total = 0
    for present, where in partners:
        total = total + present.astype(jnp.int32)

        @pl.when(present)
        def _():
            pl.semaphore_signal(barrier, inc=1, device_id=where, device_id_type=pl.DeviceIdType.MESH)

    pl.semaphore_wait(barrier, total)


def dot(a, b, dims=NN):
    return lax.dot_general(a, b, dims, preferred_element_type=F32)

def low_half(shape):
    return lax.broadcasted_iota(jnp.int32, shape, len(shape) - 1) < 64

def id_columns(ids_ref, start, count):
    row = jnp.broadcast_to(ids_ref[0:1, pl.ds(start, count)], (128, count))
    return jnp.transpose(row)

def wide(x, count):
    return jnp.concatenate([x] * (count // 128), axis=1)

def split_heads(source_ref, rows, target_ref, pairs, keep):
    for pair in range(pairs):
        block = source_ref[rows, pair * 128:pair * 128 + 128]
        target_ref[2 * pair] = jnp.where(keep, block, jnp.zeros_like(block))
        target_ref[2 * pair + 1] = jnp.where(keep, jnp.zeros_like(block), block)

def document_range(ids_ref, start, count, bk):
    mine, every = ids_ref[0:1, pl.ds(start, count)], ids_ref[0:1, :]
    low, high = jnp.min(mine), jnp.max(mine)
    begin = jnp.sum(jnp.where(every < low, 1.0, 0.0)).astype(jnp.int32)
    end = jnp.sum(jnp.where(every <= high, 1.0, 0.0)).astype(jnp.int32)
    shift = bk.bit_length() - 1
    first, last = begin >> shift, (end + bk - 1) >> shift
    full_first, full_last = (begin + bk - 1) >> shift, end >> shift
    whole = jnp.logical_and(low == high, full_first < full_last)
    return first, jnp.where(whole, full_first, first), jnp.where(whole, full_last, first), last


def sweep(span, body):
    first, full_first, full_last, last = span
    lax.fori_loop(full_first, full_last, lambda j, c: body(j, False, c), 0)

    def edge(i, c):
        j = first + i
        return body(jnp.where(j < full_first, j, j + full_last - full_first), True, c)

    lax.fori_loop(0, last - first - (full_last - full_first), edge, 0)

def fwd_kernel(bq, bk, own, q_ref, k_ref, v_ref, ids_ref, o_ref, lse_ref, acc_ref, max_ref, q_heads, cols_ref):
    pairs = q_ref.shape[1] // 128
    rows = o_ref.shape[0]
    low_q, low_k = low_half((bq, 128)), low_half((bk, 128))

    def block(qb, carry):
        mine = pl.ds(pl.multiple_of(qb * bq, bq), bq)
        cols_ref[...] = id_columns(ids_ref, pl.multiple_of(own + qb * bq, bq), bq)
        split_heads(q_ref, pl.ds(pl.multiple_of(own + qb * bq, bq), bq), q_heads, pairs, low_q)
        acc_ref[...] = jnp.zeros_like(acc_ref)
        max_ref[...] = jnp.full_like(max_ref, FLOOR)

        def step(j, masked, carry):
            there = pl.ds(pl.multiple_of(j * bk, bk), bk)
            def pair_step(pair, carry):
                lanes = pl.ds(pair * 128, 128)
                key = k_ref[there, lanes]
                value = v_ref[there, lanes]
                for odd in range(2):
                    head = 2 * pair + odd
                    scores = dot(q_heads[head], key, NT)
                    if masked:
                        scores = jnp.where(wide(cols_ref[...], bk) == ids_ref[0:1, there], scores, NEG)
                    old = max_ref[head]
                    new = jnp.maximum(old, jnp.max(scores, axis=1, keepdims=True))
                    probs = jnp.exp(scores - wide(new, bk)).astype(BF16)
                    ones = jnp.where(low_k if odd == 0 else ~low_k, value, jnp.ones_like(value))
                    acc_ref[head] = acc_ref[head] * jnp.exp(old - new) + dot(probs, ones)
                    max_ref[head] = new
                return carry
            for pair in range(pairs):
                pair_step(pair, carry)
            return carry

        sweep(document_range(ids_ref, pl.multiple_of(own + qb * bq, bq), bq, bk), step)
        stats = jnp.zeros((bq, 128), F32)
        lane = lax.broadcasted_iota(jnp.int32, (bq, 128), 1)
        for pair in range(pairs):
            even, odd = acc_ref[2 * pair], acc_ref[2 * pair + 1]
            total_even, total_odd = even[:, 64:65], odd[:, 0:1]
            mixed = jnp.where(low_q, even / total_even, odd / total_odd)
            o_ref[mine, pair * 128:pair * 128 + 128] = mixed.astype(BF16)
            stats = jnp.where(lane == 2 * pair, max_ref[2 * pair] + jnp.log(total_even), stats)
            stats = jnp.where(lane == 2 * pair + 1, max_ref[2 * pair + 1] + jnp.log(total_odd), stats)
        lse_ref[mine, :] = stats
        return carry

    lax.fori_loop(0, rows // bq, block, 0)

def attention_forward(query, key, value, ids, rows, own, bq=256, bk=256):
    width = query.shape[1]
    heads = width // 64
    return pl.pallas_call(
        functools.partial(fwd_kernel, bq, bk, own),
        out_shape=(jax.ShapeDtypeStruct((rows, width), BF16), jax.ShapeDtypeStruct((rows, 128), F32)),
        in_specs=[VMEM] * 4,
        out_specs=(pl.BlockSpec(memory_space=pltpu.VMEM),) * 2,
        scratch_shapes=[pltpu.VMEM((heads, bq, 128), F32), pltpu.VMEM((heads, bq, 128), F32), pltpu.VMEM((heads, bq, 128), BF16), pltpu.VMEM((bq, 128), F32)],
        compiler_params=pltpu.CompilerParams(vmem_limit_bytes=24 << 20),
        name="attention_forward",
    )(query, key, value, ids)

def bwd_kernel(bk, own, q_hbm, k_hbm, v_hbm, g_hbm, ids_ref, lse_ref, along_ref, rows_ref, out_ref, q_ref, k_ref, v_ref, g_ref, sems, dq_acc, dk_acc, dv_acc, q_heads, k_heads, v_heads, g_heads, lse_cols, along_cols, cols_ref):
    bq, width = out_ref.shape[0], q_ref.shape[1]
    pairs = width // 128
    heads = 2 * pairs
    low_q = low_half((bq, 128))

    blocks = document_range(ids_ref, own, bq, bk)
    first_own, last_own = own // bk, (own + bq) // bk

    def copies(j):
        there = pl.ds(pl.multiple_of(j * bk, bk), bk)
        pairs_of = ((q_hbm, q_ref), (k_hbm, k_ref), (v_hbm, v_ref), (g_hbm, g_ref))
        return [pltpu.make_async_copy(source.at[there], target.at[there], sems.at[i, j]) for i, (source, target) in enumerate(pairs_of)]

    def start_all(j, carry):
        @pl.when(jnp.logical_or(j < first_own, j >= last_own))
        def _():
            for copy in copies(j):
                copy.start()

        return carry

    for j in range(first_own, last_own):
        for copy in copies(j):
            copy.start()
    lax.fori_loop(blocks[0], blocks[3], start_all, 0)
    mine, here = pl.ds(0, bq), pl.ds(own, bq)
    cols_ref[...] = id_columns(ids_ref, own, bq)
    for acc in (dq_acc, dk_acc, dv_acc):
        acc[...] = jnp.zeros_like(acc)
    for head in range(heads):
        lse_cols[head] = jnp.broadcast_to(lse_ref[mine, head:head + 1], (bq, 128))
        along_cols[head] = jnp.broadcast_to(along_ref[mine, head:head + 1], (bq, 128))
    for j in range(first_own, last_own):
        for copy in copies(j):
            copy.wait()
    for source, target in ((q_ref, q_heads), (k_ref, k_heads), (v_ref, v_heads), (g_ref, g_heads)):
        split_heads(source, here, target, pairs, low_q)

    def step(j, masked, carry):
        there = pl.ds(pl.multiple_of(j * bk, bk), bk)

        @pl.when(jnp.logical_or(j < first_own, j >= last_own))
        def _():
            for copy in copies(j):
                copy.wait()

        def pair_step(pair, carry):
            lanes = pl.ds(pair * 128, 128)
            q_far, k_far, v_far, g_far = (r[there, lanes] for r in (q_ref, k_ref, v_ref, g_ref))
            def hide(x):
                return jnp.where(wide(cols_ref[...], bk) == ids_ref[0:1, there], x, 0.0) if masked else x
            for odd in range(2):
                head = 2 * pair + odd
                scores = dot(q_heads[head], k_far, NT)
                probs = hide(jnp.exp(scores - wide(lse_cols[head], bk)))
                slope = dot(g_heads[head], v_far, NT)
                grad = (probs * (slope - wide(along_cols[head], bk))).astype(BF16)
                dq_acc[head] += dot(grad, k_far)
                scores = dot(k_heads[head], q_far, NT)
                probs = hide(jnp.exp(scores - rows_ref[pl.ds(head, 1), there]))
                slope = dot(v_heads[head], g_far, NT)
                grad = (probs * (slope - rows_ref[pl.ds(8 + head, 1), there])).astype(BF16)
                dv_acc[head] += dot(probs.astype(BF16), g_far)
                dk_acc[head] += dot(grad, q_far)
            return carry
        for pair in range(pairs):
            pair_step(pair, carry)
        return carry

    sweep(blocks, step)
    for which, (acc, factor) in enumerate(((dq_acc, 0.125), (dk_acc, 1.0), (dv_acc, 1.0))):
        for pair in range(pairs):
            both = jnp.where(low_q, acc[2 * pair], acc[2 * pair + 1]) * factor
            out_ref[mine, which * width + pair * 128:which * width + pair * 128 + 128] = both.astype(BF16)

def attention_backward(query, key, value, grads, ids, lse, along, stat_rows, rows, own, bk=256):
    width = query.shape[1]
    heads, bq = width // 64, rows
    return pl.pallas_call(
        functools.partial(bwd_kernel, bk, own),
        out_shape=jax.ShapeDtypeStruct((rows, 3 * width), BF16),
        in_specs=[HBM] * 4 + [VMEM] * 4,
        out_specs=pl.BlockSpec(memory_space=pltpu.VMEM),
        scratch_shapes=[pltpu.VMEM(query.shape, BF16)] * 4 + [pltpu.SemaphoreType.DMA((4, query.shape[0] // bk))] + [pltpu.VMEM((heads, bq, 128), F32)] * 3 + [pltpu.VMEM((heads, bq, 128), BF16)] * 4 + [pltpu.VMEM((heads, bq, 128), F32)] * 2 + [pltpu.VMEM((bq, 128), F32)],
        compiler_params=pltpu.CompilerParams(vmem_limit_bytes=60 << 20),
        name="attention_backward",
    )(query, key, value, grads, ids, lse, along, stat_rows)

class Halo:
    def __init__(self, count, pieces, send_sem, recv_sem):
        self.count, self.pieces, self.send_sem, self.recv_sem = count, pieces, send_sem, recv_sem
        s = self.s = lax.axis_index("seq")
        self.core = lax.rem(s, 2)
        self.sibling = s + 1 - 2 * self.core
        self.left, self.right = s >= 2, s < count - 2

    def neighbours(self):
        s, count = self.s, self.count
        return [(s >= k, {"seq": s - k}) for k in (1, 2)] + [(s < count - k, {"seq": s + k}) for k in (1, 2)]

    def own(self, part, kind, slot, target):
        source, window = self.pieces[part]
        return remote(source, window(slot), self.send_sem.at[kind, part], self.recv_sem.at[slot, part], seq=target)

    def moved(self, part, kind, held, slot, target):
        window = self.pieces[part][1]
        return remote(window(held), window(slot), self.send_sem.at[kind, part], self.recv_sem.at[slot, part], seq=target)

    def first_copies(self, part):
        s, core = self.s, self.core
        return (
            (self.right, self.own(part, 0, 1, s + 2)),
            (self.left, self.own(part, 1, 5, s - 2)),
            (core == 0, self.own(part, 2, 2, self.sibling)),
            (core == 1, self.own(part, 2, 4, self.sibling)),
        )

    def from_left(self, part):
        s, core, left, right = self.s, self.core, self.left, self.right
        return (
            (jnp.logical_and(left, jnp.logical_and(core == 1, right)), self.moved(part, 3, 1, 0, s + 1)),
            (jnp.logical_and(left, core == 0), self.moved(part, 4, 1, 0, self.sibling)),
            (jnp.logical_and(left, core == 1), self.moved(part, 4, 1, 2, self.sibling)),
        )

    def from_right(self, part):
        s, core, left, right = self.s, self.core, self.left, self.right
        return (
            (jnp.logical_and(right, jnp.logical_and(core == 0, left)), self.moved(part, 5, 5, 6, s - 1)),
            (jnp.logical_and(right, core == 0), self.moved(part, 6, 5, 4, self.sibling)),
            (jnp.logical_and(right, core == 1), self.moved(part, 6, 5, 6, self.sibling)),
        )

    def each(self, copies, act):
        for present, copy in copies:
            pl.when(present)(functools.partial(act, copy))

    def send(self, part):
        self.each(self.first_copies(part), lambda copy: copy.start())

    def arrived(self, slot, part):
        self.own(part, 0, slot, self.s).wait_recv()

    def relay(self, part):
        pl.when(self.left)(functools.partial(self.arrived, 1, part))
        self.each(self.from_left(part), lambda copy: copy.start())
        pl.when(self.right)(functools.partial(self.arrived, 5, part))
        self.each(self.from_right(part), lambda copy: copy.start())

    def present(self, slot):
        block = self.s + slot - REACH
        return jnp.logical_and(block >= 0, block < self.count)

    def receive(self, slot):
        for part in range(len(self.pieces)):
            pl.when(self.present(slot))(functools.partial(self.arrived, slot, part))

    def finish(self):
        for part in range(len(self.pieces)):
            self.each(self.first_copies(part) + self.from_left(part) + self.from_right(part), lambda copy: copy.wait_send())


def project_kernel(count, parts, own_ref, slots_ref, memory_ref, weight_ref, query_bias_ref, value_bias_ref,
                   q_ref, k_ref, v_ref, source_ref, window_ref, weight, table, send_sem, recv_sem, local_sem):
    block = own_ref.shape[0]
    rows = block // parts
    tile = 256
    tiles = block // tile

    def piece(part):
        return own_ref.at[pl.ds(part * rows, rows)], lambda slot: window_ref.at[pl.ds(slot * block + part * rows, rows)]

    halo = Halo(count, [piece(part) for part in range(parts)], send_sem, recv_sem)
    greet(halo.neighbours())
    for part in range(parts):
        halo.send(part)
    local = [
        pltpu.make_async_copy(own_ref, window_ref.at[pl.ds(REACH * block, block)], local_sem.at[0]),
        pltpu.make_async_copy(weight_ref, weight, local_sem.at[1]),
    ]
    for copy in local:
        copy.start()
    table[...] = jnp.zeros_like(table)
    table[0:memory_ref.shape[0], :] = memory_ref[...]
    query_bias, value_bias = query_bias_ref[...].reshape(1, -1), value_bias_ref[...].reshape(1, -1)

    def project(load, start, keep):
        hot = (lax.broadcasted_iota(jnp.int32, (32, tile), 0) == slots_ref[0:1, pl.ds(start, tile)]).astype(F32).astype(BF16)
        tn = (((0,), (0,)), ((), ()))
        chosen = dot(hot, table[...], tn)
        inside = wide(dot(hot, jnp.ones((32, 128), BF16), tn), chosen.shape[1])
        source = jnp.where(inside > 0.5, chosen, load().astype(F32)).astype(BF16)
        keep(source)
        out = pl.ds(start, tile)
        q_ref[out, :] = (dot(source, weight[0]) + query_bias).astype(BF16) * 0.125
        k_ref[out, :] = dot(source, weight[1]).astype(BF16)
        v_ref[out, :] = (dot(source, weight[2]) + value_bias).astype(BF16)

    def own_tile(i, carry):
        at = pl.ds(pl.multiple_of(i * tile, tile), tile)

        def keep(source):
            source_ref[at, :] = source

        start = pl.multiple_of(REACH * block + i * tile, tile)
        project(lambda: window_ref[pl.ds(start, tile), :], start, keep)
        return carry

    for copy in local:
        copy.wait()
    lax.fori_loop(0, tiles, own_tile, 0)
    for part in range(parts):
        halo.relay(part)

    def two_blocks(low, high):
        def step(i, carry):
            slot = low + (high - low) * (i // tiles)

            @pl.when(halo.present(slot))
            def _():
                start = pl.multiple_of(slot * block + lax.rem(i, tiles) * tile, tile)
                project(lambda: window_ref[pl.ds(start, tile), :], start, lambda source: None)

            return carry

        lax.fori_loop(0, 2 * tiles, step, 0)

    two_blocks(1, 5)
    for slots in ((2, 4), (0, 6)):
        for slot in slots:
            halo.receive(slot)
        two_blocks(*slots)
    halo.finish()


def project_window(own, slots, memory, weight, query_bias, value_bias, count, collective_id, parts=2):
    rows, dim = own.shape
    width = weight.shape[2]
    total = (2 * REACH + 1) * rows
    wide_out = jax.ShapeDtypeStruct((total, width), BF16)
    return pl.pallas_call(
        functools.partial(project_kernel, count, parts),
        out_shape=(wide_out, wide_out, wide_out, jax.ShapeDtypeStruct((rows, dim), BF16)),
        in_specs=[HBM, VMEM, VMEM, HBM, VMEM, VMEM],
        out_specs=(VMEM,) * 4,
        scratch_shapes=[
            pltpu.VMEM((total, dim), BF16),
            pltpu.VMEM(weight.shape, BF16),
            pltpu.VMEM((32, dim), BF16),
            pltpu.SemaphoreType.DMA((7, parts)),
            pltpu.SemaphoreType.DMA((7, parts)),
            pltpu.SemaphoreType.DMA((2,)),
        ],
        compiler_params=pltpu.CompilerParams(collective_id=collective_id, has_side_effects=True, vmem_limit_bytes=40 << 20),
        name="project_window",
    )(own, slots, memory, weight, query_bias, value_bias)


def split_dot(left, right, dims):
    high = right.astype(BF16)
    low = (right - high.astype(F32)).astype(BF16)
    return dot(left, high, dims) + dot(left, low, dims)


def tail_kernel(dps, seqs, width, *refs):
    (early_refs, (out_grad_ref, proj_ref, source_ref, weight_ref, input1_ref, select_ref, small_ref),
     (up_out, down_out, out_out, qkv_out, input_out, small_out),
     (mix, y_send, y_recv, a_recv, parts, b_recv, small_in, small_recv, small_mine, small_dp),
     (mine, c_recv, last, d_recv), (y_sems, a_sems, b_sems, c_sems, d_sems, s_sems)) = (
        refs[:dps], refs[dps:dps + 7], refs[dps + 7:dps + 13], refs[dps + 13:dps + 23], refs[dps + 23:dps + 27], refs[dps + 27:])
    zs = seqs // 2
    bits = zs.bit_length() - 1
    t, d, s = lax.axis_index("tensor"), lax.axis_index("dp"), lax.axis_index("seq")
    z, core = s // 2, lax.rem(s, 2)
    sibling = s + 1 - 2 * core
    late, early = a_recv.shape[0], mine.shape[0] - a_recv.shape[0]
    chunk = a_recv.shape[3]
    shares = -(-chunk // width)
    owners = small_out.shape[0]
    block, hidden = up_out.shape
    share_width = early * width
    rows, columns = proj_ref.shape
    third = columns // 3
    steps = y_send.shape[0]
    span = rows // steps
    true = s >= 0
    partners = [(true, {"seq": lax.rem(s + k, seqs)}) for k in range(1, seqs)]
    partners += [(true, {"dp": lax.rem(d + k, dps)}) for k in range(1, dps)]
    partners += [(true, {"tensor": 1 - t})]
    greet(partners)

    def active(c):
        return true if c < early else d < shares

    def a_copy(c, j):
        start = pl.multiple_of((2 * j + 1 - core) * block, 16)
        at = (c - early) * chunk
        i = c - early
        return remote(mix.at[pl.ds(start, block), pl.ds(at, chunk)], a_recv.at[i, j], a_sems.at[0, i, j], a_sems.at[1, i, j], seq=sibling)

    def b_copy(c, k):
        other = lax.rem(d + k, dps)
        i = c - early
        return other, remote(parts.at[i, other], b_recv.at[i, k], b_sems.at[0, i, k], b_sems.at[1, i, k], dp=other)

    def first_slot(b):
        return sum(zs // (2 << e) for e in range(b))

    def c_copies(c, b):
        size = 2 << b
        high = lax.rem(z // (1 << b), 2)
        partner = z + (1 << b) - (size * high)
        low = lax.rem(partner, size)
        return [
            remote(mine.at[c, i * size + low], c_recv.at[c, first_slot(b) + i], c_sems.at[0, c, first_slot(b) + i], c_sems.at[1, c, first_slot(b) + i], seq=2 * partner + core)
            for i in range(zs // size)
        ]

    def d_copy(c, k):
        return remote(last.at[c], d_recv.at[c, k], d_sems.at[0, c, k], d_sems.at[1, c, k], dp=lax.rem(d + k, dps))

    def start_a(c):
        for j in range(zs):
            a_copy(c, j).start()

    def start_early(c):
        lanes = slice(c * width, c * width + width)
        for j in range(zs):
            total = early_refs[0][j, :, lanes].astype(F32)
            for k in range(1, dps):
                total = total + early_refs[k][j, :, lanes].astype(F32)
            mine[c, j] = total.astype(BF16)
        for copy in c_copies(c, 0):
            copy.start()

    def end_a(c):
        i = c - early
        for j in range(zs):
            a_copy(c, j).wait()
            start = pl.multiple_of((2 * j + core) * block, 16)
            for p in range(shares):
                real = min(width, chunk - p * width)
                lanes = pl.ds(i * chunk + p * width, real)
                total = mix[pl.ds(start, block), lanes].astype(F32) + a_recv[i, j, :, p * width:p * width + real].astype(F32)
                parts[i, p, j, :, 0:real] = total.astype(BF16)
                if real < width:
                    parts[i, p, j, :, real:width] = jnp.zeros((block, width - real), BF16)
        for k in range(1, dps):
            other, copy = b_copy(c, k)
            pl.when(other < shares)(copy.start)

    def end_b(c):
        i = c - early
        for k in range(1, dps):
            other, copy = b_copy(c, k)
            pl.when(other < shares)(copy.wait_send)

        @pl.when(d < shares)
        def _():
            for k in range(1, dps):
                b_copy(c, k)[1].wait_recv()
            for j in range(zs):
                total = parts[i, d, j].astype(F32)
                for k in range(1, dps):
                    total = total + b_recv[i, k, j].astype(F32)
                mine[c, j] = total.astype(BF16)
            for copy in c_copies(c, 0):
                copy.start()

    def end_c(c, b):
        size = 2 << b
        kept = lax.rem(z, size)

        @pl.when(active(c))
        def _():
            for i, copy in enumerate(c_copies(c, b)):
                copy.wait()
                held = mine[c, i * size + kept].astype(F32) + c_recv[c, first_slot(b) + i].astype(F32)
                if b < bits - 1:
                    mine[c, i * size + kept] = held.astype(BF16)
                else:
                    last[c] = held.astype(BF16)
            if b < bits - 1:
                for copy in c_copies(c, b + 1):
                    copy.start()
            else:
                for k in range(1, dps):
                    d_copy(c, k).start()

    def put(c, share, value):
        count = dps if c < early else shares
        for p in range(count):

            @pl.when(share == p)
            def _():
                if c < early:
                    which, column = divmod(p * share_width + c * width, hidden)
                    (up_out, down_out)[which][:, column:column + width] = value.astype(F32)
                    return
                first = (c - early) * chunk + p * width
                for lane in range(0, min(width, chunk - p * width), 128):
                    which, column = divmod(first + lane, third)
                    part = value[:, lane:lane + 128].astype(F32)
                    if which == 0:
                        out_out[:, column:column + 128] = part
                    else:
                        qkv_out[which - 1, :, column:column + 128] = part

    def end_d(c):
        @pl.when(active(c))
        def _():
            put(c, d, last[c])
            for k in range(1, dps):
                d_copy(c, k).wait_send()

        for k in range(1, dps):
            share = lax.rem(d + dps - k, dps)

            @pl.when(true if c < early else share < shares)
            def _():
                d_copy(c, k).wait_recv()
                put(c, share, d_recv[c, k])

    def y_copy(i):
        return remote(y_send.at[i], y_recv.at[i], y_sems.at[0, i], y_sems.at[1, i], tensor=1 - t)

    for c in range(early):
        start_early(c)
    out_width = out_grad_ref.shape[1]
    mix[:, 0:out_width] = out_grad_ref[...]
    for i in range(3):
        part = lax.dot_general(source_ref[...], proj_ref[:, i * third:(i + 1) * third], (((0,), (0,)), ((), ())), preferred_element_type=F32)
        mix[:, out_width + i * third:out_width + (i + 1) * third] = part.astype(BF16)
    for c in range(early, early + late):
        start_a(c)
    for i in range(steps):
        at = slice(i * span, (i + 1) * span)
        y_send[i] = sum(dot(proj_ref[at, j * third:(j + 1) * third], weight_ref[j], NT) for j in range(3)).astype(BF16)
        y_copy(i).start()
    small_in[0] = small_ref[...]
    for i in range(1, owners):
        small_in[i] = jnp.zeros_like(small_ref)
    small_in[1, 0:1, 0:third] = jnp.sum(proj_ref[:, 0:third].astype(F32), axis=0, keepdims=True)
    small_in[1, 0:1, third:2 * third] = jnp.sum(proj_ref[:, 2 * third:3 * third].astype(F32), axis=0, keepdims=True)

    def end_y():
        memory = jnp.zeros((32, input_out.shape[1]), F32)
        for i in range(steps):
            y_copy(i).wait()
            at = slice(i * span, (i + 1) * span)
            total = input1_ref[at, :] + (y_send[i].astype(F32) + y_recv[i].astype(F32))
            select = select_ref[at, :]
            memory = memory + split_dot(select, total, (((0,), (0,)), ((), ())))
            inside = dot(select, jnp.ones((32, total.shape[1]), BF16))
            input_out[at, :] = jnp.where(inside > 0.5, 0.0, total).astype(BF16)
        small_in[1, 1:8, :] = memory[0:7]
        small_in[2] = memory[7:15]
        small_in[3, 0:5, :] = memory[15:20]
        for hop in range(1, seqs):
            owner = lax.rem(s + hop, seqs)
            pl.when(owner < owners)(to_owner(hop, owner).start)

    def to_owner(hop, owner):
        return remote(small_in.at[owner], small_recv.at[hop], s_sems.at[0, 0, hop], s_sems.at[1, 0, hop], seq=owner)

    def across(k):
        return remote(small_mine, small_dp.at[k], s_sems.at[0, 1, k], s_sems.at[1, 1, k], dp=lax.rem(d + k, dps))

    def back(hop, owner, target):
        return remote(small_out.at[owner], small_out.at[owner], s_sems.at[0, 2, hop], s_sems.at[1, 2, hop], seq=target)

    def small_one():
        @pl.when(s < owners)
        def _():
            total = small_in[s]
            for hop in range(1, seqs):
                to_owner(hop, s).wait_recv()
                total = total + small_recv[hop]
            small_mine[...] = total
            for k in range(1, dps):
                across(k).start()

    def small_two():
        @pl.when(s < owners)
        def _():
            small_dp[0] = small_mine[...]
            for k in range(1, dps):
                across(k).wait()
            ordered = jnp.zeros(small_mine.shape, F32)
            for index in range(dps):
                ordered = ordered + small_dp[lax.rem(d + dps - index, dps)]
            small_out[s] = ordered
            for hop in range(1, seqs):
                back(hop, s, lax.rem(s + hop, seqs)).start()

    def small_three():
        for hop in range(1, seqs):
            owner = lax.rem(s + hop, seqs)
            pl.when(owner < owners)(to_owner(hop, owner).wait_send)
        for hop in range(1, seqs):
            pl.when(lax.rem(s + seqs - hop, seqs) < owners)(back(hop, 0, s).wait_recv)
            pl.when(s < owners)(back(hop, 0, s).wait_send)

    zed = [functools.partial(end_c, b=b) for b in range(bits)]
    lates = list(range(early, early + late))
    for c in lates:
        end_a(c)
    for c in range(early):
        zed[0](c)
    for c in lates:
        end_b(c)
    end_y()
    for b in range(1, bits):
        for c in range(early):
            zed[b](c)
        for c in lates:
            zed[b - 1](c)
        if b == 1:
            small_one()
    for c in range(early):
        end_d(c)
    small_two()
    for c in lates:
        zed[bits - 1](c)
    for c in lates:
        end_d(c)
    small_three()


def tail(early, out, proj, source, weight, input1, select, small, dps, seqs):
    zs = seqs // 2
    dim = source.shape[1]
    hidden = early[0].shape[2] * dps // 2
    rows = proj.shape[0]
    block = dim // seqs
    mixed = out.shape[1] + proj.shape[1]
    late = 2
    chunk = mixed // late
    width = -(-chunk // (128 * dps)) * 128
    width = early[0].shape[2] if early[0].shape[2] % width else width
    chunks = early[0].shape[2] // width + late
    steps = 4
    table = (OWNERS,) + small.shape
    dma = pltpu.SemaphoreType.DMA
    return pl.pallas_call(
        functools.partial(tail_kernel, dps, seqs, width),
        out_shape=(
            jax.ShapeDtypeStruct((block, hidden), F32),
            jax.ShapeDtypeStruct((block, hidden), F32),
            jax.ShapeDtypeStruct((block, out.shape[1]), F32),
            jax.ShapeDtypeStruct((3, block, out.shape[1]), F32),
            jax.ShapeDtypeStruct((rows, dim), BF16),
            jax.ShapeDtypeStruct(table, F32),
        ),
        in_specs=[VMEM] * (dps + 7),
        out_specs=(VMEM,) * 6,
        scratch_shapes=[
            pltpu.VMEM((dim, mixed), BF16),
            pltpu.VMEM((steps, rows // steps, dim), BF16),
            pltpu.VMEM((steps, rows // steps, dim), BF16),
            pltpu.VMEM((late, zs, block, chunk), BF16),
            pltpu.VMEM((late, dps, zs, block, width), BF16),
            pltpu.VMEM((late, dps, zs, block, width), BF16),
            pltpu.VMEM(table, F32),
            pltpu.VMEM((seqs,) + small.shape, F32),
            pltpu.VMEM(small.shape, F32),
            pltpu.VMEM((dps,) + small.shape, F32),
            pltpu.VMEM((chunks, zs, block, width), BF16),
            pltpu.VMEM((chunks, zs - 1, block, width), BF16),
            pltpu.VMEM((chunks, block, width), BF16),
            pltpu.VMEM((chunks, dps, block, width), BF16),
            dma((2, steps)),
            dma((2, late, zs)),
            dma((2, late, dps)),
            dma((2, chunks, zs)),
            dma((2, chunks, dps)),
            dma((2, 3, max(seqs, dps))),
        ],
        compiler_params=pltpu.CompilerParams(collective_id=7, has_side_effects=True, vmem_limit_bytes=48 << 20),
        name="tail",
    )(*early, out, proj, source, weight, input1, select, small)


def feed_kernel(dps, seqs, span, *refs):
    feed_body(dps, seqs, span, *refs[:8], refs[8:15], refs[15:15 + dps], *refs[15 + dps:])


def feed_body(dps, seqs, span, mixed_ref, out_ref, other_ref, source_ref, up_hbm, down_hbm, grad_ref, lse_ref, vectors, share_refs,
                y_ref, input1_ref, window_ref, stats_ref, along_ref, out_grad_ref, small_ref,
                low_ref, own_stats, h_send, h_recv,
                up_ref, down_ref, w_sems, out_all, mixed_all, first_ref, hat_ref, scale_ref, first_low, act_ref, slope_ref, second_ref, down_grad, up_grad,
                y_send, y_recv, z_send, z_recv, grads, a_recv, m_sems, y_sems, z_sems, a_sems):
    rows, dim = source_ref.shape
    width, hidden = mixed_ref.shape[1], up_ref.shape[1]
    zs, block = seqs // 2, dim // seqs
    t, d, s = lax.axis_index("tensor"), lax.axis_index("dp"), lax.axis_index("seq")
    core = lax.rem(s, 2)
    sibling = s + 1 - 2 * core
    spans = rows // span
    true = s >= 0

    def piece(part):
        return window_ref.at[pl.ds(REACH * rows + part * span, span)], lambda slot: window_ref.at[pl.ds(slot * rows + part * span, span)]

    stats_piece = own_stats, lambda slot: stats_ref.at[:, pl.ds(slot * rows, rows)]
    halo = Halo(seqs, [piece(part) for part in range(spans)] + [stats_piece], h_send, h_recv)
    greet([(true, {"tensor": 1 - t})] + halo.neighbours())
    tn = (((0,), (0,)), ((), ()))

    def at(i):
        return pl.ds(pl.multiple_of(i * span, span), span)

    mine = pl.ds(pl.multiple_of(t * width, 128), width)
    theirs = pl.ds(pl.multiple_of((1 - t) * width, 128), width)

    def m_copy(i):
        return remote(mixed_ref.at[at(i)], mixed_all.at[at(i), mine], m_sems.at[0, i], m_sems.at[1, i], tensor=1 - t)

    def y_copy(i):
        return remote(y_send.at[at(i)], y_recv.at[at(i)], y_sems.at[0, i], y_sems.at[1, i], tensor=1 - t)

    def z_copy(i):
        return remote(z_send.at[at(i)], z_recv.at[at(i)], z_sems.at[0, i], z_sems.at[1, i], tensor=1 - t)

    def a_copy(which, j):
        start = pl.multiple_of((2 * j + 1 - core) * block, 16)
        return remote(grads.at[which, pl.ds(start, block)], a_recv.at[which, j], a_sems.at[0, which, j], a_sems.at[1, which, j], seq=sibling)

    def mean(x):
        return jnp.mean(x, axis=1, keepdims=True)

    def norm(x):
        centred = x - mean(x)
        scale = lax.rsqrt(mean(centred * centred) + NORM_EPS)
        return centred * scale, scale

    def norm_back(grad, hat, scale, gain):
        grad = grad * gain
        return scale * (grad - mean(grad) - hat * mean(grad * hat))

    def add_rows(row, x):
        small_ref[row:row + 1, :] += jnp.sum(x, axis=0, keepdims=True)

    out_bias, gain1, shift1, down_bias, gain2, shift2, up_bias = (ref[...].reshape(1, -1) for ref in vectors)

    for i in range(spans):
        m_copy(i).start()
    loads = [pltpu.make_async_copy(up_hbm, up_ref, w_sems.at[0]), pltpu.make_async_copy(down_hbm, down_ref, w_sems.at[1])]
    for copy in loads:
        copy.start()
    out_all[:, mine] = out_ref[...]
    out_all[:, theirs] = other_ref[...]
    mixed_all[:, mine] = mixed_ref[...]
    small_ref[...] = jnp.zeros_like(small_ref)
    for copy in loads:
        copy.wait()

    def forward(i, carry):
        m_copy(i).wait()
        branch = dot(mixed_all[at(i), :], out_all[...], NT) + out_bias
        hat, scale = norm(source_ref[at(i), :].astype(F32) + branch)
        first = hat * gain1 + shift1
        low = first.astype(BF16)
        hat_ref[at(i), :] = hat
        scale_ref[at(i), :] = jnp.broadcast_to(scale, (span, 128))
        first_ref[at(i), :] = first
        first_low[at(i), :] = low
        part = jnp.zeros((span, dim), F32)
        for k in range(2):
            cols = slice(k * dim, (k + 1) * dim)
            up = dot(low, up_ref[:, cols]) + up_bias[:, cols]
            below = 0.5 + 0.5 * lax.erf(up * 0.7071067811865476)
            act = (up * below).astype(BF16)
            slope_ref[at(i), cols] = below + up * jnp.exp(-0.5 * up * up) * 0.3989422804014327
            act_ref[at(i), cols] = act
            part = part + dot(act, down_ref[:, cols], NT)
        y_send[at(i), :] = part.astype(BF16)
        y_copy(i).start()
        return carry

    lax.fori_loop(0, spans, forward, 0)

    def turn(i, carry):
        y_copy(i).wait()
        down = y_send[at(i), :].astype(F32) + y_recv[at(i), :].astype(F32) + down_bias
        hat, scale = norm(first_ref[at(i), :] + down)
        y_ref[at(i), :] = (hat * gain2 + shift2).astype(BF16)
        grad = grad_ref[at(i), :].astype(F32)
        add_rows(2, grad * hat)
        add_rows(3, grad)
        second = norm_back(grad, hat, scale, gain2)
        low = second.astype(BF16)
        second_ref[at(i), :] = second
        down_grad[at(i), :] = low
        add_rows(5, low.astype(F32))
        part = jnp.zeros((span, dim), F32)
        for k in range(2):
            cols = slice(k * dim, (k + 1) * dim)
            up = (slope_ref[at(i), cols] * dot(low, down_ref[:, cols])).astype(BF16)
            up_grad[at(i), cols] = up
            add_rows(6 + k, up.astype(F32))
            part = part + dot(up, up_ref[:, cols], NT)
        z_send[at(i), :] = part.astype(BF16)
        z_copy(i).start()
        return carry

    lax.fori_loop(0, spans, turn, 0)

    def products(j, carry):
        cols = pl.ds(pl.multiple_of(j * 512, 512), 512)
        grads[0, :, cols] = dot(first_low[...], up_grad[:, cols], tn).astype(BF16)
        grads[1, :, cols] = dot(down_grad[...], act_ref[:, cols], tn).astype(BF16)
        return carry

    lax.fori_loop(0, hidden // 512, products, 0)
    for which in range(2):
        for j in range(zs):
            a_copy(which, j).start()

    def back(i):
        z_copy(i).wait()
        grad = second_ref[at(i), :] + (z_send[at(i), :].astype(F32) + z_recv[at(i), :].astype(F32))
        hat = hat_ref[at(i), :]
        add_rows(0, grad * hat)
        add_rows(1, grad)
        total = norm_back(grad, hat, scale_ref[at(i), 0:1], gain1)
        low = total.astype(BF16)
        input1_ref[at(i), :] = total
        low_ref[at(i), :] = low
        add_rows(4, low.astype(F32))
        window_ref[REACH * rows + i * span:REACH * rows + (i + 1) * span, :] = dot(low, out_ref[...]).astype(BF16)
        halo.send(i)

    for i in range(spans):
        back(i)
    lane = lax.broadcasted_iota(jnp.int32, (rows, 128), 1)
    along = jnp.zeros((rows, 128), F32)
    for pair in range(width // 128):
        lanes = slice(pair * 128, pair * 128 + 128)
        product = window_ref[REACH * rows:(REACH + 1) * rows, lanes].astype(F32) * mixed_ref[:, lanes].astype(F32)
        even = jnp.sum(jnp.where(lane < 64, product, 0.0), axis=1, keepdims=True)
        odd = jnp.sum(jnp.where(lane < 64, 0.0, product), axis=1, keepdims=True)
        along = jnp.where(lane == 2 * pair, even, jnp.where(lane == 2 * pair + 1, odd, along))
    along_ref[...] = along
    own_stats[0:8, :] = jnp.transpose(lse_ref[...])[0:8, :]
    own_stats[8:16, :] = jnp.transpose(along)[0:8, :]
    stats_ref[:, REACH * rows:(REACH + 1) * rows] = own_stats[...]
    halo.send(spans)
    share = 2 * hidden // dps
    for which in range(2):
        for j in range(zs):
            a_copy(which, j).wait()
            own = pl.ds(pl.multiple_of((2 * j + core) * block, 16), block)
            for p in range(dps):
                if p * share // hidden <= which <= ((p + 1) * share - 1) // hidden:
                    first, last = max(p * share, which * hidden), min((p + 1) * share, (which + 1) * hidden)
                    cols = slice(first - which * hidden, last - which * hidden)
                    total = grads[which, own, cols].astype(F32) + a_recv[which, j, :, cols].astype(F32)
                    for k in range(dps):

                        @pl.when(lax.rem(p - d + dps, dps) == k)
                        def _():
                            share_refs[k][j, :, first - p * share:last - p * share] = total.astype(BF16)

    out_grad_ref[...] = dot(low_ref[...], mixed_ref[...], tn).astype(BF16)
    for part in range(spans + 1):
        halo.relay(part)
    for slot in (0, 2, 4, 6):
        halo.receive(slot)
    halo.finish()


def feed_forward(mixed, out_weight, out_other, source, up, down, grad, lse, vectors, dps, seqs, span=256):
    rows, dim = source.shape
    width, hidden = mixed.shape[1], up.shape[1]
    zs, block = seqs // 2, dim // seqs
    spans = rows // span
    total = (2 * REACH + 1) * rows
    dma = pltpu.SemaphoreType.DMA
    return pl.pallas_call(
        functools.partial(feed_kernel, dps, seqs, span),
        out_shape=(jax.ShapeDtypeStruct((zs, block, 2 * hidden // dps), BF16),) * dps + (
            jax.ShapeDtypeStruct((rows, dim), BF16),
            jax.ShapeDtypeStruct((rows, dim), F32),
            jax.ShapeDtypeStruct((total, width), BF16),
            jax.ShapeDtypeStruct((16, total), F32),
            jax.ShapeDtypeStruct((rows, 128), F32),
            jax.ShapeDtypeStruct((dim, width), BF16),
            jax.ShapeDtypeStruct((8, dim), F32),
        ),
        in_specs=[VMEM] * 4 + [HBM] * 2 + [VMEM] * 9,
        out_specs=(VMEM,) * (dps + 7),
        scratch_shapes=[
            pltpu.VMEM((rows, dim), BF16),
            pltpu.VMEM((16, rows), F32),
            dma((7, spans + 1)),
            dma((7, spans + 1)),
            pltpu.VMEM((dim, hidden), BF16),
            pltpu.VMEM((dim, hidden), BF16),
            dma((2,)),
            pltpu.VMEM((dim, 2 * width), BF16),
            pltpu.VMEM((rows, 2 * width), BF16),
            pltpu.VMEM((rows, dim), F32),
            pltpu.VMEM((rows, dim), F32),
            pltpu.VMEM((rows, 128), F32),
            pltpu.VMEM((rows, dim), BF16),
            pltpu.VMEM((rows, hidden), BF16),
            pltpu.VMEM((rows, hidden), F32),
            pltpu.VMEM((rows, dim), F32),
            pltpu.VMEM((rows, dim), BF16),
            pltpu.VMEM((rows, hidden), BF16),
            pltpu.VMEM((rows, dim), BF16),
            pltpu.VMEM((rows, dim), BF16),
            pltpu.VMEM((rows, dim), BF16),
            pltpu.VMEM((rows, dim), BF16),
            pltpu.VMEM((2, dim, hidden), BF16),
            pltpu.VMEM((2, zs, block, hidden), BF16),
            dma((2, spans)),
            dma((2, spans)),
            dma((2, spans)),
            dma((2, 2, zs)),
        ],
        compiler_params=pltpu.CompilerParams(collective_id=3, has_side_effects=True, vmem_limit_bytes=56 << 20),
        name="feed_forward",
    )(mixed, out_weight, out_other, source, up, down, grad, lse, *vectors)


def memory_slots(padded, count):
    id_row = padded[READ_ROWS:READ_ROWS + count]
    before = sum((padded[READ_ROWS - k:READ_ROWS - k + count] == id_row).astype(jnp.int32) for k in range(1, READ_ROWS + 1))
    behind = sum((padded[READ_ROWS + k:READ_ROWS + k + count] == id_row).astype(jnp.int32) for k in range(1, READ_ROWS + 1))
    return jnp.where(before < READ_ROWS, before, jnp.where(behind < READ_ROWS, 2 * READ_ROWS - 1 - behind, -1))


def on_device(dps, seqs, tokens, doc_ids, memory, qkv_weight, query_bias, value_bias, out_weight, out_bias, norm1_gain, norm1_bias, up_weight, up_bias, down_weight, down_bias, norm2_gain, norm2_bias, out_grad):
    rows = tokens.shape[1]
    width = qkv_weight.shape[2]
    heads = width // HEAD_DIM
    bq, bk = rows, 256
    own = REACH * rows
    pieces = 2 * REACH + 1
    s = lax.axis_index("seq")
    id_row = doc_ids[0]
    edge = (own + READ_ROWS,)
    padded = lax.dynamic_slice_in_dim(
        jnp.concatenate([jnp.full(edge, -1, jnp.int32), id_row, jnp.full(edge, 1 << 20, jnp.int32)]), s * rows, pieces * rows + 2 * READ_ROWS, 0)
    window_slots = memory_slots(padded, pieces * rows)
    window_ids = padded[READ_ROWS:READ_ROWS + pieces * rows]
    ids = jnp.broadcast_to(window_ids.astype(F32)[None], (8, pieces * rows))

    out_other = lax.ppermute(out_weight, "tensor", [(0, 1), (1, 0)])
    weight = qkv_weight.transpose(1, 0, 2)
    slots_row = jnp.broadcast_to(window_slots[None], (8, pieces * rows))
    query, key, value, source = project_window(
        tokens[0], slots_row, memory, weight, query_bias, value_bias, seqs, 1)
    own_slots = window_slots[own:own + rows]

    mixed_low, logsums = attention_forward(query, key, value, ids, rows, own, bq, bk)

    vectors = (out_bias, norm1_gain, norm1_bias, down_bias, norm2_gain, norm2_bias, up_bias)
    *shares, output, grad_input1, grads_window, stats_window, along_cols, grad_out_weight, small = feed_forward(
        mixed_low, out_weight, out_other, source, up_weight, down_weight, out_grad[0], logsums, vectors, dps, seqs)
    early = shares[:1] + [
        lax.ppermute(shares[k], "dp", [(i, (i + k) % dps) for i in range(dps)]) for k in range(1, dps)]
    proj_grad = attention_backward(query, key, value, grads_window, ids, logsums, along_cols, stats_window, rows, own, bk)

    select = (own_slots[:, None] == jnp.arange(32, dtype=jnp.int32)[None, :]).astype(BF16)
    up_sum, down_sum, out_sum, qkv_sum, input_grad, small = tail(
        early, grad_out_weight, proj_grad, source, weight, grad_input1, select, small, dps, seqs)
    small = small.reshape(32, 2 * width)
    input_grad = input_grad[None]
    piece = small.shape[1] // seqs
    vectors = lax.dynamic_slice_in_dim(small[:6], s * piece, piece, 1)
    memory_grad = small[9:29]
    return (
        output[None], input_grad, memory_grad,
        qkv_sum.transpose(1, 0, 2), small[8, :width], small[8, width:],
        out_sum, vectors[4], vectors[0], vectors[1],
        up_sum, small[6:8].reshape(-1), down_sum, vectors[5], vectors[2], vectors[3],
    )


def solution(mesh):
    in_specs = (
        P("dp", "seq", None), P("dp", None), P(), P(None, None, "tensor"), P("tensor"), P("tensor"), P(None, "tensor"), P(), P(), P(),
        P(None, "tensor"), P("tensor"), P(None, "tensor"), P(), P(), P(), P("dp", "seq", None),
    )
    out_specs = (
        P("dp", "seq", None), P("dp", "seq", None), P(), P("seq", None, "tensor"), P("tensor"), P("tensor"), P("seq", "tensor"), P("seq"), P("seq"), P("seq"),
        P("seq", "tensor"), P("tensor"), P("seq", "tensor"), P("seq"), P("seq"), P("seq"),
    )
    step = functools.partial(on_device, mesh.shape["dp"], mesh.shape["seq"])
    return jax.shard_map(step, mesh=mesh, in_specs=in_specs, out_specs=out_specs, check_vma=False)
```
